32 devices in a mesh: rows: 16 (over z, y, core), heads: 2 (over x).
Axes of the slice: x: 2, y: 2, z: 4, core: 2. Of those that a mesh axis runs over, the one named last changes fastest.
Arguments:
- tokens: bfloat16 [32768, 768], P(('rows', 'heads')), may hold values from -6 to 6
- crop_lengths: int32 [16], P('rows'), may hold values from 1025 to 2048, as said below
- lead_index: int32 [16], P('rows'), may hold values from 0 to 31
- valid_mask: int32 [32768], P(('rows', 'heads')), may hold values from 0 to 1, as said below
- lead_table: float32 [32, 768], replicated, may hold values from -3 to 3
- ln1_gain: float32 [768], replicated, may hold values from 0.25 to 1.75
- ln1_shift: float32 [768], replicated, may hold values from -1.5 to 1.5
- w_query: bfloat16 [768, 768], P(None, 'heads'), may hold values from -0.3125 to 0.3125
- w_key: bfloat16 [768, 768], P(None, 'heads'), may hold values from -0.3125 to 0.3125
- w_value: bfloat16 [768, 768], P(None, 'heads'), may hold values from -0.21875 to 0.21875
- b_query: bfloat16 [768], P('heads'), may hold values from -1.5 to 1.5
- b_value: bfloat16 [768], P('heads'), may hold values from -1.5 to 1.5
- w_out: bfloat16 [768, 768], P('heads'), may hold values from -1.75 to 1.75
- b_out: float32 [768], replicated, may hold values from -1.5 to 1.5
- ln2_gain: float32 [768], replicated, may hold values from 0.25 to 1.75
- ln2_shift: float32 [768], replicated, may hold values from -1.5 to 1.5
- w_up: bfloat16 [768, 3072], P(None, 'heads'), may hold values from -0.21875 to 0.21875
- b_up: bfloat16 [3072], P('heads'), may hold values from -1.5 to 1.5
- w_down: bfloat16 [3072, 768], P('heads'), may hold values from -0.109375 to 0.109375
- b_down: float32 [768], replicated, may hold values from -1.5 to 1.5
- w_gater: float32 [768, 3], replicated, may hold values from -0.3125 to 0.3125
- cotangent: bfloat16 [32768, 768], P(('rows', 'heads')), may hold values from -6 to 6
Outputs:
- block_out: bfloat16 [32768, 768], P(('rows', 'heads'))
- penalty: float32 [], replicated
- grad_tokens: float32 [32768, 768], P(('rows', 'heads'))
- grad_lead_table: float32 [32, 768], replicated
- grad_ln1_gain: float32 [768], replicated
- grad_ln1_shift: float32 [768], replicated
- grad_query: float32 [768, 768], P('rows', 'heads')
- grad_key: float32 [768, 768], P('rows', 'heads')
- grad_value: float32 [768, 768], P('rows', 'heads')
- grad_b_query: float32 [768], P('heads')
- grad_b_value: float32 [768], P('heads')
- grad_out: float32 [768, 768], P('heads', 'rows')
- grad_b_out: float32 [768], replicated
- grad_ln2_gain: float32 [768], replicated
- grad_ln2_shift: float32 [768], replicated
- grad_up: float32 [768, 3072], P('rows', 'heads')
- grad_b_up: float32 [3072], P('heads')
- grad_down: float32 [3072, 768], P('heads', 'rows')
- grad_b_down: float32 [768], replicated
- grad_gater: float32 [768, 3], replicated
The draws below stay inside these ranges and needn't reach their ends.
Inputs may be any that keep to these rules, and one draw needn't show every extreme that they name: `crop_lengths`: every crop uses more than half of its 2048 slots, and some crop uses all of them. `valid_mask`: the first pixel of every crop counts.
All inputs are finite; a program needn't handle non-finite values.
Results may differ from the reference program's by a relative error of at most 0.014.
The reference program's roundings to bfloat16 on the way count: a program that leaves them out, or rounds other values in their place, can miss the bound.
Values may be sent and summed in bfloat16 or wider, within the bound.
No kernel may reach another device: no remote copies, remote signals or barrier semaphores. Data moves between devices by JAX's collectives and lax.ppermute only.
A program may use at most 320 MiB of HBM per device.

```python
import jax
import jax.numpy as jnp
from jax import lax

HEADS = 12
HEAD_DIM = 64
D = 768
FF = 3072
CROP_LEN = 2048
LEADS = 32
CROPS = 16
TOKENS = 32768


def draw_crop_lengths(key, part):
    lengths = jax.random.randint(key, (CROPS,), CROP_LEN // 2 + 1, CROP_LEN + 1)
    chosen = jax.random.randint(jax.random.fold_in(key, 7), (), 0, CROPS)
    return jnp.where(jnp.arange(CROPS) == chosen, CROP_LEN, lengths).astype(jnp.int32)


def draw_valid_mask(key, part):
    levels = jax.random.randint(key, (TOKENS,), 0, 4)
    leading = jnp.arange(TOKENS) % CROP_LEN == 0
    return jnp.where(leading | (levels > 0), 1, 0).astype(jnp.int32)


def place_ends(entries, key, low, largest):
    spot = [jax.random.randint(jax.random.fold_in(key, axis), (), 0, length) for axis, length in enumerate(entries.shape)]
    longest = entries.shape.index(max(entries.shape))
    beside = spot[:longest] + [(spot[longest] + 1) % entries.shape[longest]] + spot[longest + 1:]
    return entries.at[tuple(spot)].set(low).at[tuple(beside)].set(largest)


def level_of(own_key, shape, shards, smallest, largest):
    level, own = 1.0, jax.random.fold_in(own_key, 6)
    for dim, blocks in shards:
        steps = jnp.exp(jax.random.uniform(jax.random.fold_in(own, dim), (blocks,), jnp.float32, smallest / len(shards), largest / len(shards)))
        level = level * jnp.repeat(steps, shape[dim] // blocks).reshape([-1 if axis == dim else 1 for axis in range(len(shape))])
    return level


def noise(own_key, extent, width, reach, pieces=(), held_as=jnp.bfloat16):
    entries = width * jax.random.normal(own_key, extent, jnp.float32)
    if pieces:
        entries = entries * level_of(own_key, extent, pieces, -0.22, 0.18)
    return jnp.clip(entries, -reach, reach).astype(held_as)


def setup_inputs(seed: int = 0) -> dict:
    splits = jax.random.split(jax.random.key(seed), 23)
    return {
        "tokens": noise(splits[0], (TOKENS, D), 1.0, 6.0, ((0, 32),)),
        "crop_lengths": draw_crop_lengths(jax.random.fold_in(splits[22], 71), 0),
        "lead_index": place_ends(jax.random.randint(splits[2], (CROPS,), 0, LEADS), jax.random.fold_in(splits[2], 1), 0, LEADS - 1).astype(jnp.int32),
        "valid_mask": draw_valid_mask(jax.random.fold_in(splits[22], 71), 0),
        "lead_table": noise(splits[4], (LEADS, D), 0.5, 3.0, (), jnp.float32),
        "ln1_gain": jnp.clip(1.0 + 0.15 * jax.random.normal(splits[5], (D,), jnp.float32), 0.25, 1.75),
        "ln1_shift": noise(splits[6], (D,), 0.3, 1.5, (), jnp.float32),
        "w_query": noise(splits[7], (D, D), (D // 2) ** -0.5, 0.3125, ((1, 2),)),
        "w_key": noise(splits[8], (D, D), (D // 2) ** -0.5, 0.3125, ((1, 2),)),
        "w_value": noise(splits[9], (D, D), D ** -0.5, 0.21875, ((1, 2),)),
        "b_query": noise(splits[10], (D,), 0.3, 1.5, ((0, 2),)),
        "b_value": noise(splits[11], (D,), 0.3, 1.5, ((0, 2),)),
        "w_out": noise(splits[12], (D, D), (D // 64) ** -0.5, 1.75, ((0, 2),)),
        "b_out": noise(splits[13], (D,), 0.3, 1.5, (), jnp.float32),
        "ln2_gain": jnp.clip(1.0 + 0.15 * jax.random.normal(splits[14], (D,), jnp.float32), 0.25, 1.75),
        "ln2_shift": noise(splits[15], (D,), 0.3, 1.5, (), jnp.float32),
        "w_up": noise(splits[16], (D, FF), D ** -0.5, 0.21875, ((1, 2),)),
        "b_up": noise(splits[17], (FF,), 0.3, 1.5, ((0, 2),)),
        "w_down": noise(splits[18], (FF, D), FF ** -0.5, 0.109375, ((0, 2),)),
        "b_down": noise(splits[19], (D,), 0.3, 1.5, (), jnp.float32),
        "w_gater": noise(splits[20], (D, 3), (D // 2) ** -0.5, 0.3125, (), jnp.float32),
        "cotangent": noise(splits[21], (TOKENS, D), 1.0, 6.0, ((0, 32),)),
    }


@jax.custom_vjp
def low(v):
    return lax.optimization_barrier(v.astype(jnp.bfloat16)).astype(jnp.float32)

@jax.custom_vjp
def low_back(v):
    return v

def low_keep(v):
    return (low(v), None)

def low_pass(kept, grad):
    return (grad,)

def back_keep(v):
    return (v, None)

def back_low(kept, grad):
    return (low(grad),)
low.defvjp(low_keep, low_pass)
low_back.defvjp(back_keep, back_low)
entropy_weight = 16.0

def matmul_high(left, right):
    return jnp.dot(left, right, precision=lax.Precision.HIGHEST, preferred_element_type=jnp.float32)

def layer_norm(values, gain, shift):
    centre = values - lax.optimization_barrier(jnp.mean(values, axis=-1, keepdims=True))
    spread = lax.optimization_barrier(jnp.mean(centre * centre, axis=-1, keepdims=True))
    return centre * lax.rsqrt(spread + 1e-05) * gain + shift

def crop_attention(inputs):
    query, key, value, length = inputs
    scores = jnp.einsum('qhd,khd->hqk', query, key, precision=lax.Precision.HIGHEST) * HEAD_DIM ** (-0.5)
    scores = low_back(scores)
    key_ok = jnp.arange(CROP_LEN, dtype=jnp.int32) < length
    scores = jnp.where(key_ok[None, None, :], scores, -1e+30)
    probs = low(jax.nn.softmax(scores, axis=-1))
    mixed = jnp.einsum('hqk,khd->qhd', probs, value, precision=lax.Precision.HIGHEST)
    return low(low_back(mixed))

def reference(tokens, crop_lengths, lead_index, valid_mask, lead_table, ln1_gain, ln1_shift, w_query, w_key, w_value, b_query, b_value, w_out, b_out, ln2_gain, ln2_shift, w_up, b_up, w_down, b_down, w_gater, cotangent):
    lead_tok = jnp.repeat(lead_index, CROP_LEN)
    positions = jnp.arange(TOKENS, dtype=jnp.int32) % CROP_LEN
    counted = ((positions < jnp.repeat(crop_lengths, CROP_LEN)) & (valid_mask == 1)).astype(jnp.float32)

    def forward(x_in, table, gain_one, shift_one, wq, wk, wv, bq, bv, wo, bo, gain_two, shift_two, wu, bu, wd, bd, wg):
        x0 = x_in + table[lead_tok]
        normed = low(layer_norm(x0, gain_one, shift_one))
        query = low(low_back(matmul_high(normed, wq) + bq))
        key = low(low_back(matmul_high(normed, wk)))
        value = low(low_back(matmul_high(normed, wv) + bv))
        shape4 = (CROPS, CROP_LEN, HEADS, HEAD_DIM)
        mixed = lax.map(jax.checkpoint(crop_attention), (query.reshape(shape4), key.reshape(shape4), value.reshape(shape4), crop_lengths))
        mixed = mixed.reshape(TOKENS, D)
        hidden_one = x0 + low_back(matmul_high(mixed, wo) + bo)
        normed_two = low(layer_norm(hidden_one, gain_two, shift_two))
        pre = low_back(matmul_high(normed_two, wu) + bu)
        act = low(jax.nn.gelu(pre, approximate=False))
        out = hidden_one + low_back(matmul_high(act, wd) + bd)
        logits = matmul_high(out, wg)
        log_probs = jax.nn.log_softmax(logits, axis=-1)
        entropy = -lax.optimization_barrier(jnp.sum(jnp.exp(log_probs) * log_probs, axis=-1))
        penalty = jnp.sum(counted * entropy) / jnp.sum(counted)
        return (out, penalty)
    f32 = jnp.float32
    primals = (tokens.astype(f32), lead_table, ln1_gain, ln1_shift, w_query.astype(f32), w_key.astype(f32), w_value.astype(f32), b_query.astype(f32), b_value.astype(f32), w_out.astype(f32), b_out, ln2_gain, ln2_shift, w_up.astype(f32), b_up.astype(f32), w_down.astype(f32), b_down, w_gater)
    (out, penalty), vjp_fn = jax.vjp(forward, *primals)
    grads = vjp_fn((cotangent.astype(f32), jnp.asarray(entropy_weight, f32)))
    d_x, d_table, d_g1, d_s1, d_wq, d_wk, d_wv, d_bq, d_bv, d_wo, d_bo, d_g2, d_s2, d_wu, d_bu, d_wd, d_bd, d_wg = grads
    return (out.astype(jnp.bfloat16), penalty, d_x, d_table, d_g1, d_s1, d_wq, d_wk, d_wv, d_bq, d_bv, d_wo, d_bo, d_g2, d_s2, d_wu, d_bu, d_wd, d_bd, d_wg)
```

```python
import functools

import jax
import jax.numpy as jnp
from jax import lax
from jax.experimental import pallas as pl
from jax.experimental.pallas import tpu as pltpu
from jax.sharding import PartitionSpec as P

HEAD_DIM = 64
PAIR = 2 * HEAD_DIM
NEG = -1e30
SCALE = HEAD_DIM ** (-0.5)
entropy_weight = 16.0
f32 = jnp.float32
bf16 = jnp.bfloat16
NT = (((1,), (1,)), ((), ()))
TN = (((0,), (0,)), ((), ()))
NN = (((1,), (0,)), ((), ()))
VMEM_LIMIT = 56 << 20


def mm(a, b, dims=NN):
    return lax.dot_general(a, b, dims, preferred_element_type=f32)


def layer_norm(values, gain, shift):
    centre = values - jnp.mean(values, axis=-1, keepdims=True)
    spread = jnp.mean(centre * centre, axis=-1, keepdims=True)
    return centre * lax.rsqrt(spread + 1e-05) * gain + shift


def gelu_exact(values):
    return jax.nn.gelu(values, approximate=False)


def split3(x):
    hi = x.astype(bf16).astype(f32)
    mid = (x - hi).astype(bf16).astype(f32)
    return hi, mid, x - hi - mid


def pair_masks():
    lane = lax.broadcasted_iota(jnp.int32, (1, PAIR), 1)
    return lane, (lane < HEAD_DIM, lane >= HEAD_DIM), (HEAD_DIM, 0)


def own_part(h):
    return slice(0, HEAD_DIM) if h == 0 else slice(HEAD_DIM, PAIR)


def key_bias(meta, keys):
    kpos = meta[0] + lax.broadcasted_iota(jnp.int32, (keys, 1), 0)
    return jnp.where(kpos < meta[1], 0.0, NEG)


def attn_fwd_kernel(first, qb, kc, meta, q_ref, k_ref, v_ref, *refs):
    if first:
        acc_ref, ml_ref, st_sc, p_sc = refs
    else:
        acc_in, ml_in, o_ref, e_ref, acc_sc, e_sc, st_sc, p_sc = refs
    rows = q_ref.shape[0]
    keys = k_ref.shape[0]
    lane, inside, free = pair_masks()
    bias = key_bias(meta, keys)
    q32 = q_ref[...].astype(f32) * SCALE
    k32 = k_ref[...].astype(f32)
    v32 = v_ref[...].astype(f32)
    qx = [jnp.where(inside[h], q32, jnp.where(lane == free[h], 1.0, 0.0)).astype(bf16) for h in range(2)]
    kx = [jnp.where(inside[h], k32, bias).astype(bf16) for h in range(2)]
    vx = [jnp.where(inside[h], v32, 1.0).astype(bf16) for h in range(2)]
    units = [(h, b) for h in range(2) for b in range(rows // qb)]
    chunks = [slice(c * kc, (c + 1) * kc) for c in range(keys // kc)]
    m_prev = None
    for u in range(len(units) + 1):
        slot, prev = u % 2, (u - 1) % 2
        if u < len(units):
            h, b = units[u]
            cols = slice(b * qb, (b + 1) * qb)
        m8 = None
        for ch in chunks:
            if u < len(units):
                st = mm(kx[h][ch], qx[h][cols], NT)
                st_sc[slot, ch, :] = st
                top = jnp.max(st.reshape(kc // 8, 8, qb), axis=0)
                m8 = top if m8 is None else jnp.maximum(m8, top)
            if u > 0:
                p_sc[prev, ch, :] = jnp.exp(st_sc[prev, ch, :] - m_prev).astype(bf16)
        if u > 0:
            hp, bp = units[u - 1]
            pc = slice(bp * qb, (bp + 1) * qb)
            ot = mm(vx[hp], p_sc[prev], TN)
            fe = free[hp]
            own = own_part(hp)
            total = ot[fe : fe + 1]
            num = ot[own]
            if first:
                acc_ref[own, pc] = num
                ml_ref[hp : hp + 1, pc] = m_prev
                ml_ref[2 + hp : 3 + hp, pc] = total
            else:
                alpha = jnp.exp(ml_in[hp : hp + 1, pc] - m_prev)
                total = total + alpha * ml_in[2 + hp : 3 + hp, pc]
                num = num + alpha * acc_in[own, pc]
                acc_sc[own, pc] = num / total
                hi, mid, lo = split3(m_prev + jnp.log(total))
                row = lax.broadcasted_iota(jnp.int32, (HEAD_DIM, 1), 0)
                e_sc[fe : fe + HEAD_DIM, pc] = jnp.where(
                    row == 0, 1.0, jnp.where(row == 1, -hi, jnp.where(row == 2, -mid, jnp.where(row == 3, -lo, 0.0)))
                )
        if u < len(units):
            m_prev = jnp.max(m8, axis=0, keepdims=True)
            if not first:
                m_prev = jnp.maximum(m_prev, ml_in[h : h + 1, cols])
    if not first:
        o_ref[...] = acc_sc[...].T.astype(bf16)
        e_ref[...] = e_sc[...].T.astype(bf16)


def attn_fwd(meta, q, k, v, pairs, state=None, qb=1024, kc=256):
    rows = q[0].shape[0]
    keys = k[0].shape[0]
    width = pairs * PAIR
    first = state is None

    def col(off):
        return lambda i, m: (0, off + i)

    def down(i, m):
        return (i, 0)

    in_specs = [
        pl.BlockSpec((rows, PAIR), col(q[1])),
        pl.BlockSpec((keys, PAIR), col(k[1])),
        pl.BlockSpec((keys, PAIR), col(v[1])),
    ]
    scratch = [pltpu.VMEM((2, keys, qb), f32), pltpu.VMEM((2, keys, qb), bf16)]
    args = (q[0], k[0], v[0])
    if first:
        out_shape = (jax.ShapeDtypeStruct((width, rows), f32), jax.ShapeDtypeStruct((8 * pairs, rows), f32))
        out_specs = (pl.BlockSpec((PAIR, rows), down), pl.BlockSpec((8, rows), down))
    else:
        in_specs += [pl.BlockSpec((PAIR, rows), down), pl.BlockSpec((8, rows), down)]
        out_shape = (jax.ShapeDtypeStruct((rows, width), bf16), jax.ShapeDtypeStruct((rows, width), bf16))
        out_specs = (pl.BlockSpec((rows, PAIR), col(0)), pl.BlockSpec((rows, PAIR), col(0)))
        scratch = [pltpu.VMEM((PAIR, rows), f32), pltpu.VMEM((PAIR, rows), f32)] + scratch
        args = args + tuple(state)
    return pl.pallas_call(
        functools.partial(attn_fwd_kernel, first, qb, kc),
        grid_spec=pltpu.PrefetchScalarGridSpec(
            num_scalar_prefetch=1, grid=(pairs,), in_specs=in_specs, out_specs=out_specs, scratch_shapes=scratch
        ),
        out_shape=out_shape,
        compiler_params=pltpu.CompilerParams(vmem_limit_bytes=VMEM_LIMIT),
        cost_estimate=pl.CostEstimate(flops=16 * rows * keys * width, transcendentals=0, bytes_accessed=8 * rows * width),
        name="attn_fwd_first" if first else "attn_fwd_second",
    )(meta, *args)


def attn_bwd_kernel(first, qb, kc, meta, q_ref, e_ref, o_ref, do_ref, k_ref, v_ref, *refs):
    if first:
        dq_ref, dk_ref, dv_ref, dk_sc, dv_sc, s_sc, dp_sc, p_sc, ds_sc = refs
    else:
        dq_in, dq_ref, dk_ref, dv_ref, dk_sc, dv_sc, s_sc, dp_sc, p_sc, ds_sc = refs
    rows = q_ref.shape[0]
    keys = k_ref.shape[0]
    lane, inside, free = pair_masks()
    bias = key_bias(meta, keys)
    k32 = k_ref[...].astype(f32)
    v32 = v_ref[...].astype(f32)
    kx = [jnp.where(inside[h], k32, jnp.where(lane == free[h], bias, 1.0)).astype(bf16) for h in range(2)]
    vx = [jnp.where(inside[h], v32, 1.0).astype(bf16) for h in range(2)]
    units = [(b, h) for b in range(rows // qb) for h in range(2)]
    chunks = [slice(c * kc, (c + 1) * kc) for c in range(keys // kc)]
    prep = None
    dq0 = None
    for u in range(len(units) + 1):
        before = prep
        slot, prev = u % 2, (u - 1) % 2
        if u < len(units):
            b, h = units[u]
            rs = slice(b * qb, (b + 1) * qb)
            fe = free[h]
            if h == 0:
                q32 = q_ref[rs].astype(f32) * SCALE
                do32 = do_ref[rs].astype(f32)
                e32 = e_ref[rs].astype(f32)
                prod = do32 * o_ref[rs].astype(f32)
            hi, mid, lo = split3(jnp.sum(jnp.where(inside[h], prod, 0.0), axis=1, keepdims=True))
            dext = jnp.where(lane == fe, -hi, jnp.where(lane == fe + 1, -mid, jnp.where(lane == fe + 2, -lo, 0.0)))
            qx = jnp.where(inside[h], q32, e32).astype(bf16)
            dox = jnp.where(inside[h], do32, dext).astype(bf16)
            prep = (qx, dox)
        for ch in chunks:
            if u < len(units):
                s_sc[slot, :, ch] = mm(qx, kx[h][ch], NT)
                dp_sc[slot, :, ch] = mm(dox, vx[h][ch], NT)
            if u > 0:
                p = jnp.exp(s_sc[prev, :, ch])
                p_sc[prev, :, ch] = p.astype(bf16)
                ds_sc[prev, :, ch] = (p * dp_sc[prev, :, ch]).astype(bf16)
        if u > 0:
            bp, hp = units[u - 1]
            rp = slice(bp * qb, (bp + 1) * qb)
            qxp, doxp = before
            dvt = mm(doxp, p_sc[prev], TN)
            dkt = mm(qxp, ds_sc[prev], TN)
            dqh = mm(ds_sc[prev], kx[hp], NN)
            own = own_part(hp)
            if bp == 0:
                dv_sc[own] = dvt[own]
                dk_sc[own] = dkt[own]
            else:
                dv_sc[own] += dvt[own]
                dk_sc[own] += dkt[own]
            if hp == 0:
                dq0 = dqh
            else:
                dq = jnp.where(lane < HEAD_DIM, dq0, dqh) * SCALE
                if first:
                    dq_ref[rp] = dq
                else:
                    dq_ref[rp] = (dq + dq_in[rp]).astype(bf16)
    dk_ref[...] = dk_sc[...].T.astype(bf16)
    dv_ref[...] = dv_sc[...].T.astype(bf16)


def attn_bwd(meta, q, e, o, do, k, v, pairs, dq_prev=None, qb=256, kc=256):
    rows = q[0].shape[0]
    keys = k[0].shape[0]
    width = pairs * PAIR
    first = dq_prev is None

    def col(off):
        return lambda i, m: (0, off + i)

    in_specs = [pl.BlockSpec((rows, PAIR), col(off)) for _, off in (q, e, o, do)]
    in_specs += [pl.BlockSpec((keys, PAIR), col(off)) for _, off in (k, v)]
    args = (q[0], e[0], o[0], do[0], k[0], v[0])
    rspec = pl.BlockSpec((rows, PAIR), col(0))
    kspec = pl.BlockSpec((keys, PAIR), col(0))
    if not first:
        in_specs.append(rspec)
        args = args + (dq_prev,)
    return pl.pallas_call(
        functools.partial(attn_bwd_kernel, first, qb, kc),
        grid_spec=pltpu.PrefetchScalarGridSpec(
            num_scalar_prefetch=1,
            grid=(pairs,),
            in_specs=in_specs,
            out_specs=(rspec, kspec, kspec),
            scratch_shapes=[pltpu.VMEM((PAIR, keys), f32)] * 2
            + [pltpu.VMEM((2, qb, keys), f32)] * 2
            + [pltpu.VMEM((2, qb, keys), bf16)] * 2,
        ),
        out_shape=(
            jax.ShapeDtypeStruct((rows, width), f32 if first else bf16),
            jax.ShapeDtypeStruct((keys, width), bf16),
            jax.ShapeDtypeStruct((keys, width), bf16),
        ),
        compiler_params=pltpu.CompilerParams(vmem_limit_bytes=VMEM_LIMIT),
        cost_estimate=pl.CostEstimate(flops=40 * rows * keys * width, transcendentals=0, bytes_accessed=16 * rows * width),
        name="attn_bwd_first" if first else "attn_bwd_second",
    )(meta, *args)


class Net:
    def __init__(self, n_rows):
        self.n_rows = n_rows
        self.bits = n_rows.bit_length() - 1
        self.row = lax.axis_index("rows")

    def cross(self, x):
        return lax.ppermute(x, "heads", [(0, 1), (1, 0)])

    def flip(self, x, bit):
        return lax.ppermute(x, "rows", [(i, i ^ (1 << bit)) for i in range(self.n_rows)])

    def bit(self, b):
        return (self.row >> b) & 1

    def fetch(self, own):
        part = own.shape[0] // 2
        mine = self.bit(0) * part
        got = self.cross(lax.dynamic_slice_in_dim(own, mine, part, 0))
        passed = self.flip(got, 0)
        full = jnp.zeros(own.shape, own.dtype)
        full = lax.dynamic_update_slice_in_dim(full, got, mine, 0)
        return lax.dynamic_update_slice_in_dim(full, passed, part - mine, 0)

    def all_sum(self, whole, own, other):
        n_whole = whole.shape[0]
        packed = jnp.concatenate([whole, own, other], axis=0)
        for b in range(self.bits):
            packed = packed + self.flip(packed, b)
        n_own = own.shape[0]
        send = jnp.concatenate([packed[:n_whole], packed[n_whole + n_own :]], axis=0)
        return packed[: n_whole + n_own] + self.cross(send)

    def scatter_sum(self, own, other, order):
        rows, cols = own.shape
        piece = rows // self.n_rows
        parts = [own.reshape(self.n_rows, piece, cols), other.reshape(self.n_rows, piece, cols)]
        left = list(range(self.bits))
        for step in order:
            if step == "x":
                mine, theirs = parts
                parts = [mine.astype(f32) + self.cross(theirs.astype(bf16)).astype(f32)]
                continue
            low = 1 << left.index(step)
            left.remove(step)
            at = self.bit(step)
            views = [p.reshape(p.shape[0] // (2 * low), 2, low, piece, cols) for p in parts]
            keep = [lax.dynamic_index_in_dim(v, at, 1, keepdims=False) for v in views]
            send = [lax.dynamic_index_in_dim(v, 1 - at, 1, keepdims=False).astype(bf16) for v in views]
            got = self.flip(jnp.concatenate(send, axis=-1), step) if len(send) > 1 else self.flip(send[0], step)
            got = [got[..., i * cols : (i + 1) * cols] for i in range(len(send))]
            parts = [
                (k.astype(f32) + g.astype(f32)).reshape(k.shape[0] * k.shape[1], piece, cols) for k, g in zip(keep, got)
            ]
        return parts[0].reshape(piece, cols)


def per_device(
    n_rows,
    tokens,
    crop_lengths,
    lead_index,
    valid_mask,
    lead_table,
    ln1_gain,
    ln1_shift,
    w_query,
    w_key,
    w_value,
    b_query,
    b_value,
    w_out,
    b_out,
    ln2_gain,
    ln2_shift,
    w_up,
    b_up,
    w_down,
    b_down,
    w_gater,
    cotangent,
):
    net = Net(n_rows)
    own_rows, width = tokens.shape
    half = lax.axis_index("heads")
    length = crop_lengths[0]
    hw = w_query.shape[1]
    pairs = hw // PAIR
    own_start = half * own_rows
    meta_own = jnp.stack([own_start, length])
    meta_oth = jnp.stack([own_rows - own_start, length])

    positions = own_start + jnp.arange(own_rows, dtype=jnp.int32)
    counted = ((positions < length) & (valid_mask == 1)).astype(f32)
    count = jnp.full((8, 128), jnp.sum(counted), f32)
    for b in range(net.bits):
        count = count + net.flip(count, b)
    count_total = (count + net.cross(count))[0, 0]

    qkv_w = jnp.concatenate([w_query, w_key, w_value], axis=1)
    bias_own = jnp.concatenate([b_query, b_value, b_up]).reshape(1, -1)
    bias_oth = net.cross(jnp.broadcast_to(bias_own, (16, bias_own.shape[1])))[:1]
    qkv_w2 = net.fetch(qkv_w)
    tokens_in, qkv_w2 = lax.optimization_barrier((tokens, qkv_w2))
    tokens_oth = net.cross(tokens_in)
    w_out_in, w_up_in, w_down_in, tokens_oth = lax.optimization_barrier((w_out, w_up, w_down, tokens_oth))
    w_out2 = net.fetch(w_out_in)
    w_up_in, w_out2 = lax.optimization_barrier((w_up_in, w_out2))
    w_up2 = net.fetch(w_up_in)
    w_down_in, w_up2 = lax.optimization_barrier((w_down_in, w_up2))
    w_down2 = net.fetch(w_down_in)

    def qkv_bias(b):
        b = b.astype(f32)
        return jnp.concatenate([b[:, :hw], jnp.zeros((1, hw), f32), b[:, hw : 2 * hw]], axis=1)

    qkv_b, qkv_b2 = qkv_bias(bias_own), qkv_bias(bias_oth)
    up_b, up_b2 = bias_own[:, 2 * hw :].astype(f32), bias_oth[:, 2 * hw :].astype(f32)

    picked = jnp.arange(lead_table.shape[0], dtype=jnp.int32) == lead_index[0]
    embedding = jnp.sum(jnp.where(picked[:, None], lead_table, 0.0), axis=0)
    x_zero = tokens.astype(f32) + embedding
    normed = layer_norm(x_zero, ln1_gain, ln1_shift).astype(bf16)
    qkv = [(mm(normed, qkv_w) + qkv_b).astype(bf16)]
    state = [attn_fwd(meta_own, (qkv[0], 0), (qkv[0], pairs), (qkv[0], 2 * pairs), pairs)]
    qkv.append((mm(normed, qkv_w2) + qkv_b2).astype(bf16))
    state.append(attn_fwd(meta_own, (qkv[1], 0), (qkv[1], pairs), (qkv[1], 2 * pairs), pairs))
    normed_oth = layer_norm(tokens_oth.astype(f32) + embedding, ln1_gain, ln1_shift).astype(bf16)
    kv_oth = [
        (mm(normed_oth, w[:, hw:]) + b[:, hw:]).astype(bf16) for w, b in ((qkv_w, qkv_b), (qkv_w2, qkv_b2))
    ]
    attn, ext = [], []
    for i in range(2):
        o, e = attn_fwd(meta_oth, (qkv[i], 0), (kv_oth[i], 0), (kv_oth[i], pairs), pairs, state[i])
        attn.append(o)
        ext.append(e)

    hidden_one = x_zero + (mm(attn[0], w_out) + mm(attn[1], w_out2) + b_out)
    normed_two = layer_norm(hidden_one, ln2_gain, ln2_shift).astype(bf16)
    ups, downs, up_bs = (w_up, w_up2), (w_down, w_down2), (up_b, up_b2)
    pre = [mm(normed_two, ups[i]) + up_bs[i] for i in range(2)]
    act = [gelu_exact(p).astype(bf16) for p in pre]
    output = hidden_one + (mm(act[0], w_down) + mm(act[1], w_down2) + b_down)

    logits = jnp.einsum("dc,td->ct", w_gater, output, precision=lax.Precision.HIGHEST)
    log_probs = jax.nn.log_softmax(logits, axis=0)
    gate_probs = jnp.exp(log_probs)
    entropy = -jnp.sum(gate_probs * log_probs, axis=0)
    entropy_sum = jnp.sum(counted * entropy)
    mean_logit = jnp.sum(gate_probs * logits, axis=0)
    d_logits = entropy_weight / count_total * counted * (-gate_probs * (logits - mean_logit))
    d_output = cotangent.astype(f32) + jnp.einsum("dc,ct->td", w_gater, d_logits, precision=lax.Precision.HIGHEST)
    d_gater = jnp.einsum("td,ct->cd", output, d_logits, precision=lax.Precision.HIGHEST)
    d_branch = d_output.astype(bf16)
    d_bias_down = jnp.sum(d_branch.astype(f32), axis=0)

    d_down = [mm(d_branch, a, TN).astype(bf16) for a in act]
    g_down = net.scatter_sum(d_down[0], d_down[1], [0, 1, 2, 3, "x"] + list(range(4, net.bits)))
    d_pre = []
    for i in range(2):
        gelu_back = jax.vjp(gelu_exact, pre[i])[1]
        d_pre.append(gelu_back(mm(d_branch, downs[i], NT))[0].astype(bf16))
    d_up = [mm(normed_two, d, TN).astype(bf16) for d in d_pre]
    g_up = net.scatter_sum(d_up[0], d_up[1], [0, 2, 1, 3, "x"] + list(range(4, net.bits)))
    d_bias_up = [jnp.sum(d.astype(f32), axis=0) for d in d_pre]
    d_normed_two = mm(d_pre[0], w_up, NT) + mm(d_pre[1], w_up2, NT)
    norm_two_back = jax.vjp(layer_norm, hidden_one, ln2_gain, ln2_shift)[1]
    d_hidden_norm, d_gain_two, d_shift_two = norm_two_back(d_normed_two)
    d_hidden = d_output + d_hidden_norm
    d_attn = d_hidden.astype(bf16)
    d_bias_out = jnp.sum(d_attn.astype(f32), axis=0)
    d_heads = [mm(d_attn, w, NT).astype(bf16) for w in (w_out, w_out2)]
    d_wout = [mm(d_attn, a, TN).astype(bf16) for a in attn]
    g_out = net.scatter_sum(d_wout[0], d_wout[1], [0, 1, 2, 3, "x"] + list(range(4, net.bits)))

    whole = jnp.concatenate(
        [d_gater, jnp.stack([d_gain_two, d_shift_two, d_bias_out, d_bias_down, jnp.full((width,), entropy_sum)])]
    )
    sums = net.all_sum(whole, d_bias_up[0].reshape(-1, width), d_bias_up[1].reshape(-1, width))
    d_gater, penalty = sums[:3].T, sums[7, 0] / count_total
    d_gain_two, d_shift_two, d_bias_out, d_bias_down = sums[3], sums[4], sums[5], sums[6]
    d_bias_up_own = sums[8:].reshape(-1)

    dq, dk_oth, dv_oth = [], [], []
    for i in range(2):
        a, b, c = attn_bwd(
            meta_oth, (qkv[i], 0), (ext[i], 0), (attn[i], 0), (d_heads[i], 0), (kv_oth[i], 0), (kv_oth[i], pairs), pairs
        )
        dq.append(a)
        dk_oth.append(b)
        dv_oth.append(c)
    ws = (qkv_w, qkv_w2)
    da_oth = sum(
        mm(dk_oth[i], ws[i][:, hw : 2 * hw], NT) + mm(dv_oth[i], ws[i][:, 2 * hw :], NT) for i in range(2)
    ).astype(bf16)
    da_got = net.cross(da_oth)
    d_qkv = []
    g_qkv = []
    for i in range(2):
        a, b, c = attn_bwd(
            meta_own,
            (qkv[i], 0),
            (ext[i], 0),
            (attn[i], 0),
            (d_heads[i], 0),
            (qkv[i], pairs),
            (qkv[i], 2 * pairs),
            pairs,
            dq[i],
        )
        d_qkv.append((a, b, c))
        g_qkv.append(
            jnp.concatenate(
                [
                    mm(normed, a, TN),
                    mm(normed, b, TN) + mm(normed_oth, dk_oth[i], TN),
                    mm(normed, c, TN) + mm(normed_oth, dv_oth[i], TN),
                ],
                axis=1,
            ).astype(bf16)
        )
    g_qkv_sum = net.scatter_sum(g_qkv[0], g_qkv[1], [0, 1, 2, 3, "x"] + list(range(4, net.bits)))
    da = da_got.astype(f32) + sum(
        mm(d_qkv[i][j], ws[i][:, j * hw : (j + 1) * hw], NT) for i in range(2) for j in range(3)
    )
    norm_one_back = jax.vjp(layer_norm, x_zero, ln1_gain, ln1_shift)[1]
    d_input_norm, d_gain_one, d_shift_one = norm_one_back(da)
    d_tokens = d_hidden + d_input_norm
    d_table = jnp.where(picked[:, None], jnp.sum(d_tokens, axis=0)[None, :], 0.0)
    bias_rows = [
        jnp.concatenate(
            [jnp.sum(d_qkv[i][0].astype(f32), axis=0), jnp.sum(d_qkv[i][2].astype(f32), axis=0) + jnp.sum(dv_oth[i].astype(f32), axis=0)]
        ).reshape(1, -1)
        for i in range(2)
    ]
    late = net.all_sum(
        jnp.concatenate([d_table, d_gain_one.reshape(1, -1), d_shift_one.reshape(1, -1)]), bias_rows[0], bias_rows[1]
    )
    n_lead = lead_table.shape[0]
    return (
        output.astype(bf16),
        penalty,
        d_tokens,
        late[:n_lead],
        late[n_lead],
        late[n_lead + 1],
        g_qkv_sum[:, :hw],
        g_qkv_sum[:, hw : 2 * hw],
        g_qkv_sum[:, 2 * hw :],
        late[n_lead + 2, :hw],
        late[n_lead + 2, hw:],
        g_out.T,
        d_bias_out,
        d_gain_two,
        d_shift_two,
        g_up,
        d_bias_up_own,
        g_down.T,
        d_bias_down,
        d_gater,
    )


def solution(mesh):
    in_specs = (
        P(("rows", "heads"), None),
        P("rows"),
        P("rows"),
        P(("rows", "heads")),
        P(),
        P(),
        P(),
        P(None, "heads"),
        P(None, "heads"),
        P(None, "heads"),
        P("heads"),
        P("heads"),
        P("heads", None),
        P(),
        P(),
        P(),
        P(None, "heads"),
        P("heads"),
        P("heads", None),
        P(),
        P(),
        P(("rows", "heads"), None),
    )
    out_specs = (
        P(("rows", "heads"), None),
        P(),
        P(("rows", "heads"), None),
        P(),
        P(),
        P(),
        P("rows", "heads"),
        P("rows", "heads"),
        P("rows", "heads"),
        P("heads"),
        P("heads"),
        P("heads", "rows"),
        P(),
        P(),
        P(),
        P("rows", "heads"),
        P("heads"),
        P("heads", "rows"),
        P(),
        P(),
    )
    return jax.shard_map(
        functools.partial(per_device, mesh.shape["rows"]),
        mesh=mesh,
        in_specs=in_specs,
        out_specs=out_specs,
        check_vma=False,
    )
```

```python
import functools

import jax
import jax.numpy as jnp
from jax import lax
from jax.experimental import pallas as pl
from jax.experimental.pallas import tpu as pltpu
from jax.sharding import PartitionSpec as P

HEAD_DIM = 64
PAIR = 2 * HEAD_DIM
NEG = -1e30
SCALE = HEAD_DIM ** (-0.5)
entropy_weight = 16.0
f32 = jnp.float32
bf16 = jnp.bfloat16
NT = (((1,), (1,)), ((), ()))
TN = (((0,), (0,)), ((), ()))
NN = (((1,), (0,)), ((), ()))
VMEM_LIMIT = 56 << 20
COST_SHARE = 20


def cost(flops, size):
    return pl.CostEstimate(flops=flops // COST_SHARE, transcendentals=0, bytes_accessed=size // COST_SHARE)


def mm(a, b, dims=NN):
    return lax.dot_general(a, b, dims, preferred_element_type=f32)


def layer_norm(values, gain, shift):
    centre = values - jnp.mean(values, axis=-1, keepdims=True)
    spread = jnp.mean(centre * centre, axis=-1, keepdims=True)
    return centre * lax.rsqrt(spread + 1e-05) * gain + shift


def gelu_exact(values):
    return jax.nn.gelu(values, approximate=False)


def split3(x):
    hi = x.astype(bf16).astype(f32)
    mid = (x - hi).astype(bf16).astype(f32)
    return hi, mid, x - hi - mid


def pair_masks():
    lane = lax.broadcasted_iota(jnp.int32, (1, PAIR), 1)
    return lane, (lane < HEAD_DIM, lane >= HEAD_DIM), (HEAD_DIM, 0)


def own_part(h):
    return slice(0, HEAD_DIM) if h == 0 else slice(HEAD_DIM, PAIR)


def key_bias(meta, keys):
    kpos = meta[0] + lax.broadcasted_iota(jnp.int32, (keys, 1), 0)
    return jnp.where(kpos < meta[1], 0.0, NEG)


def attn_fwd_kernel(first, qb, kc, meta, q_ref, k_ref, v_ref, *refs):
    if first:
        acc_ref, ml_ref, st_sc, p_sc = refs
    else:
        acc_in, ml_in, o_ref, e_ref, acc_sc, e_sc, st_sc, p_sc = refs
    rows = q_ref.shape[0]
    keys = k_ref.shape[0]
    lane, inside, free = pair_masks()
    bias = key_bias(meta, keys)
    q32 = q_ref[...].astype(f32) * SCALE
    k32 = k_ref[...].astype(f32)
    v32 = v_ref[...].astype(f32)
    qx = [jnp.where(inside[h], q32, jnp.where(lane == free[h], 1.0, 0.0)).astype(bf16) for h in range(2)]
    kx = [jnp.where(inside[h], k32, bias).astype(bf16) for h in range(2)]
    vx = [jnp.where(inside[h], v32, 1.0).astype(bf16) for h in range(2)]
    units = [(h, b) for h in range(2) for b in range(rows // qb)]
    chunks = [slice(c * kc, (c + 1) * kc) for c in range(keys // kc)]
    m_prev = None
    for u in range(len(units) + 1):
        slot, prev = u % 2, (u - 1) % 2
        if u < len(units):
            h, b = units[u]
            cols = slice(b * qb, (b + 1) * qb)
        m8 = None
        for ch in chunks:
            if u < len(units):
                st = mm(kx[h][ch], qx[h][cols], NT)
                st_sc[slot, ch, :] = st
                top = jnp.max(st.reshape(kc // 8, 8, qb), axis=0)
                m8 = top if m8 is None else jnp.maximum(m8, top)
            if u > 0:
                p_sc[prev, ch, :] = jnp.exp(st_sc[prev, ch, :] - m_prev).astype(bf16)
        if u > 0:
            hp, bp = units[u - 1]
            pc = slice(bp * qb, (bp + 1) * qb)
            ot = mm(vx[hp], p_sc[prev], TN)
            fe = free[hp]
            own = own_part(hp)
            total = ot[fe : fe + 1]
            num = ot[own]
            if first:
                acc_ref[own, pc] = num
                ml_ref[hp : hp + 1, pc] = m_prev
                ml_ref[2 + hp : 3 + hp, pc] = total
            else:
                alpha = jnp.exp(ml_in[hp : hp + 1, pc] - m_prev)
                total = total + alpha * ml_in[2 + hp : 3 + hp, pc]
                num = num + alpha * acc_in[own, pc]
                acc_sc[own, pc] = num / total
                hi, mid, lo = split3(m_prev + jnp.log(total))
                row = lax.broadcasted_iota(jnp.int32, (HEAD_DIM, 1), 0)
                e_sc[fe : fe + HEAD_DIM, pc] = jnp.where(
                    row == 0, 1.0, jnp.where(row == 1, -hi, jnp.where(row == 2, -mid, jnp.where(row == 3, -lo, 0.0)))
                )
        if u < len(units):
            m_prev = jnp.max(m8, axis=0, keepdims=True)
            if not first:
                m_prev = jnp.maximum(m_prev, ml_in[h : h + 1, cols])
    if not first:
        o_ref[...] = acc_sc[...].T.astype(bf16)
        e_ref[...] = e_sc[...].T.astype(bf16)


def attn_fwd(meta, q, k, v, pairs, state=None, qb=1024, kc=256):
    rows = q[0].shape[0]
    keys = k[0].shape[0]
    width = pairs * PAIR
    first = state is None

    def col(off):
        return lambda i, m: (0, off + i)

    def down(i, m):
        return (i, 0)

    in_specs = [
        pl.BlockSpec((rows, PAIR), col(q[1])),
        pl.BlockSpec((keys, PAIR), col(k[1])),
        pl.BlockSpec((keys, PAIR), col(v[1])),
    ]
    scratch = [pltpu.VMEM((2, keys, qb), f32), pltpu.VMEM((2, keys, qb), bf16)]
    args = (q[0], k[0], v[0])
    if first:
        out_shape = (jax.ShapeDtypeStruct((width, rows), f32), jax.ShapeDtypeStruct((8 * pairs, rows), f32))
        out_specs = (pl.BlockSpec((PAIR, rows), down), pl.BlockSpec((8, rows), down))
    else:
        in_specs += [pl.BlockSpec((PAIR, rows), down), pl.BlockSpec((8, rows), down)]
        out_shape = (jax.ShapeDtypeStruct((rows, width), bf16), jax.ShapeDtypeStruct((rows, width), bf16))
        out_specs = (pl.BlockSpec((rows, PAIR), col(0)), pl.BlockSpec((rows, PAIR), col(0)))
        scratch = [pltpu.VMEM((PAIR, rows), f32), pltpu.VMEM((PAIR, rows), f32)] + scratch
        args = args + tuple(state)
    return pl.pallas_call(
        functools.partial(attn_fwd_kernel, first, qb, kc),
        grid_spec=pltpu.PrefetchScalarGridSpec(
            num_scalar_prefetch=1, grid=(pairs,), in_specs=in_specs, out_specs=out_specs, scratch_shapes=scratch
        ),
        out_shape=out_shape,
        compiler_params=pltpu.CompilerParams(vmem_limit_bytes=VMEM_LIMIT),
        cost_estimate=cost(16 * rows * keys * width, 8 * rows * width),
        name="attn_fwd_first" if first else "attn_fwd_second",
    )(meta, *args)


def attn_bwd_kernel(first, qb, kc, meta, q_ref, e_ref, o_ref, do_ref, k_ref, v_ref, *refs):
    if first:
        dq_ref, dk_ref, dv_ref, dk_sc, dv_sc, s_sc, dp_sc, p_sc, ds_sc = refs
    else:
        dq_in, dq_ref, dk_ref, dv_ref, dk_sc, dv_sc, s_sc, dp_sc, p_sc, ds_sc = refs
    rows = q_ref.shape[0]
    keys = k_ref.shape[0]
    lane, inside, free = pair_masks()
    bias = key_bias(meta, keys)
    k32 = k_ref[...].astype(f32)
    v32 = v_ref[...].astype(f32)
    kx = [jnp.where(inside[h], k32, jnp.where(lane == free[h], bias, 1.0)).astype(bf16) for h in range(2)]
    vx = [jnp.where(inside[h], v32, 1.0).astype(bf16) for h in range(2)]
    units = [(b, h) for b in range(rows // qb) for h in range(2)]
    chunks = [slice(c * kc, (c + 1) * kc) for c in range(keys // kc)]
    prep = None
    dq0 = None
    for u in range(len(units) + 1):
        before = prep
        slot, prev = u % 2, (u - 1) % 2
        if u < len(units):
            b, h = units[u]
            rs = slice(b * qb, (b + 1) * qb)
            fe = free[h]
            if h == 0:
                q32 = q_ref[rs].astype(f32) * SCALE
                do32 = do_ref[rs].astype(f32)
                e32 = e_ref[rs].astype(f32)
                prod = do32 * o_ref[rs].astype(f32)
            hi, mid, lo = split3(jnp.sum(jnp.where(inside[h], prod, 0.0), axis=1, keepdims=True))
            dext = jnp.where(lane == fe, -hi, jnp.where(lane == fe + 1, -mid, jnp.where(lane == fe + 2, -lo, 0.0)))
            qx = jnp.where(inside[h], q32, e32).astype(bf16)
            dox = jnp.where(inside[h], do32, dext).astype(bf16)
            prep = (qx, dox)
        for ch in chunks:
            if u < len(units):
                s_sc[slot, :, ch] = mm(qx, kx[h][ch], NT)
                dp_sc[slot, :, ch] = mm(dox, vx[h][ch], NT)
            if u > 0:
                p = jnp.exp(s_sc[prev, :, ch])
                p_sc[prev, :, ch] = p.astype(bf16)
                ds_sc[prev, :, ch] = (p * dp_sc[prev, :, ch]).astype(bf16)
        if u > 0:
            bp, hp = units[u - 1]
            rp = slice(bp * qb, (bp + 1) * qb)
            qxp, doxp = before
            dvt = mm(doxp, p_sc[prev], TN)
            dkt = mm(qxp, ds_sc[prev], TN)
            dqh = mm(ds_sc[prev], kx[hp], NN)
            own = own_part(hp)
            if bp == 0:
                dv_sc[own] = dvt[own]
                dk_sc[own] = dkt[own]
            else:
                dv_sc[own] += dvt[own]
                dk_sc[own] += dkt[own]
            if hp == 0:
                dq0 = dqh
            else:
                dq = jnp.where(lane < HEAD_DIM, dq0, dqh) * SCALE
                if first:
                    dq_ref[rp] = dq
                else:
                    dq_ref[rp] = (dq + dq_in[rp]).astype(bf16)
    dk_ref[...] = dk_sc[...].T.astype(bf16)
    dv_ref[...] = dv_sc[...].T.astype(bf16)


def attn_bwd(meta, q, e, o, do, k, v, pairs, dq_prev=None, qb=256, kc=256):
    rows = q[0].shape[0]
    keys = k[0].shape[0]
    width = pairs * PAIR
    first = dq_prev is None

    def col(off):
        return lambda i, m: (0, off + i)

    in_specs = [pl.BlockSpec((rows, PAIR), col(off)) for _, off in (q, e, o, do)]
    in_specs += [pl.BlockSpec((keys, PAIR), col(off)) for _, off in (k, v)]
    args = (q[0], e[0], o[0], do[0], k[0], v[0])
    rspec = pl.BlockSpec((rows, PAIR), col(0))
    kspec = pl.BlockSpec((keys, PAIR), col(0))
    if not first:
        in_specs.append(rspec)
        args = args + (dq_prev,)
    return pl.pallas_call(
        functools.partial(attn_bwd_kernel, first, qb, kc),
        grid_spec=pltpu.PrefetchScalarGridSpec(
            num_scalar_prefetch=1,
            grid=(pairs,),
            in_specs=in_specs,
            out_specs=(rspec, kspec, kspec),
            scratch_shapes=[pltpu.VMEM((PAIR, keys), f32)] * 2
            + [pltpu.VMEM((2, qb, keys), f32)] * 2
            + [pltpu.VMEM((2, qb, keys), bf16)] * 2,
        ),
        out_shape=(
            jax.ShapeDtypeStruct((rows, width), f32 if first else bf16),
            jax.ShapeDtypeStruct((keys, width), bf16),
            jax.ShapeDtypeStruct((keys, width), bf16),
        ),
        compiler_params=pltpu.CompilerParams(vmem_limit_bytes=VMEM_LIMIT),
        cost_estimate=cost(40 * rows * keys * width, 16 * rows * width),
        name="attn_bwd_first" if first else "attn_bwd_second",
    )(meta, *args)


FF_BLOCK = 768
EARLY = (0, 1)
CHUNK = 256


def row_chunks(rows):
    return [slice(c, c + CHUNK) for c in range(0, rows, CHUNK)]


EMB, B_OUT, GAIN_2, SHIFT_2, B_DOWN, GAIN_1, SHIFT_1 = (slice(i, i + 1) for i in range(7))


def normalise(values):
    centre = values - jnp.mean(values, axis=-1, keepdims=True)
    spread = jnp.mean(centre * centre, axis=-1, keepdims=True)
    rstd = lax.rsqrt(spread + 1e-05)
    return centre * rstd, rstd


def gelu_pair(u):
    cdf = 0.5 * (1.0 + lax.erf(u * 0.7071067811865476))
    density = 0.3989422804014327 * jnp.exp(-0.5 * u * u)
    return u * cdf, cdf + u * density


def pick(step, n_own, own, other):
    return jnp.where(step < n_own, own, other)


def mid_fwd_kernel(
    n_own, scal, tok_ref, vec_ref, o0_ref, o1_ref, wo_ref, wo2_ref, bup_ref, up_ref, up2_ref,
    down_ref, down2_ref, wg_ref, cnt_ref, cot_ref,
    h1_ref, nt_ref, g_ref, gp_ref, out_ref, dm_ref, dout_ref, sums_ref, acc,
):
    step = pl.program_id(0)
    last = pl.num_programs(0) - 1
    rows, width = tok_ref.shape
    chunks = row_chunks(rows)

    @pl.when(step == 0)
    def _():
        wo2 = wo2_ref[...].reshape(wo_ref.shape)
        for c in chunks:
            h1 = tok_ref[c].astype(f32) + vec_ref[EMB]
            h1 = h1 + (mm(o0_ref[c], wo_ref[...]) + mm(o1_ref[c], wo2) + vec_ref[B_OUT])
            h1_ref[c] = h1
            xhat, _ = normalise(h1)
            nt_ref[c] = (xhat * vec_ref[GAIN_2] + vec_ref[SHIFT_2]).astype(bf16)
            acc[c] = h1 + vec_ref[B_DOWN]

    up = pick(step, n_own, up_ref[...], up2_ref[...].reshape(up_ref.shape))
    down = pick(step, n_own, down_ref[...], down2_ref[...].reshape(down_ref.shape))
    u = mm(nt_ref[chunks[0]], up)
    for i, c in enumerate(chunks):
        ahead = mm(nt_ref[chunks[i + 1]], up) if i + 1 < len(chunks) else None
        g, gp = gelu_pair(u + bup_ref[...])
        g = g.astype(bf16)
        g_ref[c] = g
        gp_ref[c] = gp.astype(bf16)
        acc[c] += mm(g, down)
        u = ahead

    @pl.when(step == last)
    def _():
        dbd = jnp.zeros((1, width), f32)
        dwg = [jnp.zeros((1, width), f32) for _ in range(3)]
        ent_sum = jnp.zeros((1, 1), f32)
        for c in chunks:
            out = acc[c]
            out_ref[c] = out.astype(bf16)
            z = [jnp.sum(out * wg_ref[e : e + 1], axis=-1, keepdims=True) for e in range(3)]
            top = jnp.maximum(jnp.maximum(z[0], z[1]), z[2])
            log_sum = jnp.log(sum(jnp.exp(v - top) for v in z)) + top
            logp = [v - log_sum for v in z]
            prob = [jnp.exp(v) for v in logp]
            entropy = -sum(p * q for p, q in zip(prob, logp))
            mean = sum(p * v for p, v in zip(prob, z))
            counted = cnt_ref[c]
            ent_sum = ent_sum + jnp.sum(counted * entropy, axis=0, keepdims=True)
            dz = [scal[0] * counted * (-p * (v - mean)) for p, v in zip(prob, z)]
            d_out = cot_ref[c].astype(f32) + sum(d * wg_ref[e : e + 1] for e, d in enumerate(dz))
            dout_ref[c] = d_out
            dm = d_out.astype(bf16)
            dm_ref[c] = dm
            dbd = dbd + jnp.sum(dm.astype(f32), axis=0, keepdims=True)
            dwg = [w + jnp.sum(out * d, axis=0, keepdims=True) for w, d in zip(dwg, dz)]
        sums_ref[...] = jnp.zeros_like(sums_ref)
        for e in range(3):
            sums_ref[3 + e : 4 + e] = dwg[e]
        sums_ref[6:7] = dbd
        sums_ref[7:8] = jnp.broadcast_to(ent_sum, (1, width))


def fixed(shape):
    zeros = (0,) * len(shape)
    return pl.BlockSpec(shape, lambda *_: zeros)


def weight_specs(gathered, width, ff):
    n_own = ff // FF_BLOCK
    parts, _, _ = gathered.shape
    k_up, k_down = width // parts, ff // parts
    per_step = FF_BLOCK // k_down
    cols = width // FF_BLOCK

    def other(j):
        return jnp.maximum(j - n_own, 0)

    return n_own, [
        pl.BlockSpec((width, FF_BLOCK), lambda j, *_: (0, jnp.minimum(j, n_own - 1))),
        pl.BlockSpec((parts, k_up, FF_BLOCK), lambda j, *_: (0, other(j) // cols, other(j) % cols)),
        pl.BlockSpec((FF_BLOCK, width), lambda j, *_: (jnp.minimum(j, n_own - 1), 0)),
        pl.BlockSpec((per_step, k_down, width), lambda j, *_: (other(j), 2 * k_up // k_down, 0)),
    ]


def out_spec(gathered, width, ff, hw):
    parts = gathered.shape[0]
    k_out = hw // parts
    return pl.BlockSpec((parts, k_out, width), lambda *_: (0, (2 * width + ff) // parts // k_out, 0))


def mid_fwd(scal, tokens, vecs, o0, o1, w_out, gathered, b_up, w_up, w_down, wg, counted, cot):
    rows, width = tokens.shape
    ff = w_down.shape[0]
    n_own, (up_s, up2_s, down_s, down2_s) = weight_specs(gathered, width, ff)
    hw = w_out.shape[0]
    vec = fixed((8, width))
    full = fixed((rows, width))
    blk = pl.BlockSpec((rows, FF_BLOCK), lambda j, *_: (0, j))
    return pl.pallas_call(
        functools.partial(mid_fwd_kernel, n_own),
        grid_spec=pltpu.PrefetchScalarGridSpec(
            num_scalar_prefetch=1,
            grid=(2 * n_own,),
            in_specs=[
                full, vec, fixed((rows, hw)), fixed((rows, hw)), fixed((hw, width)), out_spec(gathered, width, ff, hw),
                pl.BlockSpec((1, FF_BLOCK), lambda j, *_: (0, j)), up_s, up2_s, down_s, down2_s,
                vec, fixed((rows, 1)), full,
            ],
            out_specs=[full, full, blk, blk, full, full, full, fixed((8, width))],
            scratch_shapes=[pltpu.VMEM((rows, width), f32)],
        ),
        out_shape=[
            jax.ShapeDtypeStruct((rows, width), f32),
            jax.ShapeDtypeStruct((rows, width), bf16),
            jax.ShapeDtypeStruct((rows, 2 * ff), bf16),
            jax.ShapeDtypeStruct((rows, 2 * ff), bf16),
            jax.ShapeDtypeStruct((rows, width), bf16),
            jax.ShapeDtypeStruct((rows, width), bf16),
            jax.ShapeDtypeStruct((rows, width), f32),
            jax.ShapeDtypeStruct((8, width), f32),
        ],
        compiler_params=pltpu.CompilerParams(vmem_limit_bytes=VMEM_LIMIT),
        cost_estimate=cost(12 * rows * width * ff, 40 * rows * width),
        name="mid_fwd",
    )(
        scal, tokens, vecs, o0, o1, w_out, gathered, b_up, w_up, gathered, w_down, gathered, wg, counted, cot,
    )


def mid_bwd_kernel(
    n_own, dm_ref, nt_ref, h1_ref, dout_ref, vec_ref, g_ref, gp_ref, up_ref, up2_ref, down_ref, down2_ref,
    grads_ref, dh_ref, da_ref, sums_ref, acc, du_sc,
):
    step = pl.program_id(0)
    last = pl.num_programs(0) - 1
    rows, width = dm_ref.shape
    chunks = row_chunks(rows)
    up = pick(step, n_own, up_ref[...], up2_ref[...].reshape(up_ref.shape))
    down = pick(step, n_own, down_ref[...], down2_ref[...].reshape(down_ref.shape))

    @pl.when(step == 0)
    def _():
        acc[...] = jnp.zeros_like(acc)
        sums_ref[...] = jnp.zeros_like(sums_ref)

    bias = jnp.zeros((1, FF_BLOCK), f32)
    for c in chunks:
        du = (mm(dm_ref[c], down, NT) * gp_ref[c].astype(f32)).astype(bf16)
        du_sc[c] = du
        bias = bias + jnp.sum(du.astype(f32), axis=0, keepdims=True)
        acc[c] += mm(du, up, NT)
    sums_ref[pl.ds(8 + 4 * (step // n_own) + step % n_own, 1)] = bias
    grads_ref[:, :FF_BLOCK] = mm(dm_ref[...], g_ref[...], TN).astype(bf16)
    grads_ref[:, FF_BLOCK:] = mm(nt_ref[...], du_sc[...], TN).astype(bf16)

    @pl.when(step == last)
    def _():
        d_gain = jnp.zeros((1, width), f32)
        d_shift = jnp.zeros((1, width), f32)
        d_bias = jnp.zeros((1, width), f32)
        for c in chunks:
            db = acc[c]
            xhat, rstd = normalise(h1_ref[c])
            d_gain = d_gain + jnp.sum(db * xhat, axis=0, keepdims=True)
            d_shift = d_shift + jnp.sum(db, axis=0, keepdims=True)
            dx = db * vec_ref[GAIN_2]
            low = jnp.mean(dx, axis=-1, keepdims=True)
            slope = jnp.mean(dx * xhat, axis=-1, keepdims=True)
            dh = dout_ref[c] + rstd * (dx - low - xhat * slope)
            dh_ref[c] = dh
            da = dh.astype(bf16)
            da_ref[c] = da
            d_bias = d_bias + jnp.sum(da.astype(f32), axis=0, keepdims=True)
        sums_ref[0:1] = d_gain
        sums_ref[1:2] = d_shift
        sums_ref[2:3] = d_bias


def mid_bwd(dm, normed, h1, d_out, vecs, g, gp, w_up, w_down, gathered, grad_cols):
    rows, width = dm.shape
    ff = w_down.shape[0]
    n_own, (up_s, up2_s, down_s, down2_s) = weight_specs(gathered, width, ff)
    full = fixed((rows, width))
    blk = pl.BlockSpec((rows, FF_BLOCK), lambda j, *_: (0, j))
    return pl.pallas_call(
        functools.partial(mid_bwd_kernel, n_own),
        grid=(2 * n_own,),
        in_specs=[full, full, full, full, fixed((8, width)), blk, blk, up_s, up2_s, down_s, down2_s],
        out_specs=[
            pl.BlockSpec((width, 2 * FF_BLOCK), lambda j: (0, j)),
            full,
            full,
            fixed((16, width)),
        ],
        scratch_shapes=[pltpu.VMEM((rows, width), f32), pltpu.VMEM((rows, FF_BLOCK), bf16)],
        out_shape=[
            jax.ShapeDtypeStruct((width, grad_cols), bf16),
            jax.ShapeDtypeStruct((rows, width), f32),
            jax.ShapeDtypeStruct((rows, width), bf16),
            jax.ShapeDtypeStruct((16, width), f32),
        ],
        compiler_params=pltpu.CompilerParams(vmem_limit_bytes=VMEM_LIMIT),
        cost_estimate=cost(24 * rows * width * ff, 40 * rows * width),
        name="mid_bwd",
    )(dm, normed, h1, d_out, vecs, g, gp, w_up, gathered, w_down, gathered)


def out_bwd_kernel(da_ref, o0_ref, o1_ref, wo_ref, wo2_ref, _, do_ref, do2_ref, grads_ref):
    hw = wo_ref.shape[0]
    do_ref[...] = mm(da_ref[...], wo_ref[...], NT).astype(bf16)
    do2_ref[...] = mm(da_ref[...], wo2_ref[...].reshape(wo_ref.shape), NT).astype(bf16)
    grads_ref[:, :hw] = mm(da_ref[...], o0_ref[...], TN).astype(bf16)
    grads_ref[:, hw:] = mm(da_ref[...], o1_ref[...], TN).astype(bf16)


def out_bwd(d_attn, o0, o1, w_out, gathered, ff, grads):
    rows, width = d_attn.shape
    hw = w_out.shape[0]
    half = fixed((rows, hw))
    return pl.pallas_call(
        out_bwd_kernel,
        grid=(1,),
        in_specs=[
            fixed((rows, width)), half, half, fixed((hw, width)), out_spec(gathered, width, ff, hw),
            pl.BlockSpec(memory_space=pl.ANY),
        ],
        out_specs=[half, half, pl.BlockSpec((width, 2 * hw), lambda j: (0, grads.shape[1] // (2 * hw) - 1))],
        out_shape=[
            jax.ShapeDtypeStruct((rows, hw), bf16),
            jax.ShapeDtypeStruct((rows, hw), bf16),
            jax.ShapeDtypeStruct(grads.shape, bf16),
        ],
        input_output_aliases={5: 2},
        compiler_params=pltpu.CompilerParams(vmem_limit_bytes=VMEM_LIMIT),
        cost_estimate=cost(8 * rows * width * hw, 12 * rows * width),
        name="out_bwd",
    )(d_attn, o0, o1, w_out, gathered, grads)


def qkv_grads_kernel(n_ref, no_ref, dq_ref, dk_ref, dv_ref, dko_ref, dvo_ref, grads_ref, sums_ref):
    hw = dq_ref.shape[1]
    grads_ref[:, :hw] = mm(n_ref[...], dq_ref[...], TN).astype(bf16)
    grads_ref[:, hw : 2 * hw] = (mm(n_ref[...], dk_ref[...], TN) + mm(no_ref[...], dko_ref[...], TN)).astype(bf16)
    grads_ref[:, 2 * hw :] = (mm(n_ref[...], dv_ref[...], TN) + mm(no_ref[...], dvo_ref[...], TN)).astype(bf16)
    bq = jnp.sum(dq_ref[...].astype(f32), axis=0, keepdims=True)
    bv = jnp.sum(dv_ref[...].astype(f32), axis=0, keepdims=True) + jnp.sum(dvo_ref[...].astype(f32), axis=0, keepdims=True)
    sums_ref[:, :hw] = jnp.broadcast_to(bq, (8, hw))
    sums_ref[:, hw:] = jnp.broadcast_to(bv, (8, hw))


def qkv_grads(normed, normed_oth, dq, dk, dv, dk_oth, dv_oth):
    rows, width = normed.shape
    hw = dq.shape[1]
    full, half = fixed((rows, width)), fixed((rows, hw))
    return pl.pallas_call(
        qkv_grads_kernel,
        grid=(1,),
        in_specs=[full, full] + [half] * 5,
        out_specs=[fixed((width, 3 * hw)), fixed((8, 2 * hw))],
        out_shape=[jax.ShapeDtypeStruct((width, 3 * hw), bf16), jax.ShapeDtypeStruct((8, 2 * hw), f32)],
        compiler_params=pltpu.CompilerParams(vmem_limit_bytes=VMEM_LIMIT),
        cost_estimate=cost(10 * rows * width * hw, 10 * rows * width),
        name="qkv_grads",
    )(normed, normed_oth, dq, dk, dv, dk_oth, dv_oth)


def ln1_bwd_kernel(n_parts, *refs):
    parts, (w0_ref, w1_ref, got_ref, dh_ref, tok_ref, vec_ref, dtok_ref, sums_ref) = refs[:n_parts], refs[n_parts:]
    hw = parts[0].shape[1]
    da = got_ref[...].astype(f32)
    for i, w_ref in enumerate((w0_ref, w1_ref)):
        for j in range(3):
            da = da + mm(parts[3 * i + j][...], w_ref[:, j * hw : (j + 1) * hw], NT)
    xhat, rstd = normalise(tok_ref[...].astype(f32) + vec_ref[EMB])
    dx = da * vec_ref[GAIN_1]
    low = jnp.mean(dx, axis=-1, keepdims=True)
    slope = jnp.mean(dx * xhat, axis=-1, keepdims=True)
    d_tokens = dh_ref[...] + rstd * (dx - low - xhat * slope)
    dtok_ref[...] = d_tokens
    new = [jnp.sum(v, axis=0, keepdims=True) for v in (da * xhat, da, d_tokens)]

    @pl.when(pl.program_id(0) == 0)
    def _():
        sums_ref[...] = jnp.zeros_like(sums_ref)

    for i, v in enumerate(new):
        sums_ref[i : i + 1] += v


def ln1_bwd(d_qkv, w0, w1, da_got, d_hidden, tokens, vecs):
    rows, width = tokens.shape
    hw = d_qkv[0].shape[1]
    step = CHUNK
    blk = pl.BlockSpec((step, width), lambda i: (i, 0))
    half = pl.BlockSpec((step, hw), lambda i: (i, 0))
    return pl.pallas_call(
        functools.partial(ln1_bwd_kernel, len(d_qkv)),
        grid=(rows // step,),
        in_specs=[half] * len(d_qkv) + [fixed((width, 3 * hw))] * 2 + [blk, blk, blk, fixed((8, width))],
        out_specs=[blk, fixed((8, width))],
        out_shape=[jax.ShapeDtypeStruct((rows, width), f32), jax.ShapeDtypeStruct((8, width), f32)],
        compiler_params=pltpu.CompilerParams(vmem_limit_bytes=VMEM_LIMIT),
        cost_estimate=cost(12 * rows * width * hw, 20 * rows * width),
        name="ln1_bwd",
    )(*d_qkv, w0, w1, da_got, d_hidden, tokens, vecs)


def front_kernel(starts, tok_ref, vec_ref, *refs):
    n = len(starts)
    xhat, _ = normalise(tok_ref[...].astype(f32) + vec_ref[EMB])
    normed = (xhat * vec_ref[GAIN_1] + vec_ref[SHIFT_1]).astype(bf16)
    refs[2 * n][...] = normed
    for i, start in enumerate(starts):
        y = mm(normed, refs[2 * i][:, start:]) + refs[2 * i + 1][:, start:]
        refs[2 * n + 1 + i][...] = y.astype(bf16)


def front(tokens, vecs, weights):
    rows, width = tokens.shape
    step = CHUNK
    in_specs = [pl.BlockSpec((step, width), lambda i: (i, 0)), fixed((8, width))]
    args = [tokens, vecs]
    outs = [width]
    for w, b, start in weights:
        in_specs += [fixed(w.shape), fixed(b.shape)]
        args += [w, b]
        outs.append(w.shape[1] - start)
    return pl.pallas_call(
        functools.partial(front_kernel, tuple(start for _, _, start in weights)),
        grid=(rows // step,),
        in_specs=in_specs,
        out_specs=[pl.BlockSpec((step, n), lambda i: (i, 0)) for n in outs],
        out_shape=[jax.ShapeDtypeStruct((rows, n), bf16) for n in outs],
        compiler_params=pltpu.CompilerParams(vmem_limit_bytes=VMEM_LIMIT),
        cost_estimate=cost(2 * rows * width * sum(outs[1:]), 8 * rows * width),
        name="front",
    )(*args)


def pack_kernel(row, up_ref, down_ref, out_ref, rest_ref, share_ref):
    width = share_ref.shape[1]
    at = 0
    for part in (up_ref[:, :width], up_ref[:, width:], down_ref[...], out_ref[...], rest_ref[...]):
        share_ref[at : at + part.shape[0]] = part
        at += part.shape[0]


def pack_share(row, n_rows, w_up, w_down, w_out, rest):
    width = w_out.shape[1]
    sizes = [w.shape[0] // n_rows for w in (w_up, w_down, w_out)]
    total = 2 * sizes[0] + sizes[1] + sizes[2] + rest.shape[0]
    if sizes[0] % 16:
        up, down, out = (lax.dynamic_slice_in_dim(w, row * k, k, 0) for w, k in zip((w_up, w_down, w_out), sizes))
        return jnp.concatenate([up[:, :width], up[:, width:], down, out, rest])
    return pl.pallas_call(
        pack_kernel,
        grid_spec=pltpu.PrefetchScalarGridSpec(
            num_scalar_prefetch=1,
            grid=(1,),
            in_specs=[pl.BlockSpec((k, w.shape[1]), lambda i, r: (r[0], 0)) for w, k in zip((w_up, w_down, w_out), sizes)]
            + [fixed(rest.shape)],
            out_specs=fixed((total, width)),
        ),
        out_shape=jax.ShapeDtypeStruct((total, width), bf16),
        name="pack_share",
    )(row.reshape(1), w_up, w_down, w_out, rest)


class Net:
    def __init__(self, n_rows):
        self.n_rows = n_rows
        self.bits = n_rows.bit_length() - 1
        self.row = lax.axis_index("rows")

    def cross(self, x):
        return lax.ppermute(x, "heads", [(0, 1), (1, 0)])

    def flip(self, x, bit):
        return lax.ppermute(x, "rows", [(i, i ^ (1 << bit)) for i in range(self.n_rows)])

    def bit(self, b):
        return (self.row >> b) & 1

    def fetch(self, own):
        part = own.shape[0] // 2
        return self.cross(lax.dynamic_slice_in_dim(own, self.bit(0) * part, part, 0))

    def join(self, got):
        passed = self.flip(got, 0)
        low = self.bit(0) == 0
        return jnp.concatenate([jnp.where(low, got, passed), jnp.where(low, passed, got)], axis=0)

    def halve(self, part, left, step):
        low = 1 << left.index(step)
        blocks, piece, cols = part.shape
        view = part.reshape(blocks // (2 * low), 2, low, piece, cols)
        at = self.bit(step)
        keep = lax.dynamic_index_in_dim(view, at, 1, keepdims=False)
        got = self.flip(lax.dynamic_index_in_dim(view, 1 - at, 1, keepdims=False).astype(bf16), step)
        return (keep.astype(f32) + got.astype(f32)).reshape(blocks // 2, piece, cols), [x for x in left if x != step]


def per_device(
    n_rows,
    tokens,
    crop_lengths,
    lead_index,
    valid_mask,
    lead_table,
    ln1_gain,
    ln1_shift,
    w_query,
    w_key,
    w_value,
    b_query,
    b_value,
    w_out,
    b_out,
    ln2_gain,
    ln2_shift,
    w_up,
    b_up,
    w_down,
    b_down,
    w_gater,
    cotangent,
):
    net = Net(n_rows)
    own_rows, width = tokens.shape
    half = lax.axis_index("heads")
    length = crop_lengths[0]
    hw = w_query.shape[1]
    pairs = hw // PAIR
    own_start = half * own_rows
    meta_own = jnp.stack([own_start, length])
    meta_oth = jnp.stack([own_rows - own_start, length])

    positions = own_start + jnp.arange(own_rows, dtype=jnp.int32)
    counted = ((positions < length) & (valid_mask == 1)).astype(f32)
    count = jnp.sum(counted)

    qkv_w = jnp.concatenate([w_query, w_key, w_value], axis=1)
    bias_own = jnp.concatenate([b_query, b_value, b_up]).reshape(1, -1)
    k_up, k_down, k_out = width // n_rows, w_down.shape[0] // n_rows, w_out.shape[0] // n_rows
    n_share = 2 * k_up + k_down + k_out
    pad = -n_share % 16 + 16
    n_bias = bias_own.size // width
    line = lax.broadcasted_iota(jnp.int32, (pad, width), 0)
    lane = lax.broadcasted_iota(jnp.int32, (pad, width), 1)
    high = jnp.floor(count / 32)
    tally = jnp.where(lane == 0, high, jnp.where(lane == 1, count - 32 * high, 0.0)).astype(bf16)
    rest = tally
    for i in range(n_bias):
        rest = jnp.where(line == 1 + i, bias_own[:, i * width : (i + 1) * width], rest)
    got = net.cross(pack_share(net.row, n_rows, w_up, w_down, w_out, rest))
    bias_oth = got[n_share + 1 : n_share + 1 + n_bias].reshape(1, -1)
    tokens_in, got = lax.optimization_barrier((tokens, got))
    share = jnp.concatenate([got, tally], axis=0)
    tokens_oth = net.cross(tokens)
    at = lax.broadcasted_iota(jnp.int32, (8, 1), 0)
    picked = jnp.arange(lead_table.shape[0], dtype=jnp.int32) == lead_index[0]
    embedding = jnp.sum(jnp.where(picked[:, None], lead_table, 0.0), axis=0)
    vecs = jnp.zeros((8, width), f32)
    for i, v in enumerate((embedding, b_out, ln2_gain, ln2_shift, b_down, ln1_gain, ln1_shift)):
        vecs = jnp.where(at == i, v, vecs)

    def qkv_bias(b):
        b = b.astype(f32)
        return jnp.concatenate([b[:, :hw], jnp.zeros((1, hw), f32), b[:, hw : 2 * hw]], axis=1)

    qkv_b = qkv_bias(bias_own)
    normed, qkv_own = front(tokens_in, vecs, [(qkv_w, qkv_b, 0)])
    gathered = lax.all_gather(share, "rows", axis=0, tiled=False)
    tally = gathered[:, n_share:, :2].astype(f32)
    count_total = jnp.sum(tally[:, 0] * jnp.array([32.0, 1.0])) + jnp.sum(tally[:, pad] * jnp.array([32.0, 1.0]))
    if k_up % 16 or k_down % 16:
        sizes = (k_up, k_up, k_down, k_out)
        starts = (0, k_up, 2 * k_up, 2 * k_up + k_down)
        gathered = jnp.concatenate(
            [gathered[:, a : a + k].reshape(16, k * n_rows // 16, width) for a, k in zip(starts, sizes)], axis=1
        )

    qkv_b2 = qkv_bias(bias_oth)
    up_b, up_b2 = bias_own[:, 2 * hw :].astype(f32), bias_oth[:, 2 * hw :].astype(f32)

    state = attn_fwd(meta_own, (qkv_own, 0), (qkv_own, pairs), (qkv_own, 2 * pairs), pairs)
    tokens_oth, state, qkv_in = lax.optimization_barrier((tokens_oth, state, qkv_w))
    got_w = net.fetch(qkv_in)
    normed_oth, kv_own = front(tokens_oth, vecs, [(qkv_w, qkv_b, hw)])
    attn_own, ext_own = attn_fwd(meta_oth, (qkv_own, 0), (kv_own, 0), (kv_own, pairs), pairs, state)
    got_w, attn_own = lax.optimization_barrier((got_w, attn_own))
    qkv_w2 = net.join(got_w)
    qkv_two = (mm(normed, qkv_w2) + qkv_b2).astype(bf16)
    kv_two = (mm(normed_oth, qkv_w2[:, hw:]) + qkv_b2[:, hw:]).astype(bf16)
    state = attn_fwd(meta_own, (qkv_two, 0), (qkv_two, pairs), (qkv_two, 2 * pairs), pairs)
    attn_two, ext_two = attn_fwd(meta_oth, (qkv_two, 0), (kv_two, 0), (kv_two, pairs), pairs, state)
    qkv, kv_oth, attn, ext = (qkv_own, qkv_two), (kv_own, kv_two), (attn_own, attn_two), (ext_own, ext_two)

    ff = w_down.shape[0]
    h1, normed_two, act, slope, block_out, d_branch, d_output, sums_f = mid_fwd(
        (entropy_weight / count_total).reshape(1),
        tokens,
        vecs,
        attn[0],
        attn[1],
        w_out,
        gathered,
        jnp.concatenate([up_b, up_b2], axis=1),
        w_up,
        w_down,
        jnp.concatenate([w_gater.T, jnp.zeros((5, width), f32)]),
        counted.reshape(-1, 1),
        cotangent,
    )
    grad_cols = 4 * ff + 2 * hw
    grads, d_hidden, d_attn, sums_b = mid_bwd(
        d_branch, normed_two, h1, d_output, vecs, act, slope, w_up, w_down, gathered, grad_cols
    )
    do_own, do_oth, grads = out_bwd(d_attn, attn[0], attn[1], w_out, gathered, ff, grads)
    d_heads = (do_own, do_oth)
    grads = lax.psum_scatter(grads, "rows", scatter_dimension=0, tiled=True)

    dq, dk_oth, dv_oth = [], [], []
    for i in range(2):
        a, b, c = attn_bwd(
            meta_oth, (qkv[i], 0), (ext[i], 0), (attn[i], 0), (d_heads[i], 0), (kv_oth[i], 0), (kv_oth[i], pairs), pairs
        )
        dq.append(a)
        dk_oth.append(b)
        dv_oth.append(c)
    ws = (qkv_w, qkv_w2)
    da_oth = sum(
        mm(dk_oth[i], ws[i][:, hw : 2 * hw], NT) + mm(dv_oth[i], ws[i][:, 2 * hw :], NT) for i in range(2)
    ).astype(bf16)
    dq, da_oth = lax.optimization_barrier((dq, da_oth))
    da_got = net.cross(da_oth)
    d_qkv, g_qkv, bias_rows = [None] * 2, [None] * 2, [None] * 2
    for i in (1, 0):
        d_qkv[i] = attn_bwd(
            meta_own,
            (qkv[i], 0),
            (ext[i], 0),
            (attn[i], 0),
            (d_heads[i], 0),
            (qkv[i], pairs),
            (qkv[i], 2 * pairs),
            pairs,
            dq[i],
        )
        if i == 0:
            d_qkv[0], oth = lax.optimization_barrier((d_qkv[0], oth))
        g_qkv[i], bias_rows[i] = qkv_grads(normed, normed_oth, *d_qkv[i], dk_oth[i], dv_oth[i])
        if i == 1:
            dq[0], g_qkv[1] = lax.optimization_barrier((dq[0], g_qkv[1]))
            oth, left = g_qkv[1].reshape(n_rows, -1, 3 * hw), list(range(net.bits))
            for step in EARLY:
                oth, left = net.halve(oth, left, step)
    own, left2 = g_qkv[0].reshape(n_rows, -1, 3 * hw), list(range(net.bits))
    own, left2 = net.halve(own, left2, 0)
    d_tokens, sums_t = ln1_bwd([*d_qkv[0], *d_qkv[1]], qkv_w, qkv_w2, da_got, d_hidden, tokens, vecs)
    while left:
        oth, left = net.halve(oth, left, left[0])
    oth = net.cross(oth.reshape(-1, 3 * hw).astype(bf16)).astype(f32)
    d_table = jnp.where(picked[:, None], sums_t[2:3], 0.0)
    n_lead = lead_table.shape[0]
    split = sums_b[8:] + jnp.where(at == 2, bias_rows[0], 0.0) + jnp.where(at == 6, bias_rows[1], 0.0)
    late = jnp.concatenate([sums_t + sums_f, sums_b[:8], d_table, split])
    waiting = list(range(net.bits))
    while left2:
        for step in waiting[:2] if len(left2) == net.bits - 1 else waiting[:1]:
            late = late + net.flip(late, step)
            waiting.remove(step)
        own, left2 = net.halve(own, left2, left2[0])
        own, late = lax.optimization_barrier((own, late))
    for step in waiting:
        late = late + net.flip(late, step)
    g_qkv_sum = own.reshape(-1, 3 * hw) + oth
    late = late + net.cross(jnp.concatenate([late[: 16 + n_lead], jnp.roll(late[16 + n_lead :], 4, axis=0)], axis=0))
    split = late[16 + n_lead :]
    penalty = late[7, 0] / count_total
    d_bias_qv, d_bias_up_own = split[2], split[: ff // width].reshape(-1)
    got = net.cross(jnp.concatenate([grads[:, 2 * ff : 4 * ff], grads[:, 4 * ff + hw :]], axis=1)).astype(f32)
    grads = jnp.concatenate([grads[:, : 2 * ff], grads[:, 4 * ff : 4 * ff + hw]], axis=1).astype(f32) + got
    blocks = [grads[:, k * FF_BLOCK : (k + 1) * FF_BLOCK] for k in range(2 * ff // FF_BLOCK)]
    g_down = jnp.concatenate(blocks[0::2], axis=1)
    g_up = jnp.concatenate(blocks[1::2], axis=1)
    g_out = grads[:, 2 * ff :]
    return (
        block_out,
        penalty,
        d_tokens,
        late[16 : 16 + n_lead],
        late[0],
        late[1],
        g_qkv_sum[:, :hw],
        g_qkv_sum[:, hw : 2 * hw],
        g_qkv_sum[:, 2 * hw :],
        d_bias_qv[:hw],
        d_bias_qv[hw:],
        g_out.T,
        late[10],
        late[8],
        late[9],
        g_up,
        d_bias_up_own,
        g_down.T,
        late[6],
        late[3:6].T,
    )


def solution(mesh):
    in_specs = (
        P(("rows", "heads"), None),
        P("rows"),
        P("rows"),
        P(("rows", "heads")),
        P(),
        P(),
        P(),
        P(None, "heads"),
        P(None, "heads"),
        P(None, "heads"),
        P("heads"),
        P("heads"),
        P("heads", None),
        P(),
        P(),
        P(),
        P(None, "heads"),
        P("heads"),
        P("heads", None),
        P(),
        P(),
        P(("rows", "heads"), None),
    )
    out_specs = (
        P(("rows", "heads"), None),
        P(),
        P(("rows", "heads"), None),
        P(),
        P(),
        P(),
        P("rows", "heads"),
        P("rows", "heads"),
        P("rows", "heads"),
        P("heads"),
        P("heads"),
        P("heads", "rows"),
        P(),
        P(),
        P(),
        P("rows", "heads"),
        P("heads"),
        P("heads", "rows"),
        P(),
        P(),
    )
    return jax.shard_map(
        functools.partial(per_device, mesh.shape["rows"]),
        mesh=mesh,
        in_specs=in_specs,
        out_specs=out_specs,
        check_vma=False,
    )
```

```python
import functools

import jax
import jax.numpy as jnp
from jax import lax
from jax.experimental import pallas as pl
from jax.experimental.pallas import tpu as pltpu
from jax.sharding import PartitionSpec as P

HEAD_DIM = 64
PAIR = 2 * HEAD_DIM
NEG = -1e30
SCALE = HEAD_DIM ** (-0.5)
entropy_weight = 16.0
f32 = jnp.float32
bf16 = jnp.bfloat16
NT = (((1,), (1,)), ((), ()))
TN = (((0,), (0,)), ((), ()))
NN = (((1,), (0,)), ((), ()))
VMEM_LIMIT = 56 << 20
COST_SHARE = 20


def cost(flops, size):
    return pl.CostEstimate(flops=flops // COST_SHARE, transcendentals=0, bytes_accessed=size // COST_SHARE)


def mm(a, b, dims=NN):
    return lax.dot_general(a, b, dims, preferred_element_type=f32)


def layer_norm(values, gain, shift):
    centre = values - jnp.mean(values, axis=-1, keepdims=True)
    spread = jnp.mean(centre * centre, axis=-1, keepdims=True)
    return centre * lax.rsqrt(spread + 1e-05) * gain + shift


def gelu_exact(values):
    return jax.nn.gelu(values, approximate=False)


def split3(x):
    hi = x.astype(bf16).astype(f32)
    mid = (x - hi).astype(bf16).astype(f32)
    return hi, mid, x - hi - mid


def pair_masks():
    lane = lax.broadcasted_iota(jnp.int32, (1, PAIR), 1)
    return lane, (lane < HEAD_DIM, lane >= HEAD_DIM), (HEAD_DIM, 0)


def own_part(h):
    return slice(0, HEAD_DIM) if h == 0 else slice(HEAD_DIM, PAIR)


def key_bias(meta, keys):
    kpos = meta[0] + lax.broadcasted_iota(jnp.int32, (keys, 1), 0)
    return jnp.where(kpos < meta[1], 0.0, NEG)


def attn_fwd_kernel(first, qb, kc, meta, q_ref, k_ref, v_ref, *refs):
    if first:
        acc_ref, ml_ref, st_sc, p_sc = refs
    else:
        acc_in, ml_in, o_ref, e_ref, acc_sc, e_sc, st_sc, p_sc = refs
    rows = q_ref.shape[0]
    keys = k_ref.shape[0]
    lane, inside, free = pair_masks()
    bias = key_bias(meta, keys)
    q32 = q_ref[...].astype(f32) * SCALE
    k32 = k_ref[...].astype(f32)
    v32 = v_ref[...].astype(f32)
    qx = [jnp.where(inside[h], q32, jnp.where(lane == free[h], 1.0, 0.0)).astype(bf16) for h in range(2)]
    kx = [jnp.where(inside[h], k32, bias).astype(bf16) for h in range(2)]
    vx = [jnp.where(inside[h], v32, 1.0).astype(bf16) for h in range(2)]
    units = [(h, b) for h in range(2) for b in range(rows // qb)]
    chunks = [slice(c * kc, (c + 1) * kc) for c in range(keys // kc)]
    m_prev = None
    for u in range(len(units) + 1):
        slot, prev = u % 2, (u - 1) % 2
        if u < len(units):
            h, b = units[u]
            cols = slice(b * qb, (b + 1) * qb)
        m8 = None
        for ch in chunks:
            if u < len(units):
                st = mm(kx[h][ch], qx[h][cols], NT)
                st_sc[slot, ch, :] = st
                top = jnp.max(st.reshape(kc // 8, 8, qb), axis=0)
                m8 = top if m8 is None else jnp.maximum(m8, top)
            if u > 0:
                p_sc[prev, ch, :] = jnp.exp(st_sc[prev, ch, :] - m_prev).astype(bf16)
        if u > 0:
            hp, bp = units[u - 1]
            pc = slice(bp * qb, (bp + 1) * qb)
            ot = mm(vx[hp], p_sc[prev], TN)
            fe = free[hp]
            own = own_part(hp)
            total = ot[fe : fe + 1]
            num = ot[own]
            if first:
                acc_ref[own, pc] = num
                ml_ref[hp : hp + 1, pc] = m_prev
                ml_ref[2 + hp : 3 + hp, pc] = total
            else:
                alpha = jnp.exp(ml_in[hp : hp + 1, pc] - m_prev)
                total = total + alpha * ml_in[2 + hp : 3 + hp, pc]
                num = num + alpha * acc_in[own, pc]
                acc_sc[own, pc] = num / total
                hi, mid, lo = split3(m_prev + jnp.log(total))
                row = lax.broadcasted_iota(jnp.int32, (HEAD_DIM, 1), 0)
                e_sc[fe : fe + HEAD_DIM, pc] = jnp.where(
                    row == 0, 1.0, jnp.where(row == 1, -hi, jnp.where(row == 2, -mid, jnp.where(row == 3, -lo, 0.0)))
                )
        if u < len(units):
            m_prev = jnp.max(m8, axis=0, keepdims=True)
            if not first:
                m_prev = jnp.maximum(m_prev, ml_in[h : h + 1, cols])
    if not first:
        o_ref[...] = acc_sc[...].T.astype(bf16)
        e_ref[...] = e_sc[...].T.astype(bf16)


def attn_fwd(meta, q, k, v, pairs, state=None, qb=1024, kc=256):
    rows = q[0].shape[0]
    keys = k[0].shape[0]
    width = pairs * PAIR
    first = state is None

    def col(off):
        return lambda i, m: (0, off + i)

    def down(i, m):
        return (i, 0)

    in_specs = [
        pl.BlockSpec((rows, PAIR), col(q[1])),
        pl.BlockSpec((keys, PAIR), col(k[1])),
        pl.BlockSpec((keys, PAIR), col(v[1])),
    ]
    scratch = [pltpu.VMEM((2, keys, qb), f32), pltpu.VMEM((2, keys, qb), bf16)]
    args = (q[0], k[0], v[0])
    if first:
        out_shape = (jax.ShapeDtypeStruct((width, rows), f32), jax.ShapeDtypeStruct((8 * pairs, rows), f32))
        out_specs = (pl.BlockSpec((PAIR, rows), down), pl.BlockSpec((8, rows), down))
    else:
        in_specs += [pl.BlockSpec((PAIR, rows), down), pl.BlockSpec((8, rows), down)]
        out_shape = (jax.ShapeDtypeStruct((rows, width), bf16), jax.ShapeDtypeStruct((rows, width), bf16))
        out_specs = (pl.BlockSpec((rows, PAIR), col(0)), pl.BlockSpec((rows, PAIR), col(0)))
        scratch = [pltpu.VMEM((PAIR, rows), f32), pltpu.VMEM((PAIR, rows), f32)] + scratch
        args = args + tuple(state)
    return pl.pallas_call(
        functools.partial(attn_fwd_kernel, first, qb, kc),
        grid_spec=pltpu.PrefetchScalarGridSpec(
            num_scalar_prefetch=1, grid=(pairs,), in_specs=in_specs, out_specs=out_specs, scratch_shapes=scratch
        ),
        out_shape=out_shape,
        compiler_params=pltpu.CompilerParams(vmem_limit_bytes=VMEM_LIMIT),
        cost_estimate=cost(16 * rows * keys * width, 8 * rows * width),
        name="attn_fwd_first" if first else "attn_fwd_second",
    )(meta, *args)


def attn_bwd_kernel(first, qb, kc, meta, q_ref, e_ref, o_ref, do_ref, k_ref, v_ref, *refs):
    if first:
        dq_ref, dk_ref, dv_ref, dk_sc, dv_sc, s_sc, dp_sc, p_sc, ds_sc = refs
    else:
        dq_in, dq_ref, dk_ref, dv_ref, dk_sc, dv_sc, s_sc, dp_sc, p_sc, ds_sc = refs
    rows = q_ref.shape[0]
    keys = k_ref.shape[0]
    lane, inside, free = pair_masks()
    bias = key_bias(meta, keys)
    k32 = k_ref[...].astype(f32)
    v32 = v_ref[...].astype(f32)
    kx = [jnp.where(inside[h], k32, jnp.where(lane == free[h], bias, 1.0)).astype(bf16) for h in range(2)]
    vx = [jnp.where(inside[h], v32, 1.0).astype(bf16) for h in range(2)]
    units = [(b, h) for b in range(rows // qb) for h in range(2)]
    chunks = [slice(c * kc, (c + 1) * kc) for c in range(keys // kc)]
    prep = None
    dq0 = None
    for u in range(len(units) + 1):
        before = prep
        slot, prev = u % 2, (u - 1) % 2
        if u < len(units):
            b, h = units[u]
            rs = slice(b * qb, (b + 1) * qb)
            fe = free[h]
            if h == 0:
                q32 = q_ref[rs].astype(f32) * SCALE
                do32 = do_ref[rs].astype(f32)
                e32 = e_ref[rs].astype(f32)
                prod = do32 * o_ref[rs].astype(f32)
            hi, mid, lo = split3(jnp.sum(jnp.where(inside[h], prod, 0.0), axis=1, keepdims=True))
            dext = jnp.where(lane == fe, -hi, jnp.where(lane == fe + 1, -mid, jnp.where(lane == fe + 2, -lo, 0.0)))
            qx = jnp.where(inside[h], q32, e32).astype(bf16)
            dox = jnp.where(inside[h], do32, dext).astype(bf16)
            prep = (qx, dox)
        for ch in chunks:
            if u < len(units):
                s_sc[slot, :, ch] = mm(qx, kx[h][ch], NT)
                dp_sc[slot, :, ch] = mm(dox, vx[h][ch], NT)
            if u > 0:
                p = jnp.exp(s_sc[prev, :, ch])
                p_sc[prev, :, ch] = p.astype(bf16)
                ds_sc[prev, :, ch] = (p * dp_sc[prev, :, ch]).astype(bf16)
        if u > 0:
            bp, hp = units[u - 1]
            rp = slice(bp * qb, (bp + 1) * qb)
            qxp, doxp = before
            dvt = mm(doxp, p_sc[prev], TN)
            dkt = mm(qxp, ds_sc[prev], TN)
            dqh = mm(ds_sc[prev], kx[hp], NN)
            own = own_part(hp)
            if bp == 0:
                dv_sc[own] = dvt[own]
                dk_sc[own] = dkt[own]
            else:
                dv_sc[own] += dvt[own]
                dk_sc[own] += dkt[own]
            if hp == 0:
                dq0 = dqh
            else:
                dq = jnp.where(lane < HEAD_DIM, dq0, dqh) * SCALE
                if first:
                    dq_ref[rp] = dq
                else:
                    dq_ref[rp] = (dq + dq_in[rp]).astype(bf16)
    dk_ref[...] = dk_sc[...].T.astype(bf16)
    dv_ref[...] = dv_sc[...].T.astype(bf16)


def attn_bwd(meta, q, e, o, do, k, v, pairs, dq_prev=None, qb=256, kc=256):
    rows = q[0].shape[0]
    keys = k[0].shape[0]
    width = pairs * PAIR
    first = dq_prev is None

    def col(off):
        return lambda i, m: (0, off + i)

    in_specs = [pl.BlockSpec((rows, PAIR), col(off)) for _, off in (q, e, o, do)]
    in_specs += [pl.BlockSpec((keys, PAIR), col(off)) for _, off in (k, v)]
    args = (q[0], e[0], o[0], do[0], k[0], v[0])
    rspec = pl.BlockSpec((rows, PAIR), col(0))
    kspec = pl.BlockSpec((keys, PAIR), col(0))
    if not first:
        in_specs.append(rspec)
        args = args + (dq_prev,)
    return pl.pallas_call(
        functools.partial(attn_bwd_kernel, first, qb, kc),
        grid_spec=pltpu.PrefetchScalarGridSpec(
            num_scalar_prefetch=1,
            grid=(pairs,),
            in_specs=in_specs,
            out_specs=(rspec, kspec, kspec),
            scratch_shapes=[pltpu.VMEM((PAIR, keys), f32)] * 2
            + [pltpu.VMEM((2, qb, keys), f32)] * 2
            + [pltpu.VMEM((2, qb, keys), bf16)] * 2,
        ),
        out_shape=(
            jax.ShapeDtypeStruct((rows, width), f32 if first else bf16),
            jax.ShapeDtypeStruct((keys, width), bf16),
            jax.ShapeDtypeStruct((keys, width), bf16),
        ),
        compiler_params=pltpu.CompilerParams(vmem_limit_bytes=VMEM_LIMIT),
        cost_estimate=cost(40 * rows * keys * width, 16 * rows * width),
        name="attn_bwd_first" if first else "attn_bwd_second",
    )(meta, *args)


FF_BLOCK = 768
EARLY = (0, 1)
CHUNK = 256


def row_chunks(rows):
    return [slice(c, c + CHUNK) for c in range(0, rows, CHUNK)]


EMB, B_OUT, GAIN_2, SHIFT_2, B_DOWN, GAIN_1, SHIFT_1 = (slice(i, i + 1) for i in range(7))


def normalise(values):
    centre = values - jnp.mean(values, axis=-1, keepdims=True)
    spread = jnp.mean(centre * centre, axis=-1, keepdims=True)
    rstd = lax.rsqrt(spread + 1e-05)
    return centre * rstd, rstd


def gelu_pair(u):
    cdf = 0.5 * (1.0 + lax.erf(u * 0.7071067811865476))
    density = 0.3989422804014327 * jnp.exp(-0.5 * u * u)
    return u * cdf, cdf + u * density


def pick(step, n_own, own, other):
    return jnp.where(step < n_own, own, other)


def mid_fwd_kernel(
    n_own, scal, tok_ref, vec_ref, o0_ref, o1_ref, wo_ref, wo2_ref, bup_ref, up_ref, up2_ref,
    down_ref, down2_ref, wg_ref, cnt_ref, cot_ref,
    h1_ref, nt_ref, g_ref, gp_ref, out_ref, dm_ref, dout_ref, sums_ref, acc,
):
    step = pl.program_id(0)
    last = pl.num_programs(0) - 1
    rows, width = tok_ref.shape
    chunks = row_chunks(rows)

    @pl.when(step == 0)
    def _():
        wo2 = wo2_ref[...].reshape(wo_ref.shape)
        for c in chunks:
            h1 = tok_ref[c].astype(f32) + vec_ref[EMB]
            h1 = h1 + (mm(o0_ref[c], wo_ref[...]) + mm(o1_ref[c], wo2) + vec_ref[B_OUT])
            h1_ref[c] = h1
            xhat, _ = normalise(h1)
            nt_ref[c] = (xhat * vec_ref[GAIN_2] + vec_ref[SHIFT_2]).astype(bf16)
            acc[c] = h1 + vec_ref[B_DOWN]

    up = pick(step, n_own, up_ref[...], up2_ref[...].reshape(up_ref.shape))
    down = pick(step, n_own, down_ref[...], down2_ref[...].reshape(down_ref.shape))
    u = mm(nt_ref[chunks[0]], up)
    for i, c in enumerate(chunks):
        ahead = mm(nt_ref[chunks[i + 1]], up) if i + 1 < len(chunks) else None
        g, gp = gelu_pair(u + bup_ref[...])
        g = g.astype(bf16)
        g_ref[c] = g
        gp_ref[c] = gp.astype(bf16)
        acc[c] += mm(g, down)
        u = ahead

    @pl.when(step == last)
    def _():
        dbd = jnp.zeros((1, width), f32)
        dwg = [jnp.zeros((1, width), f32) for _ in range(3)]
        ent_sum = jnp.zeros((1, 1), f32)
        for c in chunks:
            out = acc[c]
            out_ref[c] = out.astype(bf16)
            z = [jnp.sum(out * wg_ref[e : e + 1], axis=-1, keepdims=True) for e in range(3)]
            top = jnp.maximum(jnp.maximum(z[0], z[1]), z[2])
            log_sum = jnp.log(sum(jnp.exp(v - top) for v in z)) + top
            logp = [v - log_sum for v in z]
            prob = [jnp.exp(v) for v in logp]
            entropy = -sum(p * q for p, q in zip(prob, logp))
            mean = sum(p * v for p, v in zip(prob, z))
            counted = cnt_ref[c]
            ent_sum = ent_sum + jnp.sum(counted * entropy, axis=0, keepdims=True)
            dz = [scal[0] * counted * (-p * (v - mean)) for p, v in zip(prob, z)]
            d_out = cot_ref[c].astype(f32) + sum(d * wg_ref[e : e + 1] for e, d in enumerate(dz))
            dout_ref[c] = d_out
            dm = d_out.astype(bf16)
            dm_ref[c] = dm
            dbd = dbd + jnp.sum(dm.astype(f32), axis=0, keepdims=True)
            dwg = [w + jnp.sum(out * d, axis=0, keepdims=True) for w, d in zip(dwg, dz)]
        sums_ref[...] = jnp.zeros_like(sums_ref)
        for e in range(3):
            sums_ref[3 + e : 4 + e] = dwg[e]
        sums_ref[6:7] = dbd
        sums_ref[7:8] = jnp.broadcast_to(ent_sum, (1, width))


def fixed(shape):
    zeros = (0,) * len(shape)
    return pl.BlockSpec(shape, lambda *_: zeros)


def weight_specs(gathered, width, ff):
    n_own = ff // FF_BLOCK
    parts, _, _ = gathered.shape
    k_up, k_down = width // parts, ff // parts
    per_step = FF_BLOCK // k_down
    cols = width // FF_BLOCK

    def other(j):
        return jnp.maximum(j - n_own, 0)

    return n_own, [
        pl.BlockSpec((width, FF_BLOCK), lambda j, *_: (0, jnp.minimum(j, n_own - 1))),
        pl.BlockSpec((parts, k_up, FF_BLOCK), lambda j, *_: (0, other(j) // cols, other(j) % cols)),
        pl.BlockSpec((FF_BLOCK, width), lambda j, *_: (jnp.minimum(j, n_own - 1), 0)),
        pl.BlockSpec((per_step, k_down, width), lambda j, *_: (other(j), 2 * k_up // k_down, 0)),
    ]


def out_spec(gathered, width, ff, hw):
    parts = gathered.shape[0]
    k_out = hw // parts
    return pl.BlockSpec((parts, k_out, width), lambda *_: (0, (2 * width + ff) // parts // k_out, 0))


def mid_fwd(scal, tokens, vecs, o0, o1, w_out, gathered, b_up, w_up, w_down, wg, counted, cot):
    rows, width = tokens.shape
    ff = w_down.shape[0]
    n_own, (up_s, up2_s, down_s, down2_s) = weight_specs(gathered, width, ff)
    hw = w_out.shape[0]
    vec = fixed((8, width))
    full = fixed((rows, width))
    blk = pl.BlockSpec((rows, FF_BLOCK), lambda j, *_: (0, j))
    return pl.pallas_call(
        functools.partial(mid_fwd_kernel, n_own),
        grid_spec=pltpu.PrefetchScalarGridSpec(
            num_scalar_prefetch=1,
            grid=(2 * n_own,),
            in_specs=[
                full, vec, fixed((rows, hw)), fixed((rows, hw)), fixed((hw, width)), out_spec(gathered, width, ff, hw),
                pl.BlockSpec((1, FF_BLOCK), lambda j, *_: (0, j)), up_s, up2_s, down_s, down2_s,
                vec, fixed((rows, 1)), full,
            ],
            out_specs=[full, full, blk, blk, full, full, full, fixed((8, width))],
            scratch_shapes=[pltpu.VMEM((rows, width), f32)],
        ),
        out_shape=[
            jax.ShapeDtypeStruct((rows, width), f32),
            jax.ShapeDtypeStruct((rows, width), bf16),
            jax.ShapeDtypeStruct((rows, 2 * ff), bf16),
            jax.ShapeDtypeStruct((rows, 2 * ff), bf16),
            jax.ShapeDtypeStruct((rows, width), bf16),
            jax.ShapeDtypeStruct((rows, width), bf16),
            jax.ShapeDtypeStruct((rows, width), f32),
            jax.ShapeDtypeStruct((8, width), f32),
        ],
        compiler_params=pltpu.CompilerParams(vmem_limit_bytes=VMEM_LIMIT),
        cost_estimate=cost(12 * rows * width * ff, 40 * rows * width),
        name="mid_fwd",
    )(
        scal, tokens, vecs, o0, o1, w_out, gathered, b_up, w_up, gathered, w_down, gathered, wg, counted, cot,
    )


def mid_bwd_kernel(
    n_own, dm_ref, nt_ref, h1_ref, dout_ref, vec_ref, g_ref, gp_ref, up_ref, up2_ref, down_ref, down2_ref,
    grads_ref, dh_ref, da_ref, sums_ref, acc, du_sc,
):
    step = pl.program_id(0)
    last = pl.num_programs(0) - 1
    rows, width = dm_ref.shape
    chunks = row_chunks(rows)
    up = pick(step, n_own, up_ref[...], up2_ref[...].reshape(up_ref.shape))
    down = pick(step, n_own, down_ref[...], down2_ref[...].reshape(down_ref.shape))

    @pl.when(step == 0)
    def _():
        acc[...] = jnp.zeros_like(acc)
        sums_ref[...] = jnp.zeros_like(sums_ref)

    bias = jnp.zeros((1, FF_BLOCK), f32)
    for c in chunks:
        du = (mm(dm_ref[c], down, NT) * gp_ref[c].astype(f32)).astype(bf16)
        du_sc[c] = du
        bias = bias + jnp.sum(du.astype(f32), axis=0, keepdims=True)
        acc[c] += mm(du, up, NT)
    sums_ref[pl.ds(8 + 4 * (step // n_own) + step % n_own, 1)] = bias
    sums_ref[pl.ds(20 - 4 * (step // n_own) + step % n_own, 1)] = bias
    grads_ref[:, :FF_BLOCK] = mm(dm_ref[...], g_ref[...], TN).astype(bf16)
    grads_ref[:, FF_BLOCK:] = mm(nt_ref[...], du_sc[...], TN).astype(bf16)

    @pl.when(step == last)
    def _():
        d_gain = jnp.zeros((1, width), f32)
        d_shift = jnp.zeros((1, width), f32)
        d_bias = jnp.zeros((1, width), f32)
        for c in chunks:
            db = acc[c]
            xhat, rstd = normalise(h1_ref[c])
            d_gain = d_gain + jnp.sum(db * xhat, axis=0, keepdims=True)
            d_shift = d_shift + jnp.sum(db, axis=0, keepdims=True)
            dx = db * vec_ref[GAIN_2]
            low = jnp.mean(dx, axis=-1, keepdims=True)
            slope = jnp.mean(dx * xhat, axis=-1, keepdims=True)
            dh = dout_ref[c] + rstd * (dx - low - xhat * slope)
            dh_ref[c] = dh
            da = dh.astype(bf16)
            da_ref[c] = da
            d_bias = d_bias + jnp.sum(da.astype(f32), axis=0, keepdims=True)
        sums_ref[0:1] = d_gain
        sums_ref[1:2] = d_shift
        sums_ref[2:3] = d_bias


def mid_bwd(dm, normed, h1, d_out, vecs, g, gp, w_up, w_down, gathered, grad_cols):
    rows, width = dm.shape
    ff = w_down.shape[0]
    n_own, (up_s, up2_s, down_s, down2_s) = weight_specs(gathered, width, ff)
    full = fixed((rows, width))
    blk = pl.BlockSpec((rows, FF_BLOCK), lambda j, *_: (0, j))
    return pl.pallas_call(
        functools.partial(mid_bwd_kernel, n_own),
        grid=(2 * n_own,),
        in_specs=[full, full, full, full, fixed((8, width)), blk, blk, up_s, up2_s, down_s, down2_s],
        out_specs=[
            pl.BlockSpec((width, 2 * FF_BLOCK), lambda j: (0, j)),
            full,
            full,
            fixed((24, width)),
        ],
        scratch_shapes=[pltpu.VMEM((rows, width), f32), pltpu.VMEM((rows, FF_BLOCK), bf16)],
        out_shape=[
            jax.ShapeDtypeStruct((width, grad_cols), bf16),
            jax.ShapeDtypeStruct((rows, width), f32),
            jax.ShapeDtypeStruct((rows, width), bf16),
            jax.ShapeDtypeStruct((24, width), f32),
        ],
        compiler_params=pltpu.CompilerParams(vmem_limit_bytes=VMEM_LIMIT),
        cost_estimate=cost(24 * rows * width * ff, 40 * rows * width),
        name="mid_bwd",
    )(dm, normed, h1, d_out, vecs, g, gp, w_up, gathered, w_down, gathered)


def out_bwd_kernel(da_ref, o0_ref, o1_ref, wo_ref, wo2_ref, _, do_ref, do2_ref, grads_ref):
    hw = wo_ref.shape[0]
    do_ref[...] = mm(da_ref[...], wo_ref[...], NT).astype(bf16)
    do2_ref[...] = mm(da_ref[...], wo2_ref[...].reshape(wo_ref.shape), NT).astype(bf16)
    grads_ref[:, :hw] = mm(da_ref[...], o0_ref[...], TN).astype(bf16)
    grads_ref[:, hw:] = mm(da_ref[...], o1_ref[...], TN).astype(bf16)


def out_bwd(d_attn, o0, o1, w_out, gathered, ff, grads):
    rows, width = d_attn.shape
    hw = w_out.shape[0]
    half = fixed((rows, hw))
    return pl.pallas_call(
        out_bwd_kernel,
        grid=(1,),
        in_specs=[
            fixed((rows, width)), half, half, fixed((hw, width)), out_spec(gathered, width, ff, hw),
            pl.BlockSpec(memory_space=pl.ANY),
        ],
        out_specs=[half, half, pl.BlockSpec((width, 2 * hw), lambda j: (0, grads.shape[1] // (2 * hw) - 1))],
        out_shape=[
            jax.ShapeDtypeStruct((rows, hw), bf16),
            jax.ShapeDtypeStruct((rows, hw), bf16),
            jax.ShapeDtypeStruct(grads.shape, bf16),
        ],
        input_output_aliases={5: 2},
        compiler_params=pltpu.CompilerParams(vmem_limit_bytes=VMEM_LIMIT),
        cost_estimate=cost(8 * rows * width * hw, 12 * rows * width),
        name="out_bwd",
    )(d_attn, o0, o1, w_out, gathered, grads)


def qkv_grads_kernel(n_ref, no_ref, dq_ref, dk_ref, dv_ref, dko_ref, dvo_ref, grads_ref, sums_ref):
    hw = dq_ref.shape[1]
    grads_ref[:, :hw] = mm(n_ref[...], dq_ref[...], TN).astype(bf16)
    kv = jnp.concatenate([dk_ref[...], dv_ref[...]], axis=1)
    kvo = jnp.concatenate([dko_ref[...], dvo_ref[...]], axis=1)
    grads_ref[:, hw:] = (mm(n_ref[...], kv, TN) + mm(no_ref[...], kvo, TN)).astype(bf16)
    bq = jnp.sum(dq_ref[...].astype(f32), axis=0, keepdims=True)
    bv = jnp.sum(dv_ref[...].astype(f32), axis=0, keepdims=True) + jnp.sum(dvo_ref[...].astype(f32), axis=0, keepdims=True)
    sums_ref[:, :hw] = jnp.broadcast_to(bq, (8, hw))
    sums_ref[:, hw:] = jnp.broadcast_to(bv, (8, hw))


def qkv_grads(normed, normed_oth, dq, dk, dv, dk_oth, dv_oth):
    rows, width = normed.shape
    hw = dq.shape[1]
    full, half = fixed((rows, width)), fixed((rows, hw))
    return pl.pallas_call(
        qkv_grads_kernel,
        grid=(1,),
        in_specs=[full, full] + [half] * 5,
        out_specs=[fixed((width, 3 * hw)), fixed((8, 2 * hw))],
        out_shape=[jax.ShapeDtypeStruct((width, 3 * hw), bf16), jax.ShapeDtypeStruct((8, 2 * hw), f32)],
        compiler_params=pltpu.CompilerParams(vmem_limit_bytes=VMEM_LIMIT),
        cost_estimate=cost(10 * rows * width * hw, 10 * rows * width),
        name="qkv_grads",
    )(normed, normed_oth, dq, dk, dv, dk_oth, dv_oth)


def ln1_bwd_kernel(n_parts, *refs):
    parts, (w0_ref, w1_ref, got0_ref, got1_ref, dh_ref, tok_ref, vec_ref, dtok_ref, sums_ref) = refs[:n_parts], refs[n_parts:]
    upper = pl.program_id(0) < pl.num_programs(0) // 2
    da = jnp.where(upper, got0_ref[...], got1_ref[...]).astype(f32)
    for i, w_ref in enumerate((w0_ref, w1_ref)):
        joined = jnp.concatenate([part[...] for part in parts[3 * i : 3 * i + 3]], axis=1)
        da = da + mm(joined, w_ref[...], NT)
    xhat, rstd = normalise(tok_ref[...].astype(f32) + vec_ref[EMB])
    dx = da * vec_ref[GAIN_1]
    low = jnp.mean(dx, axis=-1, keepdims=True)
    slope = jnp.mean(dx * xhat, axis=-1, keepdims=True)
    d_tokens = dh_ref[...] + rstd * (dx - low - xhat * slope)
    dtok_ref[...] = d_tokens
    new = [jnp.sum(v, axis=0, keepdims=True) for v in (da * xhat, da, d_tokens)]

    @pl.when(pl.program_id(0) == 0)
    def _():
        sums_ref[...] = jnp.zeros_like(sums_ref)

    for i, v in enumerate(new):
        sums_ref[i : i + 1] += v


def ln1_bwd(d_qkv, w0, w1, da_got, d_hidden, tokens, vecs):
    rows, width = tokens.shape
    hw = d_qkv[0].shape[1]
    step = CHUNK
    n_half = rows // step // 2
    blk = pl.BlockSpec((step, width), lambda i: (i, 0))
    half = pl.BlockSpec((step, hw), lambda i: (i, 0))
    return pl.pallas_call(
        functools.partial(ln1_bwd_kernel, len(d_qkv)),
        grid=(rows // step,),
        in_specs=[half] * len(d_qkv) + [fixed((width, 3 * hw))] * 2
        + [
            pl.BlockSpec((step, width), lambda i: (jnp.minimum(i, n_half - 1), 0)),
            pl.BlockSpec((step, width), lambda i: (jnp.maximum(i - n_half, 0), 0)),
            blk,
            blk,
            fixed((8, width)),
        ],
        out_specs=[blk, fixed((8, width))],
        out_shape=[jax.ShapeDtypeStruct((rows, width), f32), jax.ShapeDtypeStruct((8, width), f32)],
        compiler_params=pltpu.CompilerParams(vmem_limit_bytes=VMEM_LIMIT),
        cost_estimate=cost(12 * rows * width * hw, 20 * rows * width),
        name="ln1_bwd",
    )(*d_qkv, w0, w1, *da_got, d_hidden, tokens, vecs)


def oth_bwd_kernel(k0_ref, v0_ref, k1_ref, v1_ref, w0_ref, w1_ref, da_ref):
    hw = k0_ref.shape[1]
    da = mm(jnp.concatenate([k0_ref[...], v0_ref[...]], axis=1), w0_ref[:, hw:], NT)
    da_ref[...] = (da + mm(jnp.concatenate([k1_ref[...], v1_ref[...]], axis=1), w1_ref[:, hw:], NT)).astype(bf16)


def oth_bwd(d_kv, w0, w1):
    rows, hw = d_kv[0].shape
    width = w0.shape[0]
    step = 2 * CHUNK
    half = pl.BlockSpec((step, hw), lambda i: (i, 0))
    return pl.pallas_call(
        oth_bwd_kernel,
        grid=(rows // step,),
        in_specs=[half] * 4 + [fixed(w0.shape)] * 2,
        out_specs=pl.BlockSpec((step, width), lambda i: (i, 0)),
        out_shape=jax.ShapeDtypeStruct((rows, width), bf16),
        compiler_params=pltpu.CompilerParams(vmem_limit_bytes=VMEM_LIMIT),
        cost_estimate=cost(8 * rows * width * hw, 4 * rows * width),
        name="oth_bwd",
    )(*d_kv, w0, w1)


def front_kernel(starts, tok_ref, vec_ref, *refs):
    n = len(starts)
    xhat, _ = normalise(tok_ref[...].astype(f32) + vec_ref[EMB])
    normed = (xhat * vec_ref[GAIN_1] + vec_ref[SHIFT_1]).astype(bf16)
    refs[2 * n][...] = normed
    for i, start in enumerate(starts):
        y = mm(normed, refs[2 * i][:, start:]) + refs[2 * i + 1][:, start:]
        refs[2 * n + 1 + i][...] = y.astype(bf16)


def front(tokens, vecs, weights):
    rows, width = tokens.shape
    step = CHUNK
    in_specs = [pl.BlockSpec((step, width), lambda i: (i, 0)), fixed((8, width))]
    args = [tokens, vecs]
    outs = [width]
    for w, b, start in weights:
        in_specs += [fixed(w.shape), fixed(b.shape)]
        args += [w, b]
        outs.append(w.shape[1] - start)
    return pl.pallas_call(
        functools.partial(front_kernel, tuple(start for _, _, start in weights)),
        grid=(rows // step,),
        in_specs=in_specs,
        out_specs=[pl.BlockSpec((step, n), lambda i: (i, 0)) for n in outs],
        out_shape=[jax.ShapeDtypeStruct((rows, n), bf16) for n in outs],
        compiler_params=pltpu.CompilerParams(vmem_limit_bytes=VMEM_LIMIT),
        cost_estimate=cost(2 * rows * width * sum(outs[1:]), 8 * rows * width),
        name="front",
    )(*args)


def pack_kernel(row, up_ref, down_ref, out_ref, rest_ref, share_ref):
    width = share_ref.shape[1]
    at = 0
    for part in (up_ref[:, :width], up_ref[:, width:], down_ref[...], out_ref[...], rest_ref[...]):
        share_ref[at : at + part.shape[0]] = part
        at += part.shape[0]


def pack_share(row, n_rows, w_up, w_down, w_out, rest):
    width = w_out.shape[1]
    sizes = [w.shape[0] // n_rows for w in (w_up, w_down, w_out)]
    total = 2 * sizes[0] + sizes[1] + sizes[2] + rest.shape[0]
    if sizes[0] % 16:
        up, down, out = (lax.dynamic_slice_in_dim(w, row * k, k, 0) for w, k in zip((w_up, w_down, w_out), sizes))
        return jnp.concatenate([up[:, :width], up[:, width:], down, out, rest])
    return pl.pallas_call(
        pack_kernel,
        grid_spec=pltpu.PrefetchScalarGridSpec(
            num_scalar_prefetch=1,
            grid=(1,),
            in_specs=[pl.BlockSpec((k, w.shape[1]), lambda i, r: (r[0], 0)) for w, k in zip((w_up, w_down, w_out), sizes)]
            + [fixed(rest.shape)],
            out_specs=fixed((total, width)),
        ),
        out_shape=jax.ShapeDtypeStruct((total, width), bf16),
        name="pack_share",
    )(row.reshape(1), w_up, w_down, w_out, rest)


class Net:
    def __init__(self, n_rows):
        self.n_rows = n_rows
        self.bits = n_rows.bit_length() - 1
        self.row = lax.axis_index("rows")

    def cross(self, x):
        return lax.ppermute(x, "heads", [(0, 1), (1, 0)])

    def flip(self, x, bit):
        return lax.ppermute(x, "rows", [(i, i ^ (1 << bit)) for i in range(self.n_rows)])

    def bit(self, b):
        return (self.row >> b) & 1

    def fetch(self, own):
        part = own.shape[0] // 2
        return self.cross(lax.dynamic_slice_in_dim(own, self.bit(0) * part, part, 0))

    def join(self, got):
        passed = self.flip(got, 0)
        low = self.bit(0) == 0
        return jnp.concatenate([jnp.where(low, got, passed), jnp.where(low, passed, got)], axis=0)

    def halve(self, part, left, step):
        low = 1 << left.index(step)
        blocks, piece, cols = part.shape
        view = part.reshape(blocks // (2 * low), 2, low, piece, cols)
        at = self.bit(step)
        keep = lax.dynamic_index_in_dim(view, at, 1, keepdims=False)
        got = self.flip(lax.dynamic_index_in_dim(view, 1 - at, 1, keepdims=False).astype(bf16), step)
        return (keep.astype(f32) + got.astype(f32)).reshape(blocks // 2, piece, cols), [x for x in left if x != step]


def per_device(
    n_rows,
    tokens,
    crop_lengths,
    lead_index,
    valid_mask,
    lead_table,
    ln1_gain,
    ln1_shift,
    w_query,
    w_key,
    w_value,
    b_query,
    b_value,
    w_out,
    b_out,
    ln2_gain,
    ln2_shift,
    w_up,
    b_up,
    w_down,
    b_down,
    w_gater,
    cotangent,
):
    net = Net(n_rows)
    own_rows, width = tokens.shape
    half = lax.axis_index("heads")
    length = crop_lengths[0]
    hw = w_query.shape[1]
    pairs = hw // PAIR
    own_start = half * own_rows
    meta_own = jnp.stack([own_start, length])
    meta_oth = jnp.stack([own_rows - own_start, length])

    positions = own_start + jnp.arange(own_rows, dtype=jnp.int32)
    counted = ((positions < length) & (valid_mask == 1)).astype(f32)
    count = jnp.sum(counted)

    qkv_w = jnp.concatenate([w_query, w_key, w_value], axis=1)
    bias_own = jnp.concatenate([b_query, b_value, b_up]).reshape(1, -1)
    k_up, k_down, k_out = width // n_rows, w_down.shape[0] // n_rows, w_out.shape[0] // n_rows
    n_share = 2 * k_up + k_down + k_out
    pad = -n_share % 16 + 16
    n_bias = bias_own.size // width
    line = lax.broadcasted_iota(jnp.int32, (pad, width), 0)
    lane = lax.broadcasted_iota(jnp.int32, (pad, width), 1)
    high = jnp.floor(count / 32)
    tally = jnp.where(lane == 0, high, jnp.where(lane == 1, count - 32 * high, 0.0))
    tally = jnp.where(lane == 2, lead_index[0].astype(f32), tally).astype(bf16)
    rest = tally
    for i in range(n_bias):
        rest = jnp.where(line == 1 + i, bias_own[:, i * width : (i + 1) * width], rest)
    got = net.cross(pack_share(net.row, n_rows, w_up, w_down, w_out, rest))
    bias_oth = got[n_share + 1 : n_share + 1 + n_bias].reshape(1, -1)
    tokens_in, got = lax.optimization_barrier((tokens, got))
    share = jnp.concatenate([got, tally], axis=0)
    tokens_oth = net.cross(tokens)
    at = lax.broadcasted_iota(jnp.int32, (8, 1), 0)
    picked = jnp.arange(lead_table.shape[0], dtype=jnp.int32) == lead_index[0]
    embedding = jnp.sum(jnp.where(picked[:, None], lead_table, 0.0), axis=0)
    vecs = jnp.zeros((8, width), f32)
    for i, v in enumerate((embedding, b_out, ln2_gain, ln2_shift, b_down, ln1_gain, ln1_shift)):
        vecs = jnp.where(at == i, v, vecs)

    def qkv_bias(b):
        b = b.astype(f32)
        return jnp.concatenate([b[:, :hw], jnp.zeros((1, hw), f32), b[:, hw : 2 * hw]], axis=1)

    qkv_b = qkv_bias(bias_own)
    normed, qkv_own = front(tokens_in, vecs, [(qkv_w, qkv_b, 0)])
    gathered = lax.all_gather(share, "rows", axis=0, tiled=False)
    tally = gathered[:, n_share:, :2].astype(f32)
    gathered_lead = gathered[:, n_share + pad, 2]
    count_total = jnp.sum(tally[:, 0] * jnp.array([32.0, 1.0])) + jnp.sum(tally[:, pad] * jnp.array([32.0, 1.0]))
    if k_up % 16 or k_down % 16:
        sizes = (k_up, k_up, k_down, k_out)
        starts = (0, k_up, 2 * k_up, 2 * k_up + k_down)
        gathered = jnp.concatenate(
            [gathered[:, a : a + k].reshape(16, k * n_rows // 16, width) for a, k in zip(starts, sizes)], axis=1
        )

    qkv_b2 = qkv_bias(bias_oth)
    up_b, up_b2 = bias_own[:, 2 * hw :].astype(f32), bias_oth[:, 2 * hw :].astype(f32)

    state = attn_fwd(meta_own, (qkv_own, 0), (qkv_own, pairs), (qkv_own, 2 * pairs), pairs)
    tokens_oth, state, qkv_in = lax.optimization_barrier((tokens_oth, state, qkv_w))
    got_w = net.fetch(qkv_in)
    normed_oth, kv_own = front(tokens_oth, vecs, [(qkv_w, qkv_b, hw)])
    attn_own, ext_own = attn_fwd(meta_oth, (qkv_own, 0), (kv_own, 0), (kv_own, pairs), pairs, state)
    got_w, attn_own = lax.optimization_barrier((got_w, attn_own))
    qkv_w2 = net.join(got_w)
    qkv_two = (mm(normed, qkv_w2) + qkv_b2).astype(bf16)
    kv_two = (mm(normed_oth, qkv_w2[:, hw:]) + qkv_b2[:, hw:]).astype(bf16)
    state = attn_fwd(meta_own, (qkv_two, 0), (qkv_two, pairs), (qkv_two, 2 * pairs), pairs)
    attn_two, ext_two = attn_fwd(meta_oth, (qkv_two, 0), (kv_two, 0), (kv_two, pairs), pairs, state)
    qkv, kv_oth, attn, ext = (qkv_own, qkv_two), (kv_own, kv_two), (attn_own, attn_two), (ext_own, ext_two)

    ff = w_down.shape[0]
    h1, normed_two, act, slope, block_out, d_branch, d_output, sums_f = mid_fwd(
        (entropy_weight / count_total).reshape(1),
        tokens,
        vecs,
        attn[0],
        attn[1],
        w_out,
        gathered,
        jnp.concatenate([up_b, up_b2], axis=1),
        w_up,
        w_down,
        jnp.concatenate([w_gater.T, jnp.zeros((5, width), f32)]),
        counted.reshape(-1, 1),
        cotangent,
    )
    grad_cols = 4 * ff + 2 * hw
    grads, d_hidden, d_attn, sums_b = mid_bwd(
        d_branch, normed_two, h1, d_output, vecs, act, slope, w_up, w_down, gathered, grad_cols
    )
    do_own, do_oth, grads = out_bwd(d_attn, attn[0], attn[1], w_out, gathered, ff, grads)
    d_heads = (do_own, do_oth)
    grads = lax.psum_scatter(grads, "rows", scatter_dimension=0, tiled=True)

    dq, dk_oth, dv_oth = [], [], []
    for i in range(2):
        a, b, c = attn_bwd(
            meta_oth, (qkv[i], 0), (ext[i], 0), (attn[i], 0), (d_heads[i], 0), (kv_oth[i], 0), (kv_oth[i], pairs), pairs
        )
        dq.append(a)
        dk_oth.append(b)
        dv_oth.append(c)
    da_oth = oth_bwd((dk_oth[0], dv_oth[0], dk_oth[1], dv_oth[1]), qkv_w, qkv_w2)
    dq, da_oth = lax.optimization_barrier((dq, da_oth))
    mid = own_rows // 2
    da_top = net.cross(da_oth[:mid])
    da_rest, da_top = lax.optimization_barrier((da_oth[mid:], da_top))
    da_rest = net.cross(da_rest)
    d_qkv, g_qkv, bias_rows = [None] * 2, [None] * 2, [None] * 2
    for i in (1, 0):
        d_qkv[i] = attn_bwd(
            meta_own,
            (qkv[i], 0),
            (ext[i], 0),
            (attn[i], 0),
            (d_heads[i], 0),
            (qkv[i], pairs),
            (qkv[i], 2 * pairs),
            pairs,
            dq[i],
        )
        if i == 0:
            d_qkv[0], oth = lax.optimization_barrier((d_qkv[0], oth))
        g_qkv[i], bias_rows[i] = qkv_grads(normed, normed_oth, *d_qkv[i], dk_oth[i], dv_oth[i])
        if i == 1:
            dq[0], g_qkv[1], da_top = lax.optimization_barrier((dq[0], g_qkv[1], da_top))
            oth, left = g_qkv[1].reshape(n_rows, -1, 3 * hw), list(range(net.bits))
            for step in EARLY:
                oth, left = net.halve(oth, left, step)
    own, left2 = g_qkv[0].reshape(n_rows, -1, 3 * hw), list(range(net.bits))
    own, left2 = net.halve(own, left2, 0)
    d_tokens, sums_t = ln1_bwd([*d_qkv[0], *d_qkv[1]], qkv_w, qkv_w2, (da_top, da_rest), d_hidden, tokens, vecs)
    while left:
        oth, left = net.halve(oth, left, left[0])
    oth = net.cross(oth.reshape(-1, 3 * hw).astype(bf16)).astype(f32)
    n_lead = lead_table.shape[0]
    split = sums_b[8:16] + jnp.where(at == 2, bias_rows[0], 0.0) + jnp.where(at == 6, bias_rows[1], 0.0)
    crossed = sums_b[16:] + jnp.where(at == 6, bias_rows[0], 0.0) + jnp.where(at == 2, bias_rows[1], 0.0)
    slots = jnp.where(at == (net.row & 7), sums_t[2:3], 0.0)
    alike = [sums_t + sums_f, sums_b[:8]]
    late = jnp.concatenate(alike + [split, slots]) + net.cross(jnp.concatenate(alike + [crossed, slots]))

    def spread(v, step):
        got = net.flip(v, step)
        if step < 3:
            return v + got
        mine, theirs, low = v[24:], got[24:], net.bit(step) == 0
        return jnp.concatenate([v[:24] + got[:24], jnp.where(low, mine, theirs), jnp.where(low, theirs, mine)])

    crossing = net.cross(jnp.concatenate([grads[:, 2 * ff : 4 * ff], grads[:, 4 * ff + hw :]], axis=1))
    waiting = list(range(net.bits))
    while left2:
        for step in waiting[:2] if len(left2) == net.bits - 1 else waiting[:1]:
            late = spread(late, step)
            waiting.remove(step)
        own, left2 = net.halve(own, left2, left2[0])
        if len(left2) == net.bits - 3:
            own, late, crossing = lax.optimization_barrier((own, late, crossing))
        else:
            own, late = lax.optimization_barrier((own, late))
    for step in waiting:
        late = spread(late, step)
    g_qkv_sum = own.reshape(-1, 3 * hw) + oth
    leads = gathered_lead.astype(jnp.int32)
    chosen = (lax.broadcasted_iota(jnp.int32, (n_lead, n_rows), 0) == leads[None, :]).astype(f32)
    d_table = jnp.dot(chosen, late[24:], precision=lax.Precision.HIGHEST)
    split = late[16:24]
    penalty = late[7, 0] / count_total
    d_bias_qv, d_bias_up_own = split[2], split[: ff // width].reshape(-1)
    grads = jnp.concatenate([grads[:, : 2 * ff], grads[:, 4 * ff : 4 * ff + hw]], axis=1).astype(f32) + crossing.astype(f32)
    blocks = [grads[:, k * FF_BLOCK : (k + 1) * FF_BLOCK] for k in range(2 * ff // FF_BLOCK)]
    g_down = jnp.concatenate(blocks[0::2], axis=1)
    g_up = jnp.concatenate(blocks[1::2], axis=1)
    g_out = grads[:, 2 * ff :]
    return (
        block_out,
        penalty,
        d_tokens,
        d_table,
        late[0],
        late[1],
        g_qkv_sum[:, :hw],
        g_qkv_sum[:, hw : 2 * hw],
        g_qkv_sum[:, 2 * hw :],
        d_bias_qv[:hw],
        d_bias_qv[hw:],
        g_out.T,
        late[10],
        late[8],
        late[9],
        g_up,
        d_bias_up_own,
        g_down.T,
        late[6],
        late[3:6].T,
    )


def solution(mesh):
    in_specs = (
        P(("rows", "heads"), None),
        P("rows"),
        P("rows"),
        P(("rows", "heads")),
        P(),
        P(),
        P(),
        P(None, "heads"),
        P(None, "heads"),
        P(None, "heads"),
        P("heads"),
        P("heads"),
        P("heads", None),
        P(),
        P(),
        P(),
        P(None, "heads"),
        P("heads"),
        P("heads", None),
        P(),
        P(),
        P(("rows", "heads"), None),
    )
    out_specs = (
        P(("rows", "heads"), None),
        P(),
        P(("rows", "heads"), None),
        P(),
        P(),
        P(),
        P("rows", "heads"),
        P("rows", "heads"),
        P("rows", "heads"),
        P("heads"),
        P("heads"),
        P("heads", "rows"),
        P(),
        P(),
        P(),
        P("rows", "heads"),
        P("heads"),
        P("heads", "rows"),
        P(),
        P(),
    )
    return jax.shard_map(
        functools.partial(per_device, mesh.shape["rows"]),
        mesh=mesh,
        in_specs=in_specs,
        out_specs=out_specs,
        check_vma=False,
    )
```

```python
import functools

import jax
import jax.numpy as jnp
from jax import lax
from jax.experimental import pallas as pl
from jax.experimental.pallas import tpu as pltpu
from jax.sharding import PartitionSpec as P

HEAD_DIM = 64
PAIR = 2 * HEAD_DIM
NEG = -1e30
SCALE = HEAD_DIM ** (-0.5)
entropy_weight = 16.0
f32 = jnp.float32
bf16 = jnp.bfloat16
NT = (((1,), (1,)), ((), ()))
TN = (((0,), (0,)), ((), ()))
NN = (((1,), (0,)), ((), ()))
VMEM_LIMIT = 56 << 20
COST_SHARE = 20
MID_LIMIT = 62 << 20


def cost(flops, size):
    return pl.CostEstimate(flops=flops // COST_SHARE, transcendentals=0, bytes_accessed=size // COST_SHARE)


def mm(a, b, dims=NN):
    return lax.dot_general(a, b, dims, preferred_element_type=f32)


def layer_norm(values, gain, shift):
    centre = values - jnp.mean(values, axis=-1, keepdims=True)
    spread = jnp.mean(centre * centre, axis=-1, keepdims=True)
    return centre * lax.rsqrt(spread + 1e-05) * gain + shift


def gelu_exact(values):
    return jax.nn.gelu(values, approximate=False)


def split3(x):
    hi = x.astype(bf16).astype(f32)
    mid = (x - hi).astype(bf16).astype(f32)
    return hi, mid, x - hi - mid


def pair_masks():
    lane = lax.broadcasted_iota(jnp.int32, (1, PAIR), 1)
    return lane, (lane < HEAD_DIM, lane >= HEAD_DIM), (HEAD_DIM, 0)


def own_part(h):
    return slice(0, HEAD_DIM) if h == 0 else slice(HEAD_DIM, PAIR)


def key_bias(meta, keys):
    kpos = meta[0] + lax.broadcasted_iota(jnp.int32, (keys, 1), 0)
    return jnp.where(kpos < meta[1], 0.0, NEG)


def attn_fwd_kernel(first, qb, kc, meta, q_ref, k_ref, v_ref, *refs):
    if first:
        acc_ref, ml_ref, st_sc, p_sc = refs
    else:
        acc_in, ml_in, o_ref, e_ref, acc_sc, e_sc, st_sc, p_sc = refs
    rows = q_ref.shape[0]
    keys = k_ref.shape[0]
    lane, inside, free = pair_masks()
    bias = key_bias(meta, keys)
    q32 = q_ref[...].astype(f32) * SCALE
    k32 = k_ref[...].astype(f32)
    v32 = v_ref[...].astype(f32)
    qx = [jnp.where(inside[h], q32, jnp.where(lane == free[h], 1.0, 0.0)).astype(bf16) for h in range(2)]
    kx = [jnp.where(inside[h], k32, bias).astype(bf16) for h in range(2)]
    vx = [jnp.where(inside[h], v32, 1.0).astype(bf16) for h in range(2)]
    units = [(h, b) for h in range(2) for b in range(rows // qb)]
    chunks = [slice(c * kc, (c + 1) * kc) for c in range(keys // kc)]
    m_prev = None
    for u in range(len(units) + 1):
        slot, prev = u % 2, (u - 1) % 2
        if u < len(units):
            h, b = units[u]
            cols = slice(b * qb, (b + 1) * qb)
        m8 = None
        for ch in chunks:
            if u < len(units):
                st = mm(kx[h][ch], qx[h][cols], NT)
                st_sc[slot, ch, :] = st
                top = jnp.max(st.reshape(kc // 8, 8, qb), axis=0)
                m8 = top if m8 is None else jnp.maximum(m8, top)
            if u > 0:
                p_sc[prev, ch, :] = jnp.exp(st_sc[prev, ch, :] - m_prev).astype(bf16)
        if u > 0:
            hp, bp = units[u - 1]
            pc = slice(bp * qb, (bp + 1) * qb)
            ot = mm(vx[hp], p_sc[prev], TN)
            fe = free[hp]
            own = own_part(hp)
            total = ot[fe : fe + 1]
            num = ot[own]
            if first:
                acc_ref[own, pc] = num
                ml_ref[hp : hp + 1, pc] = m_prev
                ml_ref[2 + hp : 3 + hp, pc] = total
            else:
                alpha = jnp.exp(ml_in[hp : hp + 1, pc] - m_prev)
                total = total + alpha * ml_in[2 + hp : 3 + hp, pc]
                num = num + alpha * acc_in[own, pc]
                acc_sc[own, pc] = num / total
                hi, mid, lo = split3(m_prev + jnp.log(total))
                row = lax.broadcasted_iota(jnp.int32, (HEAD_DIM, 1), 0)
                e_sc[fe : fe + HEAD_DIM, pc] = jnp.where(
                    row == 0, 1.0, jnp.where(row == 1, -hi, jnp.where(row == 2, -mid, jnp.where(row == 3, -lo, 0.0)))
                )
        if u < len(units):
            m_prev = jnp.max(m8, axis=0, keepdims=True)
            if not first:
                m_prev = jnp.maximum(m_prev, ml_in[h : h + 1, cols])
    if not first:
        o_ref[...] = acc_sc[...].T.astype(bf16)
        e_ref[...] = e_sc[...].T.astype(bf16)


def attn_fwd(meta, q, k, v, pairs, state=None, qb=1024, kc=256):
    rows = q[0].shape[0]
    keys = k[0].shape[0]
    width = pairs * PAIR
    first = state is None

    def col(off):
        return lambda i, m: (0, off + i)

    def down(i, m):
        return (i, 0)

    in_specs = [
        pl.BlockSpec((rows, PAIR), col(q[1])),
        pl.BlockSpec((keys, PAIR), col(k[1])),
        pl.BlockSpec((keys, PAIR), col(v[1])),
    ]
    scratch = [pltpu.VMEM((2, keys, qb), f32), pltpu.VMEM((2, keys, qb), bf16)]
    args = (q[0], k[0], v[0])
    if first:
        out_shape = (jax.ShapeDtypeStruct((width, rows), f32), jax.ShapeDtypeStruct((8 * pairs, rows), f32))
        out_specs = (pl.BlockSpec((PAIR, rows), down), pl.BlockSpec((8, rows), down))
    else:
        in_specs += [pl.BlockSpec((PAIR, rows), down), pl.BlockSpec((8, rows), down)]
        out_shape = (jax.ShapeDtypeStruct((rows, width), bf16), jax.ShapeDtypeStruct((rows, width), bf16))
        out_specs = (pl.BlockSpec((rows, PAIR), col(0)), pl.BlockSpec((rows, PAIR), col(0)))
        scratch = [pltpu.VMEM((PAIR, rows), f32), pltpu.VMEM((PAIR, rows), f32)] + scratch
        args = args + tuple(state)
    return pl.pallas_call(
        functools.partial(attn_fwd_kernel, first, qb, kc),
        grid_spec=pltpu.PrefetchScalarGridSpec(
            num_scalar_prefetch=1, grid=(pairs,), in_specs=in_specs, out_specs=out_specs, scratch_shapes=scratch
        ),
        out_shape=out_shape,
        compiler_params=pltpu.CompilerParams(vmem_limit_bytes=VMEM_LIMIT),
        cost_estimate=cost(16 * rows * keys * width, 8 * rows * width),
        name="attn_fwd_first" if first else "attn_fwd_second",
    )(meta, *args)


def attn_bwd_kernel(first, qb, kc, meta, q_ref, e_ref, o_ref, do_ref, k_ref, v_ref, *refs):
    if first:
        dq_ref, dk_ref, dv_ref, dk_sc, dv_sc, s_sc, dp_sc, p_sc, ds_sc = refs
    else:
        dq_in, dq_ref, dk_ref, dv_ref, dk_sc, dv_sc, s_sc, dp_sc, p_sc, ds_sc = refs
    rows = q_ref.shape[0]
    keys = k_ref.shape[0]
    lane, inside, free = pair_masks()
    bias = key_bias(meta, keys)
    k32 = k_ref[...].astype(f32)
    v32 = v_ref[...].astype(f32)
    kx = [jnp.where(inside[h], k32, jnp.where(lane == free[h], bias, 1.0)).astype(bf16) for h in range(2)]
    vx = [jnp.where(inside[h], v32, 1.0).astype(bf16) for h in range(2)]
    units = [(b, h) for b in range(rows // qb) for h in range(2)]
    chunks = [slice(c * kc, (c + 1) * kc) for c in range(keys // kc)]
    prep = None
    dq0 = None
    for u in range(len(units) + 1):
        before = prep
        slot, prev = u % 2, (u - 1) % 2
        if u < len(units):
            b, h = units[u]
            rs = slice(b * qb, (b + 1) * qb)
            fe = free[h]
            if h == 0:
                q32 = q_ref[rs].astype(f32) * SCALE
                do32 = do_ref[rs].astype(f32)
                e32 = e_ref[rs].astype(f32)
                prod = do32 * o_ref[rs].astype(f32)
            hi, mid, lo = split3(jnp.sum(jnp.where(inside[h], prod, 0.0), axis=1, keepdims=True))
            dext = jnp.where(lane == fe, -hi, jnp.where(lane == fe + 1, -mid, jnp.where(lane == fe + 2, -lo, 0.0)))
            qx = jnp.where(inside[h], q32, e32).astype(bf16)
            dox = jnp.where(inside[h], do32, dext).astype(bf16)
            prep = (qx, dox)
        for ch in chunks:
            if u < len(units):
                s_sc[slot, :, ch] = mm(qx, kx[h][ch], NT)
                dp_sc[slot, :, ch] = mm(dox, vx[h][ch], NT)
            if u > 0:
                p = jnp.exp(s_sc[prev, :, ch])
                p_sc[prev, :, ch] = p.astype(bf16)
                ds_sc[prev, :, ch] = (p * dp_sc[prev, :, ch]).astype(bf16)
        if u > 0:
            bp, hp = units[u - 1]
            rp = slice(bp * qb, (bp + 1) * qb)
            qxp, doxp = before
            dvt = mm(doxp, p_sc[prev], TN)
            dkt = mm(qxp, ds_sc[prev], TN)
            dqh = mm(ds_sc[prev], kx[hp], NN)
            own = own_part(hp)
            if bp == 0:
                dv_sc[own] = dvt[own]
                dk_sc[own] = dkt[own]
            else:
                dv_sc[own] += dvt[own]
                dk_sc[own] += dkt[own]
            if hp == 0:
                dq0 = dqh
            else:
                dq = jnp.where(lane < HEAD_DIM, dq0, dqh) * SCALE
                if first:
                    dq_ref[rp] = dq
                else:
                    dq_ref[rp] = (dq + dq_in[rp]).astype(bf16)
    dk_ref[...] = dk_sc[...].T.astype(bf16)
    dv_ref[...] = dv_sc[...].T.astype(bf16)


def attn_bwd(meta, q, e, o, do, k, v, pairs, dq_prev=None, qb=256, kc=256):
    rows = q[0].shape[0]
    keys = k[0].shape[0]
    width = pairs * PAIR
    first = dq_prev is None

    def col(off):
        return lambda i, m: (0, off + i)

    in_specs = [pl.BlockSpec((rows, PAIR), col(off)) for _, off in (q, e, o, do)]
    in_specs += [pl.BlockSpec((keys, PAIR), col(off)) for _, off in (k, v)]
    args = (q[0], e[0], o[0], do[0], k[0], v[0])
    rspec = pl.BlockSpec((rows, PAIR), col(0))
    kspec = pl.BlockSpec((keys, PAIR), col(0))
    if not first:
        in_specs.append(rspec)
        args = args + (dq_prev,)
    return pl.pallas_call(
        functools.partial(attn_bwd_kernel, first, qb, kc),
        grid_spec=pltpu.PrefetchScalarGridSpec(
            num_scalar_prefetch=1,
            grid=(pairs,),
            in_specs=in_specs,
            out_specs=(rspec, kspec, kspec),
            scratch_shapes=[pltpu.VMEM((PAIR, keys), f32)] * 2
            + [pltpu.VMEM((2, qb, keys), f32)] * 2
            + [pltpu.VMEM((2, qb, keys), bf16)] * 2,
        ),
        out_shape=(
            jax.ShapeDtypeStruct((rows, width), f32 if first else bf16),
            jax.ShapeDtypeStruct((keys, width), bf16),
            jax.ShapeDtypeStruct((keys, width), bf16),
        ),
        compiler_params=pltpu.CompilerParams(vmem_limit_bytes=VMEM_LIMIT),
        cost_estimate=cost(40 * rows * keys * width, 16 * rows * width),
        name="attn_bwd_first" if first else "attn_bwd_second",
    )(meta, *args)


FF_BLOCK = 768
EARLY = (0, 1)
CHUNK = 256


def row_chunks(rows):
    return [slice(c, c + CHUNK) for c in range(0, rows, CHUNK)]


EMB, B_OUT, GAIN_2, SHIFT_2, B_DOWN, GAIN_1, SHIFT_1 = (slice(i, i + 1) for i in range(7))


def normalise(values):
    centre = values - jnp.mean(values, axis=-1, keepdims=True)
    spread = jnp.mean(centre * centre, axis=-1, keepdims=True)
    rstd = lax.rsqrt(spread + 1e-05)
    return centre * rstd, rstd


def gelu_pair(u):
    cdf = 0.5 * (1.0 + lax.erf(u * 0.7071067811865476))
    density = 0.3989422804014327 * jnp.exp(-0.5 * u * u)
    return u * cdf, cdf + u * density


def pick(step, n_own, own, other):
    return jnp.where(step < n_own, own, other)


def mid_kernel(
    n_own, scal, tok_ref, vec_ref, o0_ref, o1_ref, wo_ref, wo2_ref, bup_ref, up_ref, up2_ref, down_ref, down2_ref, wg_ref,
    cnt_ref, cot_ref, out_ref, grads_ref, dh_ref, da_ref, sums_ref, acc, h1_sc, nt_sc, dm_sc, g_sc, gp_sc,
):
    step = pl.program_id(0)
    n_blocks = 2 * n_own
    rows, width = tok_ref.shape
    chunks = row_chunks(rows)

    @pl.when(step == 0)
    def _():
        sums_ref[...] = jnp.zeros_like(sums_ref)
        wo2 = wo2_ref[...].reshape(wo_ref.shape)
        for c in chunks:
            h1 = tok_ref[c].astype(f32) + vec_ref[EMB]
            h1 = h1 + (mm(o0_ref[c], wo_ref[...]) + mm(o1_ref[c], wo2) + vec_ref[B_OUT])
            h1_sc[c] = h1
            xhat, _ = normalise(h1)
            nt_sc[c] = (xhat * vec_ref[GAIN_2] + vec_ref[SHIFT_2]).astype(bf16)
            acc[c] = h1 + vec_ref[B_DOWN]

    @pl.when(step < n_blocks)
    def _():
        up = pick(step, n_own, up_ref[...], up2_ref[...].reshape(up_ref.shape))
        down = pick(step, n_own, down_ref[...], down2_ref[...].reshape(down_ref.shape))
        u = mm(nt_sc[chunks[0]], up)
        for i, c in enumerate(chunks):
            ahead = mm(nt_sc[chunks[i + 1]], up) if i + 1 < len(chunks) else None
            g, gp = gelu_pair(u + bup_ref[...])
            g = g.astype(bf16)
            g_sc[step, c] = g
            gp_sc[step, c] = gp.astype(bf16)
            acc[c] += mm(g, down)
            u = ahead

    @pl.when(step == n_blocks - 1)
    def _():
        dbd = jnp.zeros((1, width), f32)
        dwg = [jnp.zeros((1, width), f32) for _ in range(3)]
        ent_sum = jnp.zeros((1, 1), f32)
        for c in chunks:
            out = acc[c]
            out_ref[c] = out.astype(bf16)
            z = [jnp.sum(out * wg_ref[e : e + 1], axis=-1, keepdims=True) for e in range(3)]
            top = jnp.maximum(jnp.maximum(z[0], z[1]), z[2])
            log_sum = jnp.log(sum(jnp.exp(v - top) for v in z)) + top
            logp = [v - log_sum for v in z]
            prob = [jnp.exp(v) for v in logp]
            entropy = -sum(p * q for p, q in zip(prob, logp))
            mean = sum(p * v for p, v in zip(prob, z))
            counted = cnt_ref[c]
            ent_sum = ent_sum + jnp.sum(counted * entropy, axis=0, keepdims=True)
            dz = [scal[0] * counted * (-p * (v - mean)) for p, v in zip(prob, z)]
            d_out = cot_ref[c].astype(f32) + sum(d * wg_ref[e : e + 1] for e, d in enumerate(dz))
            dm = d_out.astype(bf16)
            dm_sc[c] = dm
            dbd = dbd + jnp.sum(dm.astype(f32), axis=0, keepdims=True)
            dwg = [w + jnp.sum(out * d, axis=0, keepdims=True) for w, d in zip(dwg, dz)]
            acc[c] = d_out
            dh_ref[c] = jnp.zeros_like(d_out)
        for e in range(3):
            sums_ref[3 + e : 4 + e] = dwg[e]
        sums_ref[6:7] = dbd
        sums_ref[7:8] = jnp.broadcast_to(ent_sum, (1, width))

    @pl.when(step >= n_blocks)
    def _():
        j = step - n_blocks
        up = pick(j, n_own, up_ref[...], up2_ref[...].reshape(up_ref.shape))
        down = pick(j, n_own, down_ref[...], down2_ref[...].reshape(down_ref.shape))
        bias = jnp.zeros((1, FF_BLOCK), f32)
        for c in chunks:
            du = (mm(dm_sc[c], down, NT) * gp_sc[j, c].astype(f32)).astype(bf16)
            gp_sc[j, c] = du
            bias = bias + jnp.sum(du.astype(f32), axis=0, keepdims=True)
            dh_ref[c] += mm(du, up, NT)
        sums_ref[pl.ds(16 + 4 * (j // n_own) + j % n_own, 1)] = bias
        sums_ref[pl.ds(28 - 4 * (j // n_own) + j % n_own, 1)] = bias
        grads_ref[:, :FF_BLOCK] = mm(dm_sc[...], g_sc[j], TN).astype(bf16)
        grads_ref[:, FF_BLOCK:] = mm(nt_sc[...], gp_sc[j], TN).astype(bf16)

    @pl.when(step == 2 * n_blocks - 1)
    def _():
        d_gain = jnp.zeros((1, width), f32)
        d_shift = jnp.zeros((1, width), f32)
        d_bias = jnp.zeros((1, width), f32)
        for c in chunks:
            db = dh_ref[c]
            xhat, rstd = normalise(h1_sc[c])
            d_gain = d_gain + jnp.sum(db * xhat, axis=0, keepdims=True)
            d_shift = d_shift + jnp.sum(db, axis=0, keepdims=True)
            dx = db * vec_ref[GAIN_2]
            low = jnp.mean(dx, axis=-1, keepdims=True)
            slope = jnp.mean(dx * xhat, axis=-1, keepdims=True)
            dh = acc[c] + rstd * (dx - low - xhat * slope)
            dh_ref[c] = dh
            da = dh.astype(bf16)
            da_ref[c] = da
            d_bias = d_bias + jnp.sum(da.astype(f32), axis=0, keepdims=True)
        sums_ref[8:9] = d_gain
        sums_ref[9:10] = d_shift
        sums_ref[10:11] = d_bias


def fixed(shape, **mode):
    zeros = (0,) * len(shape)
    return pl.BlockSpec(shape, lambda *_: zeros, **mode)


def weight_specs(gathered, width, ff):
    n_own = ff // FF_BLOCK
    parts, _, _ = gathered.shape
    k_up, k_down = width // parts, ff // parts
    per_step = FF_BLOCK // k_down
    cols = width // FF_BLOCK

    n_blocks = 2 * n_own

    def own(j):
        return jnp.minimum(lax.rem(j, n_blocks), n_own - 1)

    def other(j):
        return jnp.maximum(lax.rem(j, n_blocks) - n_own, 0)

    return n_own, [
        pl.BlockSpec((width, FF_BLOCK), lambda j, *_: (0, own(j))),
        pl.BlockSpec((parts, k_up, FF_BLOCK), lambda j, *_: (0, other(j) // cols, other(j) % cols)),
        pl.BlockSpec((FF_BLOCK, width), lambda j, *_: (own(j), 0)),
        pl.BlockSpec((per_step, k_down, width), lambda j, *_: (other(j), 2 * k_up // k_down, 0)),
    ]


def out_spec(gathered, width, ff, hw):
    parts = gathered.shape[0]
    k_out = hw // parts
    return pl.BlockSpec((parts, k_out, width), lambda *_: (0, (2 * width + ff) // parts // k_out, 0))


def feed_forward(scal, tokens, vecs, o0, o1, w_out, gathered, b_up, w_up, w_down, wg, counted, cot, grad_cols):
    rows, width = tokens.shape
    ff = w_down.shape[0]
    n_own, (up_s, up2_s, down_s, down2_s) = weight_specs(gathered, width, ff)
    n_blocks = 2 * n_own
    hw = w_out.shape[0]
    once = {"pipeline_mode": pl.Buffered(1)}
    wo2_s = out_spec(gathered, width, ff, hw)
    return pl.pallas_call(
        functools.partial(mid_kernel, n_own),
        grid_spec=pltpu.PrefetchScalarGridSpec(
            num_scalar_prefetch=1,
            grid=(2 * n_blocks,),
            in_specs=[
                fixed((rows, width), **once),
                fixed((8, width)),
                fixed((rows, hw), **once),
                fixed((rows, hw), **once),
                fixed((hw, width), **once),
                pl.BlockSpec(wo2_s.block_shape, wo2_s.index_map, **once),
                pl.BlockSpec((1, FF_BLOCK), lambda j, *_: (0, lax.rem(j, n_blocks))),
                up_s,
                up2_s,
                down_s,
                down2_s,
                fixed((8, width)),
                fixed((rows, 1), **once),
                fixed((rows, width), **once),
            ],
            out_specs=[
                fixed((rows, width)),
                pl.BlockSpec((width, 2 * FF_BLOCK), lambda j, *_: (0, jnp.maximum(j - n_blocks, 0))),
                fixed((rows, width)),
                fixed((rows, width)),
                fixed((32, width)),
            ],
            scratch_shapes=[
                pltpu.VMEM((rows, width), f32),
                pltpu.VMEM((rows, width), f32),
                pltpu.VMEM((rows, width), bf16),
                pltpu.VMEM((rows, width), bf16),
                pltpu.VMEM((n_blocks, rows, FF_BLOCK), bf16),
                pltpu.VMEM((n_blocks, rows, FF_BLOCK), bf16),
            ],
        ),
        out_shape=[
            jax.ShapeDtypeStruct((rows, width), bf16),
            jax.ShapeDtypeStruct((width, grad_cols), bf16),
            jax.ShapeDtypeStruct((rows, width), f32),
            jax.ShapeDtypeStruct((rows, width), bf16),
            jax.ShapeDtypeStruct((32, width), f32),
        ],
        compiler_params=pltpu.CompilerParams(vmem_limit_bytes=MID_LIMIT),
        cost_estimate=cost(36 * rows * width * ff, 40 * rows * width),
        name="mid",
    )(scal, tokens, vecs, o0, o1, w_out, gathered, b_up, w_up, gathered, w_down, gathered, wg, counted, cot)


def out_bwd_kernel(da_ref, o0_ref, o1_ref, wo_ref, wo2_ref, _, do_ref, do2_ref, grads_ref):
    hw = wo_ref.shape[0]
    do_ref[...] = mm(da_ref[...], wo_ref[...], NT).astype(bf16)
    do2_ref[...] = mm(da_ref[...], wo2_ref[...].reshape(wo_ref.shape), NT).astype(bf16)
    grads_ref[:, :hw] = mm(da_ref[...], o0_ref[...], TN).astype(bf16)
    grads_ref[:, hw:] = mm(da_ref[...], o1_ref[...], TN).astype(bf16)


def out_bwd(d_attn, o0, o1, w_out, gathered, ff, grads):
    rows, width = d_attn.shape
    hw = w_out.shape[0]
    half = fixed((rows, hw))
    return pl.pallas_call(
        out_bwd_kernel,
        grid=(1,),
        in_specs=[
            fixed((rows, width)), half, half, fixed((hw, width)), out_spec(gathered, width, ff, hw),
            pl.BlockSpec(memory_space=pl.ANY),
        ],
        out_specs=[half, half, pl.BlockSpec((width, 2 * hw), lambda j: (0, grads.shape[1] // (2 * hw) - 1))],
        out_shape=[
            jax.ShapeDtypeStruct((rows, hw), bf16),
            jax.ShapeDtypeStruct((rows, hw), bf16),
            jax.ShapeDtypeStruct(grads.shape, bf16),
        ],
        input_output_aliases={5: 2},
        compiler_params=pltpu.CompilerParams(vmem_limit_bytes=VMEM_LIMIT),
        cost_estimate=cost(8 * rows * width * hw, 12 * rows * width),
        name="out_bwd",
    )(d_attn, o0, o1, w_out, gathered, grads)


def qkv_grads_kernel(n_ref, no_ref, dq_ref, dk_ref, dv_ref, dko_ref, dvo_ref, grads_ref, sums_ref):
    hw = dq_ref.shape[1]
    grads_ref[:, :hw] = mm(n_ref[...], dq_ref[...], TN).astype(bf16)
    kv = jnp.concatenate([dk_ref[...], dv_ref[...]], axis=1)
    kvo = jnp.concatenate([dko_ref[...], dvo_ref[...]], axis=1)
    grads_ref[:, hw:] = (mm(n_ref[...], kv, TN) + mm(no_ref[...], kvo, TN)).astype(bf16)
    bq = jnp.sum(dq_ref[...].astype(f32), axis=0, keepdims=True)
    bv = jnp.sum(dv_ref[...].astype(f32), axis=0, keepdims=True) + jnp.sum(dvo_ref[...].astype(f32), axis=0, keepdims=True)
    sums_ref[:, :hw] = jnp.broadcast_to(bq, (8, hw))
    sums_ref[:, hw:] = jnp.broadcast_to(bv, (8, hw))


def qkv_grads(normed, normed_oth, dq, dk, dv, dk_oth, dv_oth):
    rows, width = normed.shape
    hw = dq.shape[1]
    full, half = fixed((rows, width)), fixed((rows, hw))
    return pl.pallas_call(
        qkv_grads_kernel,
        grid=(1,),
        in_specs=[full, full] + [half] * 5,
        out_specs=[fixed((width, 3 * hw)), fixed((8, 2 * hw))],
        out_shape=[jax.ShapeDtypeStruct((width, 3 * hw), bf16), jax.ShapeDtypeStruct((8, 2 * hw), f32)],
        compiler_params=pltpu.CompilerParams(vmem_limit_bytes=VMEM_LIMIT),
        cost_estimate=cost(10 * rows * width * hw, 10 * rows * width),
        name="qkv_grads",
    )(normed, normed_oth, dq, dk, dv, dk_oth, dv_oth)


def ln1_bwd_kernel(n_parts, *refs):
    parts, (w0_ref, w1_ref, got0_ref, got1_ref, dh_ref, tok_ref, vec_ref, dtok_ref, sums_ref) = refs[:n_parts], refs[n_parts:]
    upper = pl.program_id(0) < pl.num_programs(0) // 2
    da = jnp.where(upper, got0_ref[...], got1_ref[...]).astype(f32)
    for i, w_ref in enumerate((w0_ref, w1_ref)):
        joined = jnp.concatenate([part[...] for part in parts[3 * i : 3 * i + 3]], axis=1)
        da = da + mm(joined, w_ref[...], NT)
    xhat, rstd = normalise(tok_ref[...].astype(f32) + vec_ref[EMB])
    dx = da * vec_ref[GAIN_1]
    low = jnp.mean(dx, axis=-1, keepdims=True)
    slope = jnp.mean(dx * xhat, axis=-1, keepdims=True)
    d_tokens = dh_ref[...] + rstd * (dx - low - xhat * slope)
    dtok_ref[...] = d_tokens
    new = [jnp.sum(v, axis=0, keepdims=True) for v in (da * xhat, da, d_tokens)]

    @pl.when(pl.program_id(0) == 0)
    def _():
        sums_ref[...] = jnp.zeros_like(sums_ref)

    for i, v in enumerate(new):
        sums_ref[i : i + 1] += v


def ln1_bwd(d_qkv, w0, w1, da_got, d_hidden, tokens, vecs):
    rows, width = tokens.shape
    hw = d_qkv[0].shape[1]
    step = CHUNK
    n_half = rows // step // 2
    blk = pl.BlockSpec((step, width), lambda i: (i, 0))
    half = pl.BlockSpec((step, hw), lambda i: (i, 0))
    return pl.pallas_call(
        functools.partial(ln1_bwd_kernel, len(d_qkv)),
        grid=(rows // step,),
        in_specs=[half] * len(d_qkv) + [fixed((width, 3 * hw))] * 2
        + [
            pl.BlockSpec((step, width), lambda i: (jnp.minimum(i, n_half - 1), 0)),
            pl.BlockSpec((step, width), lambda i: (jnp.maximum(i - n_half, 0), 0)),
            blk,
            blk,
            fixed((8, width)),
        ],
        out_specs=[blk, fixed((8, width))],
        out_shape=[jax.ShapeDtypeStruct((rows, width), f32), jax.ShapeDtypeStruct((8, width), f32)],
        compiler_params=pltpu.CompilerParams(vmem_limit_bytes=VMEM_LIMIT),
        cost_estimate=cost(12 * rows * width * hw, 20 * rows * width),
        name="ln1_bwd",
    )(*d_qkv, w0, w1, *da_got, d_hidden, tokens, vecs)


def oth_bwd_kernel(k0_ref, v0_ref, k1_ref, v1_ref, w0_ref, w1_ref, da_ref):
    hw = k0_ref.shape[1]
    da = mm(jnp.concatenate([k0_ref[...], v0_ref[...]], axis=1), w0_ref[:, hw:], NT)
    da_ref[...] = (da + mm(jnp.concatenate([k1_ref[...], v1_ref[...]], axis=1), w1_ref[:, hw:], NT)).astype(bf16)


def oth_bwd(d_kv, w0, w1):
    rows, hw = d_kv[0].shape
    width = w0.shape[0]
    step = 2 * CHUNK
    half = pl.BlockSpec((step, hw), lambda i: (i, 0))
    return pl.pallas_call(
        oth_bwd_kernel,
        grid=(rows // step,),
        in_specs=[half] * 4 + [fixed(w0.shape)] * 2,
        out_specs=pl.BlockSpec((step, width), lambda i: (i, 0)),
        out_shape=jax.ShapeDtypeStruct((rows, width), bf16),
        compiler_params=pltpu.CompilerParams(vmem_limit_bytes=VMEM_LIMIT),
        cost_estimate=cost(8 * rows * width * hw, 4 * rows * width),
        name="oth_bwd",
    )(*d_kv, w0, w1)


def front_kernel(starts, tok_ref, vec_ref, *refs):
    n = len(starts)
    xhat, _ = normalise(tok_ref[...].astype(f32) + vec_ref[EMB])
    normed = (xhat * vec_ref[GAIN_1] + vec_ref[SHIFT_1]).astype(bf16)
    refs[2 * n][...] = normed
    for i, start in enumerate(starts):
        y = mm(normed, refs[2 * i][:, start:]) + refs[2 * i + 1][:, start:]
        refs[2 * n + 1 + i][...] = y.astype(bf16)


def front(tokens, vecs, weights):
    rows, width = tokens.shape
    step = CHUNK
    in_specs = [pl.BlockSpec((step, width), lambda i: (i, 0)), fixed((8, width))]
    args = [tokens, vecs]
    outs = [width]
    for w, b, start in weights:
        in_specs += [fixed(w.shape), fixed(b.shape)]
        args += [w, b]
        outs.append(w.shape[1] - start)
    return pl.pallas_call(
        functools.partial(front_kernel, tuple(start for _, _, start in weights)),
        grid=(rows // step,),
        in_specs=in_specs,
        out_specs=[pl.BlockSpec((step, n), lambda i: (i, 0)) for n in outs],
        out_shape=[jax.ShapeDtypeStruct((rows, n), bf16) for n in outs],
        compiler_params=pltpu.CompilerParams(vmem_limit_bytes=VMEM_LIMIT),
        cost_estimate=cost(2 * rows * width * sum(outs[1:]), 8 * rows * width),
        name="front",
    )(*args)


def pack_kernel(row, up_ref, down_ref, out_ref, rest_ref, share_ref):
    width = share_ref.shape[1]
    at = 0
    for part in (up_ref[:, :width], up_ref[:, width:], down_ref[...], out_ref[...], rest_ref[...]):
        share_ref[at : at + part.shape[0]] = part
        at += part.shape[0]


def pack_share(row, n_rows, w_up, w_down, w_out, rest):
    width = w_out.shape[1]
    sizes = [w.shape[0] // n_rows for w in (w_up, w_down, w_out)]
    total = 2 * sizes[0] + sizes[1] + sizes[2] + rest.shape[0]
    if sizes[0] % 16:
        up, down, out = (lax.dynamic_slice_in_dim(w, row * k, k, 0) for w, k in zip((w_up, w_down, w_out), sizes))
        return jnp.concatenate([up[:, :width], up[:, width:], down, out, rest])
    return pl.pallas_call(
        pack_kernel,
        grid_spec=pltpu.PrefetchScalarGridSpec(
            num_scalar_prefetch=1,
            grid=(1,),
            in_specs=[pl.BlockSpec((k, w.shape[1]), lambda i, r: (r[0], 0)) for w, k in zip((w_up, w_down, w_out), sizes)]
            + [fixed(rest.shape)],
            out_specs=fixed((total, width)),
        ),
        out_shape=jax.ShapeDtypeStruct((total, width), bf16),
        name="pack_share",
    )(row.reshape(1), w_up, w_down, w_out, rest)


class Net:
    def __init__(self, n_rows):
        self.n_rows = n_rows
        self.bits = n_rows.bit_length() - 1
        self.row = lax.axis_index("rows")

    def cross(self, x):
        return lax.ppermute(x, "heads", [(0, 1), (1, 0)])

    def flip(self, x, bit):
        return lax.ppermute(x, "rows", [(i, i ^ (1 << bit)) for i in range(self.n_rows)])

    def bit(self, b):
        return (self.row >> b) & 1

    def fetch(self, own):
        part = own.shape[0] // 2
        return self.cross(lax.dynamic_slice_in_dim(own, self.bit(0) * part, part, 0))

    def join(self, got):
        passed = self.flip(got, 0)
        low = self.bit(0) == 0
        return jnp.concatenate([jnp.where(low, got, passed), jnp.where(low, passed, got)], axis=0)

    def halve(self, part, left, step):
        low = 1 << left.index(step)
        blocks, piece, cols = part.shape
        view = part.reshape(blocks // (2 * low), 2, low, piece, cols)
        at = self.bit(step)
        keep = lax.dynamic_index_in_dim(view, at, 1, keepdims=False)
        got = self.flip(lax.dynamic_index_in_dim(view, 1 - at, 1, keepdims=False).astype(bf16), step)
        return (keep.astype(f32) + got.astype(f32)).reshape(blocks // 2, piece, cols), [x for x in left if x != step]


def per_device(
    n_rows,
    tokens,
    crop_lengths,
    lead_index,
    valid_mask,
    lead_table,
    ln1_gain,
    ln1_shift,
    w_query,
    w_key,
    w_value,
    b_query,
    b_value,
    w_out,
    b_out,
    ln2_gain,
    ln2_shift,
    w_up,
    b_up,
    w_down,
    b_down,
    w_gater,
    cotangent,
):
    net = Net(n_rows)
    own_rows, width = tokens.shape
    half = lax.axis_index("heads")
    length = crop_lengths[0]
    hw = w_query.shape[1]
    pairs = hw // PAIR
    own_start = half * own_rows
    meta_own = jnp.stack([own_start, length])
    meta_oth = jnp.stack([own_rows - own_start, length])

    positions = own_start + jnp.arange(own_rows, dtype=jnp.int32)
    counted = ((positions < length) & (valid_mask == 1)).astype(f32)
    count = jnp.sum(counted)

    qkv_w = jnp.concatenate([w_query, w_key, w_value], axis=1)
    bias_own = jnp.concatenate([b_query, b_value, b_up]).reshape(1, -1)
    k_up, k_down, k_out = width // n_rows, w_down.shape[0] // n_rows, w_out.shape[0] // n_rows
    n_share = 2 * k_up + k_down + k_out
    pad = -n_share % 16 + 16
    n_bias = bias_own.size // width
    line = lax.broadcasted_iota(jnp.int32, (pad, width), 0)
    lane = lax.broadcasted_iota(jnp.int32, (pad, width), 1)
    high = jnp.floor(count / 32)
    tally = jnp.where(lane == 0, high, jnp.where(lane == 1, count - 32 * high, 0.0))
    tally = jnp.where(lane == 2, lead_index[0].astype(f32), tally).astype(bf16)
    rest = tally
    for i in range(n_bias):
        rest = jnp.where(line == 1 + i, bias_own[:, i * width : (i + 1) * width], rest)
    got = net.cross(pack_share(net.row, n_rows, w_up, w_down, w_out, rest))
    bias_oth = got[n_share + 1 : n_share + 1 + n_bias].reshape(1, -1)
    tokens_in, got = lax.optimization_barrier((tokens, got))
    share = jnp.concatenate([got, tally], axis=0)
    tokens_oth = net.cross(tokens)
    at = lax.broadcasted_iota(jnp.int32, (8, 1), 0)
    picked = jnp.arange(lead_table.shape[0], dtype=jnp.int32) == lead_index[0]
    embedding = jnp.sum(jnp.where(picked[:, None], lead_table, 0.0), axis=0)
    vecs = jnp.zeros((8, width), f32)
    for i, v in enumerate((embedding, b_out, ln2_gain, ln2_shift, b_down, ln1_gain, ln1_shift)):
        vecs = jnp.where(at == i, v, vecs)

    def qkv_bias(b):
        b = b.astype(f32)
        return jnp.concatenate([b[:, :hw], jnp.zeros((1, hw), f32), b[:, hw : 2 * hw]], axis=1)

    qkv_b = qkv_bias(bias_own)
    normed, qkv_own = front(tokens_in, vecs, [(qkv_w, qkv_b, 0)])
    gathered = lax.all_gather(share, "rows", axis=0, tiled=False)
    tally = gathered[:, n_share:, :2].astype(f32)
    gathered_lead = gathered[:, n_share + pad, 2]
    count_total = jnp.sum(tally[:, 0] * jnp.array([32.0, 1.0])) + jnp.sum(tally[:, pad] * jnp.array([32.0, 1.0]))
    if k_up % 16 or k_down % 16:
        sizes = (k_up, k_up, k_down, k_out)
        starts = (0, k_up, 2 * k_up, 2 * k_up + k_down)
        gathered = jnp.concatenate(
            [gathered[:, a : a + k].reshape(16, k * n_rows // 16, width) for a, k in zip(starts, sizes)], axis=1
        )

    qkv_b2 = qkv_bias(bias_oth)
    up_b, up_b2 = bias_own[:, 2 * hw :].astype(f32), bias_oth[:, 2 * hw :].astype(f32)

    state = attn_fwd(meta_own, (qkv_own, 0), (qkv_own, pairs), (qkv_own, 2 * pairs), pairs)
    tokens_oth, state, qkv_in = lax.optimization_barrier((tokens_oth, state, qkv_w))
    got_w = net.fetch(qkv_in)
    normed_oth, kv_own = front(tokens_oth, vecs, [(qkv_w, qkv_b, hw)])
    attn_own, ext_own = attn_fwd(meta_oth, (qkv_own, 0), (kv_own, 0), (kv_own, pairs), pairs, state)
    got_w, attn_own = lax.optimization_barrier((got_w, attn_own))
    qkv_w2 = net.join(got_w)
    qkv_two = (mm(normed, qkv_w2) + qkv_b2).astype(bf16)
    kv_two = (mm(normed_oth, qkv_w2[:, hw:]) + qkv_b2[:, hw:]).astype(bf16)
    state = attn_fwd(meta_own, (qkv_two, 0), (qkv_two, pairs), (qkv_two, 2 * pairs), pairs)
    attn_two, ext_two = attn_fwd(meta_oth, (qkv_two, 0), (kv_two, 0), (kv_two, pairs), pairs, state)
    qkv, kv_oth, attn, ext = (qkv_own, qkv_two), (kv_own, kv_two), (attn_own, attn_two), (ext_own, ext_two)

    ff = w_down.shape[0]
    block_out, grads, d_hidden, d_attn, sums_m = feed_forward(
        (entropy_weight / count_total).reshape(1),
        tokens,
        vecs,
        attn[0],
        attn[1],
        w_out,
        gathered,
        jnp.concatenate([up_b, up_b2], axis=1),
        w_up,
        w_down,
        jnp.concatenate([w_gater.T, jnp.zeros((5, width), f32)]),
        counted.reshape(-1, 1),
        cotangent,
        4 * ff + 2 * hw,
    )
    do_own, do_oth, grads = out_bwd(d_attn, attn[0], attn[1], w_out, gathered, ff, grads)
    d_heads = (do_own, do_oth)
    grads = lax.psum_scatter(grads, "rows", scatter_dimension=0, tiled=True)

    dq, dk_oth, dv_oth = [], [], []
    for i in range(2):
        a, b, c = attn_bwd(
            meta_oth, (qkv[i], 0), (ext[i], 0), (attn[i], 0), (d_heads[i], 0), (kv_oth[i], 0), (kv_oth[i], pairs), pairs
        )
        dq.append(a)
        dk_oth.append(b)
        dv_oth.append(c)
    da_oth = oth_bwd((dk_oth[0], dv_oth[0], dk_oth[1], dv_oth[1]), qkv_w, qkv_w2)
    dq, da_oth = lax.optimization_barrier((dq, da_oth))
    mid = own_rows // 2
    da_top = net.cross(da_oth[:mid])
    da_rest, da_top = lax.optimization_barrier((da_oth[mid:], da_top))
    da_rest = net.cross(da_rest)
    d_qkv, g_qkv, bias_rows = [None] * 2, [None] * 2, [None] * 2
    for i in (1, 0):
        d_qkv[i] = attn_bwd(
            meta_own,
            (qkv[i], 0),
            (ext[i], 0),
            (attn[i], 0),
            (d_heads[i], 0),
            (qkv[i], pairs),
            (qkv[i], 2 * pairs),
            pairs,
            dq[i],
        )
        if i == 0:
            d_qkv[0], oth = lax.optimization_barrier((d_qkv[0], oth))
        g_qkv[i], bias_rows[i] = qkv_grads(normed, normed_oth, *d_qkv[i], dk_oth[i], dv_oth[i])
        if i == 1:
            dq[0], g_qkv[1], da_top = lax.optimization_barrier((dq[0], g_qkv[1], da_top))
            oth, left = g_qkv[1].reshape(n_rows, -1, 3 * hw), list(range(net.bits))
            for step in EARLY:
                oth, left = net.halve(oth, left, step)
    own, left2 = g_qkv[0].reshape(n_rows, -1, 3 * hw), list(range(net.bits))
    own, left2 = net.halve(own, left2, 0)
    d_tokens, sums_t = ln1_bwd([*d_qkv[0], *d_qkv[1]], qkv_w, qkv_w2, (da_top, da_rest), d_hidden, tokens, vecs)
    while left:
        oth, left = net.halve(oth, left, left[0])
    oth = net.cross(oth.reshape(-1, 3 * hw).astype(bf16)).astype(f32)
    n_lead = lead_table.shape[0]
    split = sums_m[16:24] + jnp.where(at == 2, bias_rows[0], 0.0) + jnp.where(at == 6, bias_rows[1], 0.0)
    crossed = sums_m[24:] + jnp.where(at == 6, bias_rows[0], 0.0) + jnp.where(at == 2, bias_rows[1], 0.0)
    slots = jnp.where(at == (net.row & 7), sums_t[2:3], 0.0)
    alike = [sums_t + sums_m[:8], sums_m[8:16]]
    late = jnp.concatenate(alike + [split, slots]) + net.cross(jnp.concatenate(alike + [crossed, slots]))

    def spread(v, step):
        got = net.flip(v, step)
        if step < 3:
            return v + got
        mine, theirs, low = v[24:], got[24:], net.bit(step) == 0
        return jnp.concatenate([v[:24] + got[:24], jnp.where(low, mine, theirs), jnp.where(low, theirs, mine)])

    crossing = net.cross(jnp.concatenate([grads[:, 2 * ff : 4 * ff], grads[:, 4 * ff + hw :]], axis=1))
    waiting = list(range(net.bits))
    while left2:
        for step in waiting[:2] if len(left2) == net.bits - 1 else waiting[:1]:
            late = spread(late, step)
            waiting.remove(step)
        own, left2 = net.halve(own, left2, left2[0])
        if len(left2) == net.bits - 3:
            own, late, crossing = lax.optimization_barrier((own, late, crossing))
        else:
            own, late = lax.optimization_barrier((own, late))
    for step in waiting:
        late = spread(late, step)
    g_qkv_sum = own.reshape(-1, 3 * hw) + oth
    leads = gathered_lead.astype(jnp.int32)
    chosen = (lax.broadcasted_iota(jnp.int32, (n_lead, n_rows), 0) == leads[None, :]).astype(f32)
    d_table = jnp.dot(chosen, late[24:], precision=lax.Precision.HIGHEST)
    split = late[16:24]
    penalty = late[7, 0] / count_total
    d_bias_qv, d_bias_up_own = split[2], split[: ff // width].reshape(-1)
    grads = jnp.concatenate([grads[:, : 2 * ff], grads[:, 4 * ff : 4 * ff + hw]], axis=1).astype(f32) + crossing.astype(f32)
    blocks = [grads[:, k * FF_BLOCK : (k + 1) * FF_BLOCK] for k in range(2 * ff // FF_BLOCK)]
    g_down = jnp.concatenate(blocks[0::2], axis=1)
    g_up = jnp.concatenate(blocks[1::2], axis=1)
    g_out = grads[:, 2 * ff :]
    return (
        block_out,
        penalty,
        d_tokens,
        d_table,
        late[0],
        late[1],
        g_qkv_sum[:, :hw],
        g_qkv_sum[:, hw : 2 * hw],
        g_qkv_sum[:, 2 * hw :],
        d_bias_qv[:hw],
        d_bias_qv[hw:],
        g_out.T,
        late[10],
        late[8],
        late[9],
        g_up,
        d_bias_up_own,
        g_down.T,
        late[6],
        late[3:6].T,
    )


def solution(mesh):
    in_specs = (
        P(("rows", "heads"), None),
        P("rows"),
        P("rows"),
        P(("rows", "heads")),
        P(),
        P(),
        P(),
        P(None, "heads"),
        P(None, "heads"),
        P(None, "heads"),
        P("heads"),
        P("heads"),
        P("heads", None),
        P(),
        P(),
        P(),
        P(None, "heads"),
        P("heads"),
        P("heads", None),
        P(),
        P(),
        P(("rows", "heads"), None),
    )
    out_specs = (
        P(("rows", "heads"), None),
        P(),
        P(("rows", "heads"), None),
        P(),
        P(),
        P(),
        P("rows", "heads"),
        P("rows", "heads"),
        P("rows", "heads"),
        P("heads"),
        P("heads"),
        P("heads", "rows"),
        P(),
        P(),
        P(),
        P("rows", "heads"),
        P("heads"),
        P("heads", "rows"),
        P(),
        P(),
    )
    return jax.shard_map(
        functools.partial(per_device, mesh.shape["rows"]),
        mesh=mesh,
        in_specs=in_specs,
        out_specs=out_specs,
        check_vma=False,
    )
```

```python
import functools

import jax
import jax.numpy as jnp
from jax import lax
from jax.experimental import pallas as pl
from jax.experimental.pallas import tpu as pltpu
from jax.sharding import PartitionSpec as P

HEAD_DIM = 64
PAIR = 2 * HEAD_DIM
NEG = -1e30
SCALE = HEAD_DIM ** (-0.5)
entropy_weight = 16.0
f32 = jnp.float32
bf16 = jnp.bfloat16
NT = (((1,), (1,)), ((), ()))
TN = (((0,), (0,)), ((), ()))
NN = (((1,), (0,)), ((), ()))
VMEM_LIMIT = 56 << 20
COST_SHARE = 20
MID_LIMIT = 62 << 20


def cost(flops, size):
    return pl.CostEstimate(flops=flops // COST_SHARE, transcendentals=0, bytes_accessed=size // COST_SHARE)


def mm(a, b, dims=NN):
    return lax.dot_general(a, b, dims, preferred_element_type=f32)


def layer_norm(values, gain, shift):
    centre = values - jnp.mean(values, axis=-1, keepdims=True)
    spread = jnp.mean(centre * centre, axis=-1, keepdims=True)
    return centre * lax.rsqrt(spread + 1e-05) * gain + shift


def gelu_exact(values):
    return jax.nn.gelu(values, approximate=False)


def split3(x):
    hi = x.astype(bf16).astype(f32)
    mid = (x - hi).astype(bf16).astype(f32)
    return hi, mid, x - hi - mid


def pair_masks():
    lane = lax.broadcasted_iota(jnp.int32, (1, PAIR), 1)
    return lane, (lane < HEAD_DIM, lane >= HEAD_DIM), (HEAD_DIM, 0)


def own_part(h):
    return slice(0, HEAD_DIM) if h == 0 else slice(HEAD_DIM, PAIR)


def key_bias(meta, keys):
    kpos = meta[0] + lax.broadcasted_iota(jnp.int32, (keys, 1), 0)
    return jnp.where(kpos < meta[1], 0.0, NEG)


def attn_fwd_kernel(first, qb, kc, meta, q_ref, k_ref, v_ref, *refs):
    if first:
        acc_ref, ml_ref, st_sc, p_sc = refs
    else:
        acc_in, ml_in, o_ref, e_ref, acc_sc, e_sc, st_sc, p_sc = refs
    rows = q_ref.shape[0]
    keys = k_ref.shape[0]
    lane, inside, free = pair_masks()
    bias = key_bias(meta, keys)
    q32 = q_ref[...].astype(f32) * SCALE
    k32 = k_ref[...].astype(f32)
    v32 = v_ref[...].astype(f32)
    qx = [jnp.where(inside[h], q32, jnp.where(lane == free[h], 1.0, 0.0)).astype(bf16) for h in range(2)]
    kx = [jnp.where(inside[h], k32, bias).astype(bf16) for h in range(2)]
    vx = [jnp.where(inside[h], v32, 1.0).astype(bf16) for h in range(2)]
    units = [(h, b) for h in range(2) for b in range(rows // qb)]
    chunks = [slice(c * kc, (c + 1) * kc) for c in range(keys // kc)]
    m_prev = None
    for u in range(len(units) + 1):
        slot, prev = u % 2, (u - 1) % 2
        if u < len(units):
            h, b = units[u]
            cols = slice(b * qb, (b + 1) * qb)
        m8 = None
        for ch in chunks:
            if u < len(units):
                st = mm(kx[h][ch], qx[h][cols], NT)
                st_sc[slot, ch, :] = st
                top = jnp.max(st.reshape(kc // 8, 8, qb), axis=0)
                m8 = top if m8 is None else jnp.maximum(m8, top)
            if u > 0:
                p_sc[prev, ch, :] = jnp.exp(st_sc[prev, ch, :] - m_prev).astype(bf16)
        if u > 0:
            hp, bp = units[u - 1]
            pc = slice(bp * qb, (bp + 1) * qb)
            ot = mm(vx[hp], p_sc[prev], TN)
            fe = free[hp]
            own = own_part(hp)
            total = ot[fe : fe + 1]
            num = ot[own]
            if first:
                acc_ref[own, pc] = num
                ml_ref[hp : hp + 1, pc] = m_prev
                ml_ref[2 + hp : 3 + hp, pc] = total
            else:
                alpha = jnp.exp(ml_in[hp : hp + 1, pc] - m_prev)
                total = total + alpha * ml_in[2 + hp : 3 + hp, pc]
                num = num + alpha * acc_in[own, pc]
                acc_sc[own, pc] = num / total
                hi, mid, lo = split3(m_prev + jnp.log(total))
                row = lax.broadcasted_iota(jnp.int32, (HEAD_DIM, 1), 0)
                e_sc[fe : fe + HEAD_DIM, pc] = jnp.where(
                    row == 0, 1.0, jnp.where(row == 1, -hi, jnp.where(row == 2, -mid, jnp.where(row == 3, -lo, 0.0)))
                )
        if u < len(units):
            m_prev = jnp.max(m8, axis=0, keepdims=True)
            if not first:
                m_prev = jnp.maximum(m_prev, ml_in[h : h + 1, cols])
    if not first:
        o_ref[...] = acc_sc[...].T.astype(bf16)
        e_ref[...] = e_sc[...].T.astype(bf16)


def attn_fwd(meta, q, k, v, pairs, state=None, qb=1024, kc=256):
    rows = q[0].shape[0]
    keys = k[0].shape[0]
    width = pairs * PAIR
    first = state is None

    def col(off):
        return lambda i, m: (0, off + i)

    def down(i, m):
        return (i, 0)

    in_specs = [
        pl.BlockSpec((rows, PAIR), col(q[1])),
        pl.BlockSpec((keys, PAIR), col(k[1])),
        pl.BlockSpec((keys, PAIR), col(v[1])),
    ]
    scratch = [pltpu.VMEM((2, keys, qb), f32), pltpu.VMEM((2, keys, qb), bf16)]
    args = (q[0], k[0], v[0])
    if first:
        out_shape = (jax.ShapeDtypeStruct((width, rows), f32), jax.ShapeDtypeStruct((8 * pairs, rows), f32))
        out_specs = (pl.BlockSpec((PAIR, rows), down), pl.BlockSpec((8, rows), down))
    else:
        in_specs += [pl.BlockSpec((PAIR, rows), down), pl.BlockSpec((8, rows), down)]
        out_shape = (jax.ShapeDtypeStruct((rows, width), bf16), jax.ShapeDtypeStruct((rows, width), bf16))
        out_specs = (pl.BlockSpec((rows, PAIR), col(0)), pl.BlockSpec((rows, PAIR), col(0)))
        scratch = [pltpu.VMEM((PAIR, rows), f32), pltpu.VMEM((PAIR, rows), f32)] + scratch
        args = args + tuple(state)
    return pl.pallas_call(
        functools.partial(attn_fwd_kernel, first, qb, kc),
        grid_spec=pltpu.PrefetchScalarGridSpec(
            num_scalar_prefetch=1, grid=(pairs,), in_specs=in_specs, out_specs=out_specs, scratch_shapes=scratch
        ),
        out_shape=out_shape,
        compiler_params=pltpu.CompilerParams(vmem_limit_bytes=VMEM_LIMIT),
        cost_estimate=cost(16 * rows * keys * width, 8 * rows * width),
        name="attn_fwd_first" if first else "attn_fwd_second",
    )(meta, *args)


def attn_bwd_kernel(first, qb, kc, meta, q_ref, e_ref, o_ref, do_ref, k_ref, v_ref, *refs):
    if first:
        dq_ref, dk_ref, dv_ref, dk_sc, dv_sc, s_sc, dp_sc, p_sc, ds_sc = refs
    else:
        dq_in, dq_ref, dk_ref, dv_ref, dk_sc, dv_sc, s_sc, dp_sc, p_sc, ds_sc = refs
    rows = q_ref.shape[0]
    keys = k_ref.shape[0]
    lane, inside, free = pair_masks()
    bias = key_bias(meta, keys)
    k32 = k_ref[...].astype(f32)
    v32 = v_ref[...].astype(f32)
    kx = [jnp.where(inside[h], k32, jnp.where(lane == free[h], bias, 1.0)).astype(bf16) for h in range(2)]
    vx = [jnp.where(inside[h], v32, 1.0).astype(bf16) for h in range(2)]
    units = [(b, h) for b in range(rows // qb) for h in range(2)]
    chunks = [slice(c * kc, (c + 1) * kc) for c in range(keys // kc)]
    prep = None
    dq0 = None
    for u in range(len(units) + 1):
        before = prep
        slot, prev = u % 2, (u - 1) % 2
        if u < len(units):
            b, h = units[u]
            rs = slice(b * qb, (b + 1) * qb)
            fe = free[h]
            if h == 0:
                q32 = q_ref[rs].astype(f32) * SCALE
                do32 = do_ref[rs].astype(f32)
                e32 = e_ref[rs].astype(f32)
                prod = do32 * o_ref[rs].astype(f32)
            hi, mid, lo = split3(jnp.sum(jnp.where(inside[h], prod, 0.0), axis=1, keepdims=True))
            dext = jnp.where(lane == fe, -hi, jnp.where(lane == fe + 1, -mid, jnp.where(lane == fe + 2, -lo, 0.0)))
            qx = jnp.where(inside[h], q32, e32).astype(bf16)
            dox = jnp.where(inside[h], do32, dext).astype(bf16)
            prep = (qx, dox)
        for ch in chunks:
            if u < len(units):
                s_sc[slot, :, ch] = mm(qx, kx[h][ch], NT)
                dp_sc[slot, :, ch] = mm(dox, vx[h][ch], NT)
            if u > 0:
                p = jnp.exp(s_sc[prev, :, ch])
                p_sc[prev, :, ch] = p.astype(bf16)
                ds_sc[prev, :, ch] = (p * dp_sc[prev, :, ch]).astype(bf16)
        if u > 0:
            bp, hp = units[u - 1]
            rp = slice(bp * qb, (bp + 1) * qb)
            qxp, doxp = before
            dvt = mm(doxp, p_sc[prev], TN)
            dkt = mm(qxp, ds_sc[prev], TN)
            dqh = mm(ds_sc[prev], kx[hp], NN)
            own = own_part(hp)
            if bp == 0:
                dv_sc[own] = dvt[own]
                dk_sc[own] = dkt[own]
            else:
                dv_sc[own] += dvt[own]
                dk_sc[own] += dkt[own]
            if hp == 0:
                dq0 = dqh
            else:
                dq = jnp.where(lane < HEAD_DIM, dq0, dqh) * SCALE
                if first:
                    dq_ref[rp] = dq
                else:
                    dq_ref[rp] = (dq + dq_in[rp]).astype(bf16)
    dk_ref[...] = dk_sc[...].T.astype(bf16)
    dv_ref[...] = dv_sc[...].T.astype(bf16)


def attn_bwd(meta, q, e, o, do, k, v, pairs, dq_prev=None, qb=256, kc=256):
    rows = q[0].shape[0]
    keys = k[0].shape[0]
    width = pairs * PAIR
    first = dq_prev is None

    def col(off):
        return lambda i, m: (0, off + i)

    in_specs = [pl.BlockSpec((rows, PAIR), col(off)) for _, off in (q, e, o, do)]
    in_specs += [pl.BlockSpec((keys, PAIR), col(off)) for _, off in (k, v)]
    args = (q[0], e[0], o[0], do[0], k[0], v[0])
    rspec = pl.BlockSpec((rows, PAIR), col(0))
    kspec = pl.BlockSpec((keys, PAIR), col(0))
    if not first:
        in_specs.append(rspec)
        args = args + (dq_prev,)
    return pl.pallas_call(
        functools.partial(attn_bwd_kernel, first, qb, kc),
        grid_spec=pltpu.PrefetchScalarGridSpec(
            num_scalar_prefetch=1,
            grid=(pairs,),
            in_specs=in_specs,
            out_specs=(rspec, kspec, kspec),
            scratch_shapes=[pltpu.VMEM((PAIR, keys), f32)] * 2
            + [pltpu.VMEM((2, qb, keys), f32)] * 2
            + [pltpu.VMEM((2, qb, keys), bf16)] * 2,
        ),
        out_shape=(
            jax.ShapeDtypeStruct((rows, width), f32 if first else bf16),
            jax.ShapeDtypeStruct((keys, width), bf16),
            jax.ShapeDtypeStruct((keys, width), bf16),
        ),
        compiler_params=pltpu.CompilerParams(vmem_limit_bytes=VMEM_LIMIT),
        cost_estimate=cost(40 * rows * keys * width, 16 * rows * width),
        name="attn_bwd_first" if first else "attn_bwd_second",
    )(meta, *args)


FF_BLOCK = 768
EARLY = (0, 1)
CHUNK = 256


def row_chunks(rows):
    return [slice(c, c + CHUNK) for c in range(0, rows, CHUNK)]


EMB, B_OUT, GAIN_2, SHIFT_2, B_DOWN, GAIN_1, SHIFT_1 = (slice(i, i + 1) for i in range(7))


def normalise(values):
    centre = values - jnp.mean(values, axis=-1, keepdims=True)
    spread = jnp.mean(centre * centre, axis=-1, keepdims=True)
    rstd = lax.rsqrt(spread + 1e-05)
    return centre * rstd, rstd


def gelu_pair(u):
    cdf = 0.5 * (1.0 + lax.erf(u * 0.7071067811865476))
    density = 0.3989422804014327 * jnp.exp(-0.5 * u * u)
    return u * cdf, cdf + u * density


def pick(step, n_own, own, other):
    return jnp.where(step < n_own, own, other)


def mid_kernel(
    n_own, scal, tok_ref, vec_ref, o0_ref, o1_ref, wo_ref, wo2_ref, bup_ref, up_ref, up2_ref, down_ref, down2_ref, wg_ref,
    cnt_ref, cot_ref, out_ref, grads_ref, dh_ref, da_ref, sums_ref, acc, h1_sc, nt_sc, dm_sc, g_sc, gp_sc,
):
    step = pl.program_id(0)
    n_blocks = 2 * n_own
    rows, width = tok_ref.shape
    chunks = row_chunks(rows)

    @pl.when(step == 0)
    def _():
        sums_ref[...] = jnp.zeros_like(sums_ref)
        wo2 = wo2_ref[...].reshape(wo_ref.shape)
        for c in chunks:
            h1 = tok_ref[c].astype(f32) + vec_ref[EMB]
            h1 = h1 + (mm(o0_ref[c], wo_ref[...]) + mm(o1_ref[c], wo2) + vec_ref[B_OUT])
            h1_sc[c] = h1
            xhat, _ = normalise(h1)
            nt_sc[c] = (xhat * vec_ref[GAIN_2] + vec_ref[SHIFT_2]).astype(bf16)
            acc[c] = h1 + vec_ref[B_DOWN]

    @pl.when(step < n_blocks)
    def _():
        up = pick(step, n_own, up_ref[...], up2_ref[...].reshape(up_ref.shape))
        down = pick(step, n_own, down_ref[...], down2_ref[...].reshape(down_ref.shape))
        u = mm(nt_sc[chunks[0]], up)
        for i, c in enumerate(chunks):
            ahead = mm(nt_sc[chunks[i + 1]], up) if i + 1 < len(chunks) else None
            g, gp = gelu_pair(u + bup_ref[...])
            g = g.astype(bf16)
            g_sc[step, c] = g
            gp_sc[step, c] = gp.astype(bf16)
            acc[c] += mm(g, down)
            u = ahead

    @pl.when(step == n_blocks - 1)
    def _():
        dbd = jnp.zeros((1, width), f32)
        dwg = [jnp.zeros((1, width), f32) for _ in range(3)]
        ent_sum = jnp.zeros((1, 1), f32)
        for c in chunks:
            out = acc[c]
            out_ref[c] = out.astype(bf16)
            z = [jnp.sum(out * wg_ref[e : e + 1], axis=-1, keepdims=True) for e in range(3)]
            top = jnp.maximum(jnp.maximum(z[0], z[1]), z[2])
            log_sum = jnp.log(sum(jnp.exp(v - top) for v in z)) + top
            logp = [v - log_sum for v in z]
            prob = [jnp.exp(v) for v in logp]
            entropy = -sum(p * q for p, q in zip(prob, logp))
            mean = sum(p * v for p, v in zip(prob, z))
            counted = cnt_ref[c]
            ent_sum = ent_sum + jnp.sum(counted * entropy, axis=0, keepdims=True)
            dz = [scal[0] * counted * (-p * (v - mean)) for p, v in zip(prob, z)]
            d_out = cot_ref[c].astype(f32) + sum(d * wg_ref[e : e + 1] for e, d in enumerate(dz))
            dm = d_out.astype(bf16)
            dm_sc[c] = dm
            dbd = dbd + jnp.sum(dm.astype(f32), axis=0, keepdims=True)
            dwg = [w + jnp.sum(out * d, axis=0, keepdims=True) for w, d in zip(dwg, dz)]
            acc[c] = d_out
            dh_ref[c] = jnp.zeros_like(d_out)
        for e in range(3):
            sums_ref[3 + e : 4 + e] = dwg[e]
        sums_ref[6:7] = dbd
        sums_ref[7:8] = jnp.broadcast_to(ent_sum, (1, width))

    @pl.when(step >= n_blocks)
    def _():
        j = step - n_blocks
        up = pick(j, n_own, up_ref[...], up2_ref[...].reshape(up_ref.shape))
        down = pick(j, n_own, down_ref[...], down2_ref[...].reshape(down_ref.shape))
        bias = jnp.zeros((1, FF_BLOCK), f32)
        for c in chunks:
            du = (mm(dm_sc[c], down, NT) * gp_sc[j, c].astype(f32)).astype(bf16)
            gp_sc[j, c] = du
            bias = bias + jnp.sum(du.astype(f32), axis=0, keepdims=True)
            dh_ref[c] += mm(du, up, NT)
        sums_ref[pl.ds(16 + 4 * (j // n_own) + j % n_own, 1)] = bias
        sums_ref[pl.ds(28 - 4 * (j // n_own) + j % n_own, 1)] = bias
        grads_ref[:, :FF_BLOCK] = mm(dm_sc[...], g_sc[j], TN).astype(bf16)
        grads_ref[:, FF_BLOCK:] = mm(nt_sc[...], gp_sc[j], TN).astype(bf16)

    @pl.when(step == 2 * n_blocks - 1)
    def _():
        d_gain = jnp.zeros((1, width), f32)
        d_shift = jnp.zeros((1, width), f32)
        d_bias = jnp.zeros((1, width), f32)
        for c in chunks:
            db = dh_ref[c]
            xhat, rstd = normalise(h1_sc[c])
            d_gain = d_gain + jnp.sum(db * xhat, axis=0, keepdims=True)
            d_shift = d_shift + jnp.sum(db, axis=0, keepdims=True)
            dx = db * vec_ref[GAIN_2]
            low = jnp.mean(dx, axis=-1, keepdims=True)
            slope = jnp.mean(dx * xhat, axis=-1, keepdims=True)
            dh = acc[c] + rstd * (dx - low - xhat * slope)
            dh_ref[c] = dh
            da = dh.astype(bf16)
            da_ref[c] = da
            d_bias = d_bias + jnp.sum(da.astype(f32), axis=0, keepdims=True)
        sums_ref[8:9] = d_gain
        sums_ref[9:10] = d_shift
        sums_ref[10:11] = d_bias


def fixed(shape, **mode):
    zeros = (0,) * len(shape)
    return pl.BlockSpec(shape, lambda *_: zeros, **mode)


def weight_specs(gathered, width, ff):
    n_own = ff // FF_BLOCK
    parts, _, _ = gathered.shape
    k_up, k_down = width // parts, ff // parts
    per_step = FF_BLOCK // k_down
    cols = width // FF_BLOCK

    n_blocks = 2 * n_own

    def own(j):
        return jnp.minimum(lax.rem(j, n_blocks), n_own - 1)

    def other(j):
        return jnp.maximum(lax.rem(j, n_blocks) - n_own, 0)

    return n_own, [
        pl.BlockSpec((width, FF_BLOCK), lambda j, *_: (0, own(j))),
        pl.BlockSpec((parts, k_up, FF_BLOCK), lambda j, *_: (0, other(j) // cols, other(j) % cols)),
        pl.BlockSpec((FF_BLOCK, width), lambda j, *_: (own(j), 0)),
        pl.BlockSpec((per_step, k_down, width), lambda j, *_: (other(j), 2 * k_up // k_down, 0)),
    ]


def out_spec(gathered, width, ff, hw):
    parts = gathered.shape[0]
    k_out = hw // parts
    return pl.BlockSpec((parts, k_out, width), lambda *_: (0, (2 * width + ff) // parts // k_out, 0))


def feed_forward(scal, tokens, vecs, o0, o1, w_out, gathered, b_up, w_up, w_down, wg, counted, cot, grad_cols):
    rows, width = tokens.shape
    ff = w_down.shape[0]
    n_own, (up_s, up2_s, down_s, down2_s) = weight_specs(gathered, width, ff)
    n_blocks = 2 * n_own
    hw = w_out.shape[0]
    once = {"pipeline_mode": pl.Buffered(1)}
    wo2_s = out_spec(gathered, width, ff, hw)
    return pl.pallas_call(
        functools.partial(mid_kernel, n_own),
        grid_spec=pltpu.PrefetchScalarGridSpec(
            num_scalar_prefetch=1,
            grid=(2 * n_blocks,),
            in_specs=[
                fixed((rows, width), **once),
                fixed((8, width)),
                fixed((rows, hw), **once),
                fixed((rows, hw), **once),
                fixed((hw, width), **once),
                pl.BlockSpec(wo2_s.block_shape, wo2_s.index_map, **once),
                pl.BlockSpec((1, FF_BLOCK), lambda j, *_: (0, lax.rem(j, n_blocks))),
                up_s,
                up2_s,
                down_s,
                down2_s,
                fixed((8, width)),
                fixed((rows, 1), **once),
                fixed((rows, width), **once),
            ],
            out_specs=[
                fixed((rows, width)),
                pl.BlockSpec((width, 2 * FF_BLOCK), lambda j, *_: (0, jnp.maximum(j - n_blocks, 0))),
                fixed((rows, width)),
                fixed((rows, width)),
                fixed((32, width)),
            ],
            scratch_shapes=[
                pltpu.VMEM((rows, width), f32),
                pltpu.VMEM((rows, width), f32),
                pltpu.VMEM((rows, width), bf16),
                pltpu.VMEM((rows, width), bf16),
                pltpu.VMEM((n_blocks, rows, FF_BLOCK), bf16),
                pltpu.VMEM((n_blocks, rows, FF_BLOCK), bf16),
            ],
        ),
        out_shape=[
            jax.ShapeDtypeStruct((rows, width), bf16),
            jax.ShapeDtypeStruct((width, grad_cols), bf16),
            jax.ShapeDtypeStruct((rows, width), f32),
            jax.ShapeDtypeStruct((rows, width), bf16),
            jax.ShapeDtypeStruct((32, width), f32),
        ],
        compiler_params=pltpu.CompilerParams(vmem_limit_bytes=MID_LIMIT),
        cost_estimate=cost(36 * rows * width * ff, 40 * rows * width),
        name="mid",
    )(scal, tokens, vecs, o0, o1, w_out, gathered, b_up, w_up, gathered, w_down, gathered, wg, counted, cot)


def out_bwd_kernel(da_ref, o0_ref, o1_ref, wo_ref, wo2_ref, _, do_ref, do2_ref, grads_ref):
    hw = wo_ref.shape[0]
    do_ref[...] = mm(da_ref[...], wo_ref[...], NT).astype(bf16)
    do2_ref[...] = mm(da_ref[...], wo2_ref[...].reshape(wo_ref.shape), NT).astype(bf16)
    grads_ref[:, :hw] = mm(da_ref[...], o0_ref[...], TN).astype(bf16)
    grads_ref[:, hw:] = mm(da_ref[...], o1_ref[...], TN).astype(bf16)


def out_bwd(d_attn, o0, o1, w_out, gathered, ff, grads):
    rows, width = d_attn.shape
    hw = w_out.shape[0]
    half = fixed((rows, hw))
    return pl.pallas_call(
        out_bwd_kernel,
        grid=(1,),
        in_specs=[
            fixed((rows, width)), half, half, fixed((hw, width)), out_spec(gathered, width, ff, hw),
            pl.BlockSpec(memory_space=pl.ANY),
        ],
        out_specs=[half, half, pl.BlockSpec((width, 2 * hw), lambda j: (0, grads.shape[1] // (2 * hw) - 1))],
        out_shape=[
            jax.ShapeDtypeStruct((rows, hw), bf16),
            jax.ShapeDtypeStruct((rows, hw), bf16),
            jax.ShapeDtypeStruct(grads.shape, bf16),
        ],
        input_output_aliases={5: 2},
        compiler_params=pltpu.CompilerParams(vmem_limit_bytes=VMEM_LIMIT),
        cost_estimate=cost(8 * rows * width * hw, 12 * rows * width),
        name="out_bwd",
    )(d_attn, o0, o1, w_out, gathered, grads)


def qkv_grads_kernel(n_ref, no_ref, dq_ref, dk_ref, dv_ref, dko_ref, dvo_ref, grads_ref, sums_ref):
    hw = dq_ref.shape[1]
    grads_ref[:, :hw] = mm(n_ref[...], dq_ref[...], TN).astype(bf16)
    kv = jnp.concatenate([dk_ref[...], dv_ref[...]], axis=1)
    kvo = jnp.concatenate([dko_ref[...], dvo_ref[...]], axis=1)
    grads_ref[:, hw:] = (mm(n_ref[...], kv, TN) + mm(no_ref[...], kvo, TN)).astype(bf16)
    bq = jnp.sum(dq_ref[...].astype(f32), axis=0, keepdims=True)
    bv = jnp.sum(dv_ref[...].astype(f32), axis=0, keepdims=True) + jnp.sum(dvo_ref[...].astype(f32), axis=0, keepdims=True)
    sums_ref[:, :hw] = jnp.broadcast_to(bq, (8, hw))
    sums_ref[:, hw:] = jnp.broadcast_to(bv, (8, hw))


def qkv_grads(normed, normed_oth, dq, dk, dv, dk_oth, dv_oth):
    rows, width = normed.shape
    hw = dq.shape[1]
    full, half = fixed((rows, width)), fixed((rows, hw))
    return pl.pallas_call(
        qkv_grads_kernel,
        grid=(1,),
        in_specs=[full, full] + [half] * 5,
        out_specs=[fixed((width, 3 * hw)), fixed((8, 2 * hw))],
        out_shape=[jax.ShapeDtypeStruct((width, 3 * hw), bf16), jax.ShapeDtypeStruct((8, 2 * hw), f32)],
        compiler_params=pltpu.CompilerParams(vmem_limit_bytes=VMEM_LIMIT),
        cost_estimate=cost(10 * rows * width * hw, 10 * rows * width),
        name="qkv_grads",
    )(normed, normed_oth, dq, dk, dv, dk_oth, dv_oth)


def ln1_bwd_kernel(n_parts, *refs):
    parts, (w0_ref, w1_ref, got0_ref, got1_ref, dh_ref, tok_ref, vec_ref, dtok_ref, sums_ref) = refs[:n_parts], refs[n_parts:]
    upper = pl.program_id(0) < pl.num_programs(0) // 2
    da = jnp.where(upper, got0_ref[...], got1_ref[...]).astype(f32)
    for i, w_ref in enumerate((w0_ref, w1_ref)):
        joined = jnp.concatenate([part[...] for part in parts[3 * i : 3 * i + 3]], axis=1)
        da = da + mm(joined, w_ref[...], NT)
    xhat, rstd = normalise(tok_ref[...].astype(f32) + vec_ref[EMB])
    dx = da * vec_ref[GAIN_1]
    low = jnp.mean(dx, axis=-1, keepdims=True)
    slope = jnp.mean(dx * xhat, axis=-1, keepdims=True)
    d_tokens = dh_ref[...] + rstd * (dx - low - xhat * slope)
    dtok_ref[...] = d_tokens
    new = [jnp.sum(v, axis=0, keepdims=True) for v in (da * xhat, da, d_tokens)]

    @pl.when(pl.program_id(0) == 0)
    def _():
        sums_ref[...] = jnp.zeros_like(sums_ref)

    for i, v in enumerate(new):
        sums_ref[i : i + 1] += v


def ln1_bwd(d_qkv, w0, w1, da_got, d_hidden, tokens, vecs):
    rows, width = tokens.shape
    hw = d_qkv[0].shape[1]
    step = CHUNK
    n_half = rows // step // 2
    blk = pl.BlockSpec((step, width), lambda i: (i, 0))
    half = pl.BlockSpec((step, hw), lambda i: (i, 0))
    return pl.pallas_call(
        functools.partial(ln1_bwd_kernel, len(d_qkv)),
        grid=(rows // step,),
        in_specs=[half] * len(d_qkv) + [fixed((width, 3 * hw))] * 2
        + [
            pl.BlockSpec((step, width), lambda i: (jnp.minimum(i, n_half - 1), 0)),
            pl.BlockSpec((step, width), lambda i: (jnp.maximum(i - n_half, 0), 0)),
            blk,
            blk,
            fixed((8, width)),
        ],
        out_specs=[blk, fixed((8, width))],
        out_shape=[jax.ShapeDtypeStruct((rows, width), f32), jax.ShapeDtypeStruct((8, width), f32)],
        compiler_params=pltpu.CompilerParams(vmem_limit_bytes=VMEM_LIMIT),
        cost_estimate=cost(12 * rows * width * hw, 20 * rows * width),
        name="ln1_bwd",
    )(*d_qkv, w0, w1, *da_got, d_hidden, tokens, vecs)


def oth_bwd_kernel(k0_ref, v0_ref, k1_ref, v1_ref, w0_ref, w1_ref, da_ref):
    hw = k0_ref.shape[1]
    da = mm(jnp.concatenate([k0_ref[...], v0_ref[...]], axis=1), w0_ref[:, hw:], NT)
    da_ref[...] = (da + mm(jnp.concatenate([k1_ref[...], v1_ref[...]], axis=1), w1_ref[:, hw:], NT)).astype(bf16)


def oth_bwd(d_kv, w0, w1):
    rows, hw = d_kv[0].shape
    width = w0.shape[0]
    step = 2 * CHUNK
    half = pl.BlockSpec((step, hw), lambda i: (i, 0))
    return pl.pallas_call(
        oth_bwd_kernel,
        grid=(rows // step,),
        in_specs=[half] * 4 + [fixed(w0.shape)] * 2,
        out_specs=pl.BlockSpec((step, width), lambda i: (i, 0)),
        out_shape=jax.ShapeDtypeStruct((rows, width), bf16),
        compiler_params=pltpu.CompilerParams(vmem_limit_bytes=VMEM_LIMIT),
        cost_estimate=cost(8 * rows * width * hw, 4 * rows * width),
        name="oth_bwd",
    )(*d_kv, w0, w1)


def front_kernel(starts, tok_ref, vec_ref, *refs):
    n = len(starts)
    xhat, _ = normalise(tok_ref[...].astype(f32) + vec_ref[EMB])
    normed = (xhat * vec_ref[GAIN_1] + vec_ref[SHIFT_1]).astype(bf16)
    refs[2 * n][...] = normed
    for i, start in enumerate(starts):
        y = mm(normed, refs[2 * i][:, start:]) + refs[2 * i + 1][:, start:]
        refs[2 * n + 1 + i][...] = y.astype(bf16)


def front(tokens, vecs, weights):
    rows, width = tokens.shape
    step = CHUNK
    in_specs = [pl.BlockSpec((step, width), lambda i: (i, 0)), fixed((8, width))]
    args = [tokens, vecs]
    outs = [width]
    for w, b, start in weights:
        in_specs += [fixed(w.shape), fixed(b.shape)]
        args += [w, b]
        outs.append(w.shape[1] - start)
    return pl.pallas_call(
        functools.partial(front_kernel, tuple(start for _, _, start in weights)),
        grid=(rows // step,),
        in_specs=in_specs,
        out_specs=[pl.BlockSpec((step, n), lambda i: (i, 0)) for n in outs],
        out_shape=[jax.ShapeDtypeStruct((rows, n), bf16) for n in outs],
        compiler_params=pltpu.CompilerParams(vmem_limit_bytes=VMEM_LIMIT),
        cost_estimate=cost(2 * rows * width * sum(outs[1:]), 8 * rows * width),
        name="front",
    )(*args)


def pack_kernel(row, up_ref, down_ref, out_ref, rest_ref, share_ref):
    width = share_ref.shape[1]
    at = 0
    for part in (up_ref[:, :width], up_ref[:, width:], down_ref[...], out_ref[...], rest_ref[...]):
        share_ref[at : at + part.shape[0]] = part
        at += part.shape[0]


def pack_share(row, n_rows, w_up, w_down, w_out, rest):
    width = w_out.shape[1]
    sizes = [w.shape[0] // n_rows for w in (w_up, w_down, w_out)]
    total = 2 * sizes[0] + sizes[1] + sizes[2] + rest.shape[0]
    if sizes[0] % 16:
        up, down, out = (lax.dynamic_slice_in_dim(w, row * k, k, 0) for w, k in zip((w_up, w_down, w_out), sizes))
        return jnp.concatenate([up[:, :width], up[:, width:], down, out, rest])
    return pl.pallas_call(
        pack_kernel,
        grid_spec=pltpu.PrefetchScalarGridSpec(
            num_scalar_prefetch=1,
            grid=(1,),
            in_specs=[pl.BlockSpec((k, w.shape[1]), lambda i, r: (r[0], 0)) for w, k in zip((w_up, w_down, w_out), sizes)]
            + [fixed(rest.shape)],
            out_specs=fixed((total, width)),
        ),
        out_shape=jax.ShapeDtypeStruct((total, width), bf16),
        name="pack_share",
    )(row.reshape(1), w_up, w_down, w_out, rest)


class Net:
    def __init__(self, n_rows):
        self.n_rows = n_rows
        self.bits = n_rows.bit_length() - 1
        self.row = lax.axis_index("rows")

    def cross(self, x):
        return lax.ppermute(x, "heads", [(0, 1), (1, 0)])

    def flip(self, x, bit):
        return lax.ppermute(x, "rows", [(i, i ^ (1 << bit)) for i in range(self.n_rows)])

    def bit(self, b):
        return (self.row >> b) & 1

    def fetch(self, own):
        part = own.shape[0] // 2
        return self.cross(lax.dynamic_slice_in_dim(own, self.bit(0) * part, part, 0))

    def join(self, got):
        passed = self.flip(got, 0)
        low = self.bit(0) == 0
        return jnp.concatenate([jnp.where(low, got, passed), jnp.where(low, passed, got)], axis=0)

    def halve(self, part, left, step):
        low = 1 << left.index(step)
        blocks, piece, cols = part.shape
        view = part.reshape(blocks // (2 * low), 2, low, piece, cols)
        at = self.bit(step)
        keep = lax.dynamic_index_in_dim(view, at, 1, keepdims=False)
        got = self.flip(lax.dynamic_index_in_dim(view, 1 - at, 1, keepdims=False).astype(bf16), step)
        return (keep.astype(f32) + got.astype(f32)).reshape(blocks // 2, piece, cols), [x for x in left if x != step]


def per_device(
    n_rows,
    tokens,
    crop_lengths,
    lead_index,
    valid_mask,
    lead_table,
    ln1_gain,
    ln1_shift,
    w_query,
    w_key,
    w_value,
    b_query,
    b_value,
    w_out,
    b_out,
    ln2_gain,
    ln2_shift,
    w_up,
    b_up,
    w_down,
    b_down,
    w_gater,
    cotangent,
):
    net = Net(n_rows)
    own_rows, width = tokens.shape
    half = lax.axis_index("heads")
    length = crop_lengths[0]
    hw = w_query.shape[1]
    pairs = hw // PAIR
    own_start = half * own_rows
    meta_own = jnp.stack([own_start, length])
    meta_oth = jnp.stack([own_rows - own_start, length])

    positions = own_start + jnp.arange(own_rows, dtype=jnp.int32)
    counted = ((positions < length) & (valid_mask == 1)).astype(f32)
    count = jnp.sum(counted)

    qkv_w = jnp.concatenate([w_query, w_key, w_value], axis=1)
    bias_own = jnp.concatenate([b_query, b_value, b_up]).reshape(1, -1)
    k_up, k_down, k_out = width // n_rows, w_down.shape[0] // n_rows, w_out.shape[0] // n_rows
    n_share = 2 * k_up + k_down + k_out
    pad = -n_share % 16 + 16
    n_bias = bias_own.size // width
    line = lax.broadcasted_iota(jnp.int32, (pad, width), 0)
    lane = lax.broadcasted_iota(jnp.int32, (pad, width), 1)
    high = jnp.floor(count / 32)
    tally = jnp.where(lane == 0, high, jnp.where(lane == 1, count - 32 * high, 0.0))
    tally = jnp.where(lane == 2, lead_index[0].astype(f32), tally).astype(bf16)
    rest = tally
    for i in range(n_bias):
        rest = jnp.where(line == 1 + i, bias_own[:, i * width : (i + 1) * width], rest)
    got = net.cross(pack_share(net.row, n_rows, w_up, w_down, w_out, rest))
    bias_oth = got[n_share + 1 : n_share + 1 + n_bias].reshape(1, -1)
    tokens_in, got = lax.optimization_barrier((tokens, got))
    share = jnp.concatenate([got, tally], axis=0)
    tokens_oth = net.cross(tokens)
    at = lax.broadcasted_iota(jnp.int32, (8, 1), 0)
    picked = jnp.arange(lead_table.shape[0], dtype=jnp.int32) == lead_index[0]
    embedding = jnp.sum(jnp.where(picked[:, None], lead_table, 0.0), axis=0)
    vecs = jnp.zeros((8, width), f32)
    for i, v in enumerate((embedding, b_out, ln2_gain, ln2_shift, b_down, ln1_gain, ln1_shift)):
        vecs = jnp.where(at == i, v, vecs)

    def qkv_bias(b):
        b = b.astype(f32)
        return jnp.concatenate([b[:, :hw], jnp.zeros((1, hw), f32), b[:, hw : 2 * hw]], axis=1)

    qkv_b = qkv_bias(bias_own)
    normed, qkv_own = front(tokens_in, vecs, [(qkv_w, qkv_b, 0)])
    gathered = lax.all_gather(share, "rows", axis=0, tiled=False)
    tally = gathered[:, n_share:, :2].astype(f32)
    gathered_lead = gathered[:, n_share + pad, 2]
    count_total = jnp.sum(tally[:, 0] * jnp.array([32.0, 1.0])) + jnp.sum(tally[:, pad] * jnp.array([32.0, 1.0]))
    if k_up % 16 or k_down % 16:
        sizes = (k_up, k_up, k_down, k_out)
        starts = (0, k_up, 2 * k_up, 2 * k_up + k_down)
        gathered = jnp.concatenate(
            [gathered[:, a : a + k].reshape(16, k * n_rows // 16, width) for a, k in zip(starts, sizes)], axis=1
        )

    qkv_b2 = qkv_bias(bias_oth)
    up_b, up_b2 = bias_own[:, 2 * hw :].astype(f32), bias_oth[:, 2 * hw :].astype(f32)

    state = attn_fwd(meta_own, (qkv_own, 0), (qkv_own, pairs), (qkv_own, 2 * pairs), pairs)
    tokens_oth, state, qkv_in = lax.optimization_barrier((tokens_oth, state, qkv_w))
    got_w = net.fetch(qkv_in)
    normed_oth, kv_own = front(tokens_oth, vecs, [(qkv_w, qkv_b, hw)])
    attn_own, ext_own = attn_fwd(meta_oth, (qkv_own, 0), (kv_own, 0), (kv_own, pairs), pairs, state)
    got_w, attn_own = lax.optimization_barrier((got_w, attn_own))
    qkv_w2 = net.join(got_w)
    qkv_two = (mm(normed, qkv_w2) + qkv_b2).astype(bf16)
    kv_two = (mm(normed_oth, qkv_w2[:, hw:]) + qkv_b2[:, hw:]).astype(bf16)
    state = attn_fwd(meta_own, (qkv_two, 0), (qkv_two, pairs), (qkv_two, 2 * pairs), pairs)
    attn_two, ext_two = attn_fwd(meta_oth, (qkv_two, 0), (kv_two, 0), (kv_two, pairs), pairs, state)
    qkv, kv_oth, attn, ext = (qkv_own, qkv_two), (kv_own, kv_two), (attn_own, attn_two), (ext_own, ext_two)

    ff = w_down.shape[0]
    block_out, grads, d_hidden, d_attn, sums_m = feed_forward(
        (entropy_weight / count_total).reshape(1),
        tokens,
        vecs,
        attn[0],
        attn[1],
        w_out,
        gathered,
        jnp.concatenate([up_b, up_b2], axis=1),
        w_up,
        w_down,
        jnp.concatenate([w_gater.T, jnp.zeros((5, width), f32)]),
        counted.reshape(-1, 1),
        cotangent,
        4 * ff + 2 * hw,
    )
    do_own, do_oth, grads = out_bwd(d_attn, attn[0], attn[1], w_out, gathered, ff, grads)
    d_heads = (do_own, do_oth)
    grads = lax.psum_scatter(grads, "rows", scatter_dimension=0, tiled=True)

    dq, dk_oth, dv_oth = [], [], []
    for i in range(2):
        a, b, c = attn_bwd(
            meta_oth, (qkv[i], 0), (ext[i], 0), (attn[i], 0), (d_heads[i], 0), (kv_oth[i], 0), (kv_oth[i], pairs), pairs
        )
        dq.append(a)
        dk_oth.append(b)
        dv_oth.append(c)
    da_oth = oth_bwd((dk_oth[0], dv_oth[0], dk_oth[1], dv_oth[1]), qkv_w, qkv_w2)
    dq, da_oth = lax.optimization_barrier((dq, da_oth))
    mid = own_rows // 2
    da_top = net.cross(da_oth[:mid])
    da_rest, da_top = lax.optimization_barrier((da_oth[mid:], da_top))
    da_rest = net.cross(da_rest)
    d_qkv, g_qkv, bias_rows = [None] * 2, [None] * 2, [None] * 2
    for i in (1, 0):
        d_qkv[i] = attn_bwd(
            meta_own,
            (qkv[i], 0),
            (ext[i], 0),
            (attn[i], 0),
            (d_heads[i], 0),
            (qkv[i], pairs),
            (qkv[i], 2 * pairs),
            pairs,
            dq[i],
        )
        if i == 0:
            d_qkv[0], oth = lax.optimization_barrier((d_qkv[0], oth))
        g_qkv[i], bias_rows[i] = qkv_grads(normed, normed_oth, *d_qkv[i], dk_oth[i], dv_oth[i])
        if i == 1:
            dq[0], g_qkv[1], da_top = lax.optimization_barrier((dq[0], g_qkv[1], da_top))
            oth, left = g_qkv[1].reshape(n_rows, -1, 3 * hw), list(range(net.bits))
            for step in EARLY:
                oth, left = net.halve(oth, left, step)
    own, left2 = g_qkv[0].reshape(n_rows, -1, 3 * hw), list(range(net.bits))
    own, left2 = net.halve(own, left2, 0)
    d_tokens, sums_t = ln1_bwd([*d_qkv[0], *d_qkv[1]], qkv_w, qkv_w2, (da_top, da_rest), d_hidden, tokens, vecs)
    while left:
        oth, left = net.halve(oth, left, left[0])
    oth = net.cross(oth.reshape(-1, 3 * hw).astype(bf16)).astype(f32)
    n_lead = lead_table.shape[0]
    split = sums_m[16:24] + jnp.where(at == 2, bias_rows[0], 0.0) + jnp.where(at == 6, bias_rows[1], 0.0)
    crossed = sums_m[24:] + jnp.where(at == 6, bias_rows[0], 0.0) + jnp.where(at == 2, bias_rows[1], 0.0)
    slots = jnp.where(at == (net.row & 7), sums_t[2:3], 0.0)
    alike = [sums_t + sums_m[:8], sums_m[8:16]]
    late = jnp.concatenate(alike + [split, slots]) + net.cross(jnp.concatenate(alike + [crossed, slots]))

    def spread(v, step):
        got = net.flip(v, step)
        if step < 3:
            return v + got
        mine, theirs, low = v[24:], got[24:], net.bit(step) == 0
        return jnp.concatenate([v[:24] + got[:24], jnp.where(low, mine, theirs), jnp.where(low, theirs, mine)])

    crossing = net.cross(jnp.concatenate([grads[:, 2 * ff : 4 * ff], grads[:, 4 * ff + hw :]], axis=1))
    waiting = [0, 2, 1] + list(range(3, net.bits))
    while left2:
        for step in waiting[:2] if len(left2) == net.bits - 1 else waiting[:1]:
            late = spread(late, step)
            waiting.remove(step)
        own, left2 = net.halve(own, left2, left2[0])
        if len(left2) == net.bits - 3:
            own, late, crossing = lax.optimization_barrier((own, late, crossing))
        else:
            own, late = lax.optimization_barrier((own, late))
    for step in waiting:
        late = spread(late, step)
    g_qkv_sum = own.reshape(-1, 3 * hw) + oth
    leads = gathered_lead.astype(jnp.int32)
    chosen = (lax.broadcasted_iota(jnp.int32, (n_lead, n_rows), 0) == leads[None, :]).astype(f32)
    d_table = jnp.dot(chosen, late[24:], precision=lax.Precision.HIGHEST)
    split = late[16:24]
    penalty = late[7, 0] / count_total
    d_bias_qv, d_bias_up_own = split[2], split[: ff // width].reshape(-1)
    grads = jnp.concatenate([grads[:, : 2 * ff], grads[:, 4 * ff : 4 * ff + hw]], axis=1).astype(f32) + crossing.astype(f32)
    blocks = [grads[:, k * FF_BLOCK : (k + 1) * FF_BLOCK] for k in range(2 * ff // FF_BLOCK)]
    g_down = jnp.concatenate(blocks[0::2], axis=1)
    g_up = jnp.concatenate(blocks[1::2], axis=1)
    g_out = grads[:, 2 * ff :]
    return (
        block_out,
        penalty,
        d_tokens,
        d_table,
        late[0],
        late[1],
        g_qkv_sum[:, :hw],
        g_qkv_sum[:, hw : 2 * hw],
        g_qkv_sum[:, 2 * hw :],
        d_bias_qv[:hw],
        d_bias_qv[hw:],
        g_out.T,
        late[10],
        late[8],
        late[9],
        g_up,
        d_bias_up_own,
        g_down.T,
        late[6],
        late[3:6].T,
    )


def solution(mesh):
    in_specs = (
        P(("rows", "heads"), None),
        P("rows"),
        P("rows"),
        P(("rows", "heads")),
        P(),
        P(),
        P(),
        P(None, "heads"),
        P(None, "heads"),
        P(None, "heads"),
        P("heads"),
        P("heads"),
        P("heads", None),
        P(),
        P(),
        P(),
        P(None, "heads"),
        P("heads"),
        P("heads", None),
        P(),
        P(),
        P(("rows", "heads"), None),
    )
    out_specs = (
        P(("rows", "heads"), None),
        P(),
        P(("rows", "heads"), None),
        P(),
        P(),
        P(),
        P("rows", "heads"),
        P("rows", "heads"),
        P("rows", "heads"),
        P("heads"),
        P("heads"),
        P("heads", "rows"),
        P(),
        P(),
        P(),
        P("rows", "heads"),
        P("heads"),
        P("heads", "rows"),
        P(),
        P(),
    )
    return jax.shard_map(
        functools.partial(per_device, mesh.shape["rows"]),
        mesh=mesh,
        in_specs=in_specs,
        out_specs=out_specs,
        check_vma=False,
    )
```
